32 devices in a mesh: ctx: 8 (over y, x, core), wshard: 4 (over z).
Axes of the slice: x: 2, y: 2, z: 4, core: 2. Of those that a mesh axis runs over, the one named last changes fastest.
Arguments:
- byte_feats: bfloat16 [8, 2048, 768], P('wshard', 'ctx'), may hold values from -6 to 6
- lengths: int32 [8], P('wshard'), may hold values from 512 to 2048, as said below
- latent_array: bfloat16 [256, 1280], P('wshard'), may hold values from -6 to 6
- lat_gain: bfloat16 [1280], P('wshard'), may hold values from 0.5 to 1.5
- lat_bias: bfloat16 [1280], P('wshard'), may hold values from -4 to 4
- in_gain: bfloat16 [768], P('wshard'), may hold values from 0.5 to 1.5
- in_bias: bfloat16 [768], P('wshard'), may hold values from -4 to 4
- w_query: bfloat16 [1280, 256], P('wshard'), may hold values from -0.25 to 0.25
- w_key: bfloat16 [768, 256], P('wshard'), may hold values from -0.3125 to 0.3125
- w_value: bfloat16 [768, 1280], P('wshard'), may hold values from -0.21875 to 0.21875
- w_output: bfloat16 [1280, 1280], P('wshard'), may hold values from -2 to 2
- mlp_gain: bfloat16 [1280], P('wshard'), may hold values from 0.5 to 1.5
- mlp_bias: bfloat16 [1280], P('wshard'), may hold values from -4 to 4
- w_up: bfloat16 [1280, 1280], P('wshard'), may hold values from -0.15625 to 0.15625
- w_down: bfloat16 [1280, 1280], P('wshard'), may hold values from -0.15625 to 0.15625
- cotangent: bfloat16 [8, 256, 1280], P('wshard'), may hold values from -6 to 6
Outputs:
- latents_out: bfloat16 [8, 256, 1280], P('wshard')
- byte_grad: bfloat16 [8, 2048, 768], P('wshard', 'ctx')
- grad_latent: float32 [256, 1280], P('wshard')
- grad_lat_gain: float32 [1280], P('wshard')
- grad_lat_bias: float32 [1280], P('wshard')
- grad_in_gain: float32 [768], P('wshard')
- grad_in_bias: float32 [768], P('wshard')
- grad_query: float32 [1280, 256], P('wshard')
- grad_key: float32 [768, 256], P('wshard')
- grad_value: float32 [768, 1280], P('wshard')
- grad_output: float32 [1280, 1280], P('wshard')
- grad_mlp_gain: float32 [1280], P('wshard')
- grad_mlp_bias: float32 [1280], P('wshard')
- grad_up: float32 [1280, 1280], P('wshard')
- grad_down: float32 [1280, 1280], P('wshard')
The draws below stay inside these ranges and needn't reach their ends.
Inputs may be any that keep to these rules, and one draw needn't show every extreme that they name: The first lengths[s] slots of sequence s hold bytes, the rest are padding; some sequence fills all 2048 slots.
All inputs are finite; a program needn't handle non-finite values.
Results may differ from the reference program's by a relative error of at most 0.019.
Values may be sent and summed in bfloat16 or wider, within the bound.
A program may use at most 256 MiB of HBM per device.

```python
import math
import jax
import jax.numpy as jnp
from jax import lax

DIN = 768
L = 256
DL = 1280
H = 8
QK = 256
VD = 1280
SEQ = 2048
SEQS = 8


def draw_lengths(key, part):
    drawn = jax.random.randint(jax.random.fold_in(key, 11), (SEQS,), SEQ // 4, SEQ + 1)
    chosen = jax.random.randint(jax.random.fold_in(key, 12), (), 0, SEQS)
    return jnp.where(jnp.arange(SEQS, dtype=jnp.int32) == chosen, SEQ, drawn).astype(jnp.int32)


def level_of(own_key, shape, shards, least, high):
    factor_of, own = 1.0, jax.random.fold_in(own_key, 6)
    for position, shards_of in shards:
        steps = jnp.exp(jax.random.uniform(jax.random.fold_in(own, position), (shards_of,), jnp.float32, least / len(shards), high / len(shards)))
        factor_of = factor_of * jnp.repeat(steps, shape[position] // shards_of).reshape([-1 if axis == position else 1 for axis in range(len(shape))])
    return factor_of


def normal_values(key, dims, deviation, most, shards=(), kind=jnp.bfloat16):
    factor_of = level_of(key, dims, shards, -0.22, 0.18) if shards else 1.0
    values = jax.random.normal(key, dims, jnp.float32) * deviation * factor_of
    return jnp.minimum(jnp.maximum(values, -most), most).astype(kind)


def setup_inputs(seed: int = 0) -> dict:
    streams_of = jax.random.split(jax.random.key(seed), 17)
    return {
        "byte_feats": normal_values(streams_of[0], (SEQS, SEQ, DIN), 1.0, 6.0, ((0, 4), (1, 8))),
        "lengths": draw_lengths(jax.random.fold_in(streams_of[16], 71), 0),
        "latent_array": normal_values(streams_of[2], (L, DL), 1.0, 6.0, ((0, 4),)),
        "lat_gain": jnp.clip(1.0 + 0.1 * jax.random.normal(streams_of[3], (DL,), jnp.float32), 0.5, 1.5).astype(jnp.bfloat16),
        "lat_bias": normal_values(streams_of[4], (DL,), 0.3, 4.0, ((0, 4),)),
        "in_gain": jnp.clip(1.0 + 0.1 * jax.random.normal(streams_of[5], (DIN,), jnp.float32), 0.5, 1.5).astype(jnp.bfloat16),
        "in_bias": normal_values(streams_of[6], (DIN,), 0.3, 4.0, ((0, 4),)),
        "w_query": normal_values(streams_of[7], (DL, QK), (DL // 2) ** -0.5, 0.25, ((0, 4),)),
        "w_key": normal_values(streams_of[8], (DIN, QK), (DIN // 2) ** -0.5, 0.3125, ((0, 4),)),
        "w_value": normal_values(streams_of[9], (DIN, VD), DIN ** -0.5, 0.21875, ((0, 4),)),
        "w_output": normal_values(streams_of[10], (VD, DL), (max(VD // 128, 1)) ** -0.5, 2.0, ((0, 4),)),
        "mlp_gain": jnp.clip(1.0 + 0.1 * jax.random.normal(streams_of[11], (DL,), jnp.float32), 0.5, 1.5).astype(jnp.bfloat16),
        "mlp_bias": normal_values(streams_of[12], (DL,), 0.3, 4.0, ((0, 4),)),
        "w_up": normal_values(streams_of[13], (DL, DL), DL ** -0.5, 0.15625, ((0, 4),)),
        "w_down": normal_values(streams_of[14], (DL, DL), DL ** -0.5, 0.15625, ((0, 4),)),
        "cotangent": normal_values(streams_of[15], (SEQS, L, DL), 1.0, 6.0, ((0, 4),)),
    }


@jax.custom_vjp
def low(v):
    return lax.optimization_barrier(v.astype(jnp.bfloat16)).astype(jnp.float32)

@jax.custom_vjp
def low_back(v):
    return v

def low_keep(v):
    return (low(v), None)

def low_pass(kept, grad):
    return (grad,)

def back_keep(v):
    return (v, None)

def back_low(kept, grad):
    return (low(grad),)
low.defvjp(low_keep, low_pass)
low_back.defvjp(back_keep, back_low)

def layer_norm(values, gain, offset):
    center = lax.optimization_barrier(jnp.mean(values, axis=-1, keepdims=True))
    centred = values - center
    variance = lax.optimization_barrier(jnp.mean(centred * centred, axis=-1, keepdims=True))
    return centred * lax.rsqrt(variance + 1e-05) * gain + offset

def matmul(left, right):
    return jnp.dot(left, right, precision=lax.Precision.HIGHEST)

def one_sequence(params, features, length):
    latent, gain_lat, bias_lat, gain_in, bias_in, query_w, key_w, value_w, output_w, gain_mlp, bias_mlp, up_w, down_w = params
    head_count = H
    slot_count = features.shape[0]
    normed_in = low(layer_norm(features, gain_in, bias_in))
    keys = low(low_back(matmul(normed_in, key_w)))
    values = low(low_back(matmul(normed_in, value_w)))
    normed_lat = low(layer_norm(latent, gain_lat, bias_lat))
    queries = low(low_back(matmul(normed_lat, query_w)))
    head_size = query_w.shape[1] // head_count
    score_scale = 1.0 / math.sqrt(head_size)
    qheads = queries.reshape(L, head_count, head_size)
    kheads = keys.reshape(slot_count, head_count, head_size)
    vheads = values.reshape(slot_count, head_count, -1)
    scores = low_back(jnp.einsum('lhd,khd->hlk', qheads, kheads, precision=lax.Precision.HIGHEST) * score_scale)
    valid = jnp.arange(slot_count, dtype=jnp.int32) < length
    probs = low(jax.nn.softmax(jnp.where(valid, scores, -1e+30), axis=-1))
    attended = jnp.einsum('hlk,khe->lhe', probs, vheads, precision=lax.Precision.HIGHEST).reshape(L, -1)
    attended = low(low_back(attended))
    branch = low_back(matmul(attended, output_w))
    hidden = latent + branch
    normed_mid = low(layer_norm(hidden, gain_mlp, bias_mlp))
    upward = low_back(matmul(normed_mid, up_w))
    activated = low(jax.nn.gelu(upward, approximate=False))
    mlp_out = low_back(matmul(activated, down_w))
    return hidden + mlp_out

def reference(byte_feats, lengths, latent_array, lat_gain, lat_bias, in_gain, in_bias, w_query, w_key, w_value, w_output, mlp_gain, mlp_bias, w_up, w_down, cotangent):
    params = tuple((weight.astype(jnp.float32) for weight in (latent_array, lat_gain, lat_bias, in_gain, in_bias, w_query, w_key, w_value, w_output, mlp_gain, mlp_bias, w_up, w_down)))
    features = byte_feats.astype(jnp.float32)

    def forward(weights, feats):

        def per_sequence(pair):
            return one_sequence(weights, pair[0], pair[1])
        return lax.map(jax.checkpoint(per_sequence), (feats, lengths))
    outputs, pullback = jax.vjp(forward, params, features)
    weight_grads, feature_grads = pullback(cotangent.astype(jnp.float32))
    return (outputs.astype(jnp.bfloat16), feature_grads.astype(jnp.bfloat16), weight_grads[0], weight_grads[1], weight_grads[2], weight_grads[3], weight_grads[4], weight_grads[5], weight_grads[6], weight_grads[7], weight_grads[8], weight_grads[9], weight_grads[10], weight_grads[11], weight_grads[12])
```

```python
import math

import jax
import jax.numpy as jnp
from jax import lax
from jax.sharding import PartitionSpec as P

H = 8
LOW = jnp.bfloat16
FULL = jnp.float32


def layer_norm(values, gain, offset):
    center = jnp.mean(values, axis=-1, keepdims=True)
    centred = values - center
    variance = jnp.mean(centred * centred, axis=-1, keepdims=True)
    return centred * lax.rsqrt(variance + 1e-05) * gain + offset


def exact_gelu(values):
    return jax.nn.gelu(values, approximate=False)


def matmul(left, right):
    return jnp.dot(left, right, preferred_element_type=FULL)


def matmul_tn(left, right):
    return lax.dot_general(left, right, (((0,), (0,)), ((), ())), preferred_element_type=FULL)


def matmul_nt(left, right):
    return lax.dot_general(left, right, (((1,), (1,)), ((), ())), preferred_element_type=FULL)


def gather(shard):
    return lax.all_gather(shard, "wshard", axis=0, tiled=True)


def scatter(total):
    return lax.psum_scatter(
        total.astype(LOW), "wshard", scatter_dimension=0, tiled=True
    ).astype(FULL)


def own_part(total, shard):
    size = shard.shape[0]
    return lax.dynamic_slice_in_dim(total, lax.axis_index("wshard") * size, size, 0)


def shards(
    byte_feats,
    lengths,
    latent_array,
    lat_gain,
    lat_bias,
    in_gain,
    in_bias,
    w_query,
    w_key,
    w_value,
    w_output,
    mlp_gain,
    mlp_bias,
    w_up,
    w_down,
    cotangent,
):
    seqs, slots, width = byte_feats.shape
    gain_in, bias_in = gather(in_gain).astype(FULL), gather(in_bias).astype(FULL)
    key_w, value_w = gather(w_key), gather(w_value)
    latent = gather(latent_array).astype(FULL)
    gain_lat, bias_lat = gather(lat_gain).astype(FULL), gather(lat_bias).astype(FULL)
    query_w = gather(w_query)
    gain_mlp, bias_mlp = gather(mlp_gain).astype(FULL), gather(mlp_bias).astype(FULL)
    output_w, up_w, down_w = gather(w_output), gather(w_up), gather(w_down)

    features = byte_feats.reshape(seqs * slots, width).astype(FULL)
    normed_in, in_back = jax.vjp(layer_norm, features, gain_in, bias_in)
    input_low = normed_in.astype(LOW)
    keys = matmul(input_low, key_w).astype(LOW)
    values = matmul(input_low, value_w).astype(LOW)
    normed_lat, lat_back = jax.vjp(layer_norm, latent, gain_lat, bias_lat)
    lat_low = normed_lat.astype(LOW)
    rows = lat_low.shape[0]
    queries = matmul(lat_low, query_w).astype(LOW)
    score_scale = 1.0 / math.sqrt(queries.shape[1] // H)
    qheads = queries.reshape(rows, H, -1)
    kheads = keys.reshape(seqs, slots, H, -1)
    vheads = values.reshape(seqs, slots, H, -1)

    scores = jnp.einsum("lhd,mkhd->mhlk", qheads, kheads, preferred_element_type=FULL) * score_scale
    slot_ids = lax.axis_index("ctx") * slots + lax.iota(jnp.int32, slots)
    valid = (slot_ids[None, :] < lengths[:, None])[:, None, None, :]
    scores = jnp.where(valid, scores, -1e30)
    highest = lax.pmax(jnp.max(scores, axis=-1), "ctx")
    weights = jnp.where(valid, jnp.exp(scores - highest[..., None]), 0.0)
    total = lax.psum(jnp.sum(weights, axis=-1), "ctx")
    numer = jnp.einsum("mhlk,mkhe->mlhe", weights.astype(LOW), vheads, preferred_element_type=FULL)
    numer = lax.psum(numer.astype(LOW), "ctx").astype(FULL)
    attended = numer / jnp.transpose(total, (0, 2, 1))[..., None]
    attended = attended.reshape(seqs * rows, -1)

    att_low = attended.astype(LOW)
    hidden = jnp.tile(latent, (seqs, 1)) + matmul(att_low, output_w)
    normed_mid, mid_back = jax.vjp(layer_norm, hidden, gain_mlp, bias_mlp)
    mid_low = normed_mid.astype(LOW)
    upward = matmul(mid_low, up_w)
    activated, gelu_back = jax.vjp(exact_gelu, upward)
    act_low = activated.astype(LOW)
    result = hidden + matmul(act_low, down_w)
    dout_low = cotangent.reshape(seqs * rows, -1)
    grad_down = scatter(matmul_tn(act_low, dout_low))
    (grad_upward,) = gelu_back(matmul_nt(dout_low, down_w))
    up_low = grad_upward.astype(LOW)
    grad_up = scatter(matmul_tn(mid_low, up_low))
    dhid_norm, grad_gmlp, grad_bmlp = mid_back(matmul_nt(up_low, up_w))
    dhidden = dout_low.astype(FULL) + dhid_norm
    dhid_low = dhidden.astype(LOW)
    grad_output = scatter(matmul_tn(att_low, dhid_low))
    grad_hidden = scatter(jnp.sum(dhidden.reshape(seqs, rows, -1), axis=0))
    grad_att = matmul_nt(dhid_low, output_w).astype(LOW)

    grad_heads = grad_att.reshape(seqs, rows, H, -1)
    delta = jnp.sum(
        grad_heads.astype(FULL) * attended.reshape(seqs, rows, H, -1), axis=-1
    ).transpose(0, 2, 1)
    probs = weights / total[..., None]
    dprobs = jnp.einsum("mlhe,mkhe->mhlk", grad_heads, vheads, preferred_element_type=FULL)
    dscores = (probs * (dprobs - delta[..., None])).astype(LOW)
    dquery = jnp.einsum("mhlk,mkhd->lhd", dscores, kheads, preferred_element_type=FULL) * score_scale
    dkeys = jnp.einsum("mhlk,lhd->mkhd", dscores, qheads, preferred_element_type=FULL) * score_scale
    dvalues = jnp.einsum("mhlk,mlhe->mkhe", probs.astype(LOW), grad_heads, preferred_element_type=FULL)
    dkeys = dkeys.astype(LOW).reshape(seqs * slots, -1)
    dvalues = dvalues.astype(LOW).reshape(seqs * slots, -1)

    dquery = lax.psum(dquery.reshape(rows, -1).astype(LOW), ("ctx", "wshard"))
    grad_query = matmul_tn(
        lax.dynamic_slice_in_dim(
            lat_low, lax.axis_index("wshard") * w_query.shape[0], w_query.shape[0], 1
        ),
        dquery,
    )
    dlat_norm, grad_glat, grad_blat = lat_back(matmul_nt(dquery, query_w))
    grad_latent = grad_hidden + own_part(dlat_norm, latent_array)

    dnorm_in = matmul_nt(dkeys, key_w) + matmul_nt(dvalues, value_w)
    dfeatures, grad_gin, grad_bin = in_back(dnorm_in)
    grad_key = lax.psum(scatter(matmul_tn(input_low, dkeys)).astype(LOW), "ctx").astype(FULL)
    grad_value = lax.psum(scatter(matmul_tn(input_low, dvalues)).astype(LOW), "ctx").astype(FULL)
    in_sums = lax.psum(jnp.concatenate([grad_gin, grad_bin]), ("ctx", "wshard"))
    grad_gin, grad_bin = jnp.split(in_sums, 2)
    mlp_sums = lax.psum(jnp.concatenate([grad_gmlp, grad_bmlp]), "wshard")
    grad_gmlp, grad_bmlp = jnp.split(mlp_sums, 2)
    return (
        result.astype(LOW).reshape(seqs, rows, -1),
        dfeatures.astype(LOW).reshape(seqs, slots, width),
        grad_latent,
        own_part(grad_glat, lat_gain),
        own_part(grad_blat, lat_bias),
        own_part(grad_gin, in_gain),
        own_part(grad_bin, in_bias),
        grad_query,
        grad_key,
        grad_value,
        grad_output,
        own_part(grad_gmlp, mlp_gain),
        own_part(grad_bmlp, mlp_bias),
        grad_up,
        grad_down,
    )


def solution(mesh):
    sharded, plain = P("wshard", None), P("wshard")
    return jax.shard_map(
        shards,
        mesh=mesh,
        in_specs=(
            P("wshard", "ctx", None),
            plain,
            sharded,
            plain,
            plain,
            plain,
            plain,
            sharded,
            sharded,
            sharded,
            sharded,
            plain,
            plain,
            sharded,
            sharded,
            P("wshard", None, None),
        ),
        out_specs=(
            P("wshard", None, None),
            P("wshard", "ctx", None),
            sharded,
            plain,
            plain,
            plain,
            plain,
            sharded,
            sharded,
            sharded,
            sharded,
            plain,
            plain,
            sharded,
            sharded,
        ),
        check_vma=False,
    )
```

```python
import functools
import math
import types

import jax
import jax.numpy as jnp
from jax import lax
from jax.experimental import pallas as pl
from jax.experimental.pallas import tpu as pltpu
from jax.sharding import PartitionSpec as P

H = 8
LOW = jnp.bfloat16
FULL = jnp.float32


def layer_norm(values, gain, offset):
    center = jnp.mean(values, axis=-1, keepdims=True)
    centred = values - center
    variance = jnp.mean(centred * centred, axis=-1, keepdims=True)
    return centred * lax.rsqrt(variance + 1e-05) * gain + offset


def exact_gelu(values):
    return jax.nn.gelu(values, approximate=False)


def matmul(left, right):
    return jnp.dot(left, right, preferred_element_type=FULL)


def matmul_tn(left, right):
    return lax.dot_general(left, right, (((0,), (0,)), ((), ())), preferred_element_type=FULL)


def matmul_nt(left, right):
    return lax.dot_general(left, right, (((1,), (1,)), ((), ())), preferred_element_type=FULL)


def gather(shard):
    return lax.all_gather(shard, "wshard", axis=0, tiled=True)


def scatter(total):
    return lax.psum_scatter(
        total.astype(LOW), "wshard", scatter_dimension=0, tiled=True
    ).astype(FULL)


SEMS = 160


def own_part(total, shard):
    size = shard.shape[0]
    return lax.dynamic_slice_in_dim(total, lax.axis_index("wshard") * size, size, 0)


def plain(
    byte_feats,
    lengths,
    latent_array,
    lat_gain,
    lat_bias,
    in_gain,
    in_bias,
    w_query,
    w_key,
    w_value,
    w_output,
    mlp_gain,
    mlp_bias,
    w_up,
    w_down,
    cotangent,
):
    seqs, slots, width = byte_feats.shape
    gain_in, bias_in = gather(in_gain).astype(FULL), gather(in_bias).astype(FULL)
    key_w, value_w = gather(w_key), gather(w_value)
    latent = gather(latent_array).astype(FULL)
    gain_lat, bias_lat = gather(lat_gain).astype(FULL), gather(lat_bias).astype(FULL)
    query_w = gather(w_query)
    gain_mlp, bias_mlp = gather(mlp_gain).astype(FULL), gather(mlp_bias).astype(FULL)
    output_w, up_w, down_w = gather(w_output), gather(w_up), gather(w_down)

    features = byte_feats.reshape(seqs * slots, width).astype(FULL)
    normed_in, in_back = jax.vjp(layer_norm, features, gain_in, bias_in)
    input_low = normed_in.astype(LOW)
    keys = matmul(input_low, key_w).astype(LOW)
    values = matmul(input_low, value_w).astype(LOW)
    normed_lat, lat_back = jax.vjp(layer_norm, latent, gain_lat, bias_lat)
    lat_low = normed_lat.astype(LOW)
    rows = lat_low.shape[0]
    queries = matmul(lat_low, query_w).astype(LOW)
    score_scale = 1.0 / math.sqrt(queries.shape[1] // H)
    qheads = queries.reshape(rows, H, -1)
    kheads = keys.reshape(seqs, slots, H, -1)
    vheads = values.reshape(seqs, slots, H, -1)

    scores = jnp.einsum("lhd,mkhd->mhlk", qheads, kheads, preferred_element_type=FULL) * score_scale
    slot_ids = lax.axis_index("ctx") * slots + lax.iota(jnp.int32, slots)
    valid = (slot_ids[None, :] < lengths[:, None])[:, None, None, :]
    scores = jnp.where(valid, scores, -1e30)
    highest = lax.pmax(jnp.max(scores, axis=-1), "ctx")
    weights = jnp.where(valid, jnp.exp(scores - highest[..., None]), 0.0)
    total = lax.psum(jnp.sum(weights, axis=-1), "ctx")
    numer = jnp.einsum("mhlk,mkhe->mlhe", weights.astype(LOW), vheads, preferred_element_type=FULL)
    numer = lax.psum(numer.astype(LOW), "ctx").astype(FULL)
    attended = numer / jnp.transpose(total, (0, 2, 1))[..., None]
    attended = attended.reshape(seqs * rows, -1)

    att_low = attended.astype(LOW)
    hidden = jnp.tile(latent, (seqs, 1)) + matmul(att_low, output_w)
    normed_mid, mid_back = jax.vjp(layer_norm, hidden, gain_mlp, bias_mlp)
    mid_low = normed_mid.astype(LOW)
    upward = matmul(mid_low, up_w)
    activated, gelu_back = jax.vjp(exact_gelu, upward)
    act_low = activated.astype(LOW)
    result = hidden + matmul(act_low, down_w)
    dout_low = cotangent.reshape(seqs * rows, -1)
    grad_down = scatter(matmul_tn(act_low, dout_low))
    (grad_upward,) = gelu_back(matmul_nt(dout_low, down_w))
    up_low = grad_upward.astype(LOW)
    grad_up = scatter(matmul_tn(mid_low, up_low))
    dhid_norm, grad_gmlp, grad_bmlp = mid_back(matmul_nt(up_low, up_w))
    dhidden = dout_low.astype(FULL) + dhid_norm
    dhid_low = dhidden.astype(LOW)
    grad_output = scatter(matmul_tn(att_low, dhid_low))
    grad_hidden = scatter(jnp.sum(dhidden.reshape(seqs, rows, -1), axis=0))
    grad_att = matmul_nt(dhid_low, output_w).astype(LOW)

    grad_heads = grad_att.reshape(seqs, rows, H, -1)
    delta = jnp.sum(
        grad_heads.astype(FULL) * attended.reshape(seqs, rows, H, -1), axis=-1
    ).transpose(0, 2, 1)
    probs = weights / total[..., None]
    dprobs = jnp.einsum("mlhe,mkhe->mhlk", grad_heads, vheads, preferred_element_type=FULL)
    dscores = (probs * (dprobs - delta[..., None])).astype(LOW)
    dquery = jnp.einsum("mhlk,mkhd->lhd", dscores, kheads, preferred_element_type=FULL) * score_scale
    dkeys = jnp.einsum("mhlk,lhd->mkhd", dscores, qheads, preferred_element_type=FULL) * score_scale
    dvalues = jnp.einsum("mhlk,mlhe->mkhe", probs.astype(LOW), grad_heads, preferred_element_type=FULL)
    dkeys = dkeys.astype(LOW).reshape(seqs * slots, -1)
    dvalues = dvalues.astype(LOW).reshape(seqs * slots, -1)

    dquery = lax.psum(dquery.reshape(rows, -1).astype(LOW), ("ctx", "wshard"))
    grad_query = matmul_tn(
        lax.dynamic_slice_in_dim(
            lat_low, lax.axis_index("wshard") * w_query.shape[0], w_query.shape[0], 1
        ),
        dquery,
    )
    dlat_norm, grad_glat, grad_blat = lat_back(matmul_nt(dquery, query_w))
    grad_latent = grad_hidden + own_part(dlat_norm, latent_array)

    dnorm_in = matmul_nt(dkeys, key_w) + matmul_nt(dvalues, value_w)
    dfeatures, grad_gin, grad_bin = in_back(dnorm_in)
    grad_key = lax.psum(scatter(matmul_tn(input_low, dkeys)).astype(LOW), "ctx").astype(FULL)
    grad_value = lax.psum(scatter(matmul_tn(input_low, dvalues)).astype(LOW), "ctx").astype(FULL)
    in_sums = lax.psum(jnp.concatenate([grad_gin, grad_bin]), ("ctx", "wshard"))
    grad_gin, grad_bin = jnp.split(in_sums, 2)
    mlp_sums = lax.psum(jnp.concatenate([grad_gmlp, grad_bmlp]), "wshard")
    grad_gmlp, grad_bmlp = jnp.split(mlp_sums, 2)
    return (
        result.astype(LOW).reshape(seqs, rows, -1),
        dfeatures.astype(LOW).reshape(seqs, slots, width),
        grad_latent,
        own_part(grad_glat, lat_gain),
        own_part(grad_blat, lat_bias),
        own_part(grad_gin, in_gain),
        own_part(grad_bin, in_bias),
        grad_query,
        grad_key,
        grad_value,
        grad_output,
        own_part(grad_gmlp, mlp_gain),
        own_part(grad_bmlp, mlp_bias),
        grad_up,
        grad_down,
    )


def ln_parts(values):
    centred = values - jnp.mean(values, axis=-1, keepdims=True)
    scale = lax.rsqrt(jnp.mean(centred * centred, axis=-1, keepdims=True) + 1e-05)
    return centred * scale, scale


def ln_grad(cotangent, gain, normed, scale):
    scaled = cotangent * gain
    first = jnp.mean(scaled, axis=-1, keepdims=True)
    second = jnp.mean(scaled * normed, axis=-1, keepdims=True)
    return scale * (scaled - first - normed * second)


def lanes(rows, columns):
    return lax.broadcasted_iota(jnp.int32, (rows, columns), 1)


def columns_sum(values):
    return jnp.sum(values, axis=0, keepdims=True)


class Plan:
    def __init__(self, ctx, zs, feats, latent, w_query, w_key, w_value, w_output, cot):
        self.ctx, self.zs = ctx, zs
        self.rows_in, self.din = feats.shape
        self.lat = latent.shape[0] * zs
        self.dl = latent.shape[1]
        self.qk, self.vd = w_key.shape[1], w_value.shape[1]
        self.seqs = cot.shape[0] // self.lat
        self.slots = self.rows_in // self.seqs
        self.head, self.vhead = self.qk // H, self.vd // H


def scratch_table(p):
    both = p.seqs * p.lat
    half = p.dl // 2
    part = p.dl // p.zs // 4
    vpart = p.din // p.zs // 4
    return dict(
        wk=((p.din, p.qk), LOW),
        wq=((p.dl, p.qk), LOW),
        lat=((p.lat, p.dl), LOW),
        wv=((p.din, p.vd), LOW),
        wo=((p.vd, p.dl), LOW),
        wu=((p.dl, p.dl), LOW),
        wd=((p.dl, p.dl), LOW),
        small_own=((8, 384), FULL),
        small=((p.zs, 8, 384), FULL),
        vec=((8, p.dl), FULL),
        feats=((p.rows_in, p.din), LOW),
        nin=((p.rows_in, p.din), LOW),
        nin_t=((p.din, p.rows_in), LOW),
        keys=((p.rows_in, p.qk), LOW),
        keys_t=((p.qk, p.rows_in), LOW),
        values=((p.rows_in, p.vd), LOW),
        nlat=((p.lat, p.dl), LOW),
        qmask=((H * p.lat, p.qk), LOW),
        scores=((p.seqs * H * p.lat, p.slots), FULL),
        stat=((p.lat, 128), FULL),
        stat_t=((128, p.lat), FULL),
        max_own=((2 * H, p.lat), FULL),
        max_in=((p.ctx, 2 * H, p.lat), FULL),
        max_all=((2 * H, p.lat), FULL),
        numer=((p.lat, p.vd), FULL),
        numer_low=((p.lat, p.vd), LOW),
        numer_in=((p.lat, p.vd), LOW),
        sums=((2, H, p.lat), FULL),
        sums_in=((H, p.lat), FULL),
        chip=((p.lat, p.vd), LOW),
        chip_in=((4, p.lat // 4, p.vd), LOW),
        chip_sums=((H, p.lat), FULL),
        chip_sums_in=((4, H, p.lat), FULL),
        scale=((p.lat // 4, p.vd), FULL),
        att=((both, p.vd), LOW),
        mid=((both, p.dl), LOW),
        act=((both, p.dl), LOW),
        dup=((both, p.dl), LOW),
        dhid=((both, p.dl), LOW),
        datt=((both, p.vd), LOW),
        cot=((both, p.dl), LOW),
        hid=((p.lat, p.dl), FULL),
        slope=((p.lat, p.dl), FULL),
        dmid=((p.lat, p.dl), FULL),
        res=((p.lat, p.dl), LOW),
        stats=((2, 2 * H, p.lat), FULL),
        dwo=((p.vd, half), LOW),
        dwu=((p.dl, half), LOW),
        dwd=((p.dl, half), LOW),
        dlat=((p.lat, half), LOW),
        zo=((p.zs, part, half), LOW),
        zu=((p.zs, part, half), LOW),
        zd=((p.zs, part, half), LOW),
        zl=((p.zs, p.lat // p.zs // 4, half), LOW),
        fo=((part, half), LOW),
        fu=((part, half), LOW),
        fd=((part, half), LOW),
        fl=((p.lat // p.zs // 4, half), LOW),
        dkeys=((p.rows_in, p.qk), LOW),
        dvalues=((p.rows_in, p.vd), LOW),
        dk_sum=((p.slots, p.qk), FULL),
        dq_t=((p.qk, p.lat), FULL),
        dq=((p.lat, p.qk), LOW),
        dq_in1=((p.lat, p.qk // 2), LOW),
        dq_chip=((p.lat, p.qk // 2), LOW),
        dq_in2=((4, p.lat, p.qk // 2), LOW),
        dq_plane=((p.lat, p.qk // 2), LOW),
        dq_in3=((p.zs, p.lat, p.qk // 2), LOW),
        dq_all=((p.lat, p.qk), LOW),
        bgrad=((p.rows_in, p.din), LOW),
        swk=((2, p.din, p.qk // 2), LOW),
        swv=((2, p.din, p.vd // 2), LOW),
        rwk=((p.din, p.qk // 2), LOW),
        rwv=((p.din, p.vd // 2), LOW),
        cwk=((p.zs, p.din // p.zs, p.qk // 2), LOW),
        cwv=((p.zs, p.din // p.zs, p.vd // 2), LOW),
        pwk_in=((4, p.zs, vpart, p.qk // 2), LOW),
        pwv_in=((4, p.zs, vpart, p.vd // 2), LOW),
        pwk=((p.zs, vpart, p.qk // 2), LOW),
        pwv=((p.zs, vpart, p.vd // 2), LOW),
        zwk_in=((p.zs, vpart, p.qk // 2), LOW),
        zwv_in=((p.zs, vpart, p.vd // 2), LOW),
        fwk=((vpart, p.qk // 2), LOW),
        fwv=((vpart, p.vd // 2), LOW),
        vs=((8, p.dl), FULL),
        vs_in1=((8, p.dl), FULL),
        vs_chip=((8, p.dl), FULL),
        vs_in2=((4, 8, p.dl), FULL),
        vs_plane=((8, p.dl), FULL),
        vs_in3=((p.zs, 8, p.dl), FULL),
        vs_all=((8, p.dl), FULL),
        gq=((p.dl, p.qk), FULL),
    )


class Copies:
    def __init__(self, sems):
        self.sems, self.used, self.open = sems, 0, []

    def new(self):
        self.used += 1
        return self.sems.at[self.used - 1]

    def group(self):
        return (self.new(), self.new())

    def send(self, pair, src, dst, ctx, z):
        pltpu.make_async_remote_copy(
            src_ref=src,
            dst_ref=dst,
            send_sem=pair[0],
            recv_sem=pair[1],
            device_id=(ctx, z),
            device_id_type=pl.DeviceIdType.MESH,
        ).start()

    def local(self, src, dst):
        copy = pltpu.make_async_copy(src, dst, self.new())
        copy.start()
        return copy

    def got(self, pair, view):
        pltpu.make_async_copy(view, view, pair[1]).wait()

    def sent(self, pair, view):
        self.open.append((pair[0], view))

    def drain(self):
        for sem, view in self.open:
            pltpu.make_async_copy(view, view, sem).wait()


def at(start, size, step=None):
    return pl.ds(pl.multiple_of(start, step or size), size)


def fused_kernel(p, names, *refs):
    ins, refs = refs[:16], refs[16:]
    lengths, feats_in, lat_in, wq_in, wk_in, wv_in, wo_in, wu_in, wd_in = ins[:9]
    smalls, cot_in = ins[9:15], ins[15]
    outs, refs = refs[:11], refs[11:]
    res_out, byte_out, go, gu, gd, gv, gk, gl, gq_out, glat_out, vec_out = outs
    sems = refs[-1]
    s = types.SimpleNamespace(**dict(zip(names, refs[:-1])))
    cp = Copies(sems)
    ctx, zs = p.ctx, p.zs
    c, z = lax.axis_index("ctx"), lax.axis_index("wshard")
    h, q = lax.rem(c, 2), lax.div(c, 2)
    x, y = lax.rem(q, 2), lax.div(q, 2)
    other = 1 - h
    core = c + 1 - 2 * h
    chips = (c + 2 - 4 * x, c + 4 - 8 * y, c + 6 - 4 * x - 8 * y)
    near = (chips[0] * (1 - h) + chips[1] * h, chips[1] * (1 - h) + chips[0] * h)
    zed = [lax.rem(z + j, zs) for j in range(1, zs)]
    plane = [lax.rem(c + j, ctx) for j in range(1, ctx)]

    barrier = pltpu.get_barrier_semaphore()
    for peer in plane:
        pl.semaphore_signal(barrier, inc=1, device_id=(peer, z), device_id_type=pl.DeviceIdType.MESH)
    for peer in zed:
        pl.semaphore_signal(barrier, inc=1, device_id=(c, peer), device_id_type=pl.DeviceIdType.MESH)
    pl.semaphore_wait(barrier, ctx - 1 + zs - 1)

    load_feats = cp.local(feats_in, s.feats)
    for row, ref in enumerate(smalls):
        s.small_own[row : row + 1, 0 : ref.shape[1]] = ref[...].astype(FULL)
    small_pair = cp.group()
    for peer in zed:
        cp.send(small_pair, s.small_own, s.small.at[z], c, peer)
    cp.sent(small_pair, s.small.at[0 : zs - 1])

    class Weight:
        def __init__(self, ref, source):
            self.ref, self.source = ref, source
            self.rows, cols = source.shape
            self.part, self.cols = self.rows // 4, cols // 2
            self.mine = at(h * self.cols, self.cols)
            self.pairs = [cp.group() for _ in range(4)]

        def view(self, rows):
            return self.ref.at[pl.ds(0, rows), pl.ds(0, self.cols)]

        def block(self, zz, qq):
            return self.ref.at[at(zz * self.rows + qq * self.part, self.part, 16), self.mine]

        def start(self):
            for peer in zed:
                cp.send(
                    self.pairs[0],
                    self.source.at[at(q * self.part, self.part, 16), self.mine],
                    self.block(z, q),
                    c,
                    peer,
                )
            cp.sent(self.pairs[0], self.view(3 * self.part))
            self.load = cp.local(self.source, self.ref.at[at(z * self.rows, self.rows, 16), :])

        def first(self):
            cp.got(self.pairs[0], self.view(3 * self.part))
            for zz in zed:
                block = self.block(zz, q)
                cp.send(self.pairs[1], block, block, near[0], z)
            cp.sent(self.pairs[1], self.view(3 * self.part))

        def second(self):
            cp.got(self.pairs[1], self.view(3 * self.part))
            for zz in zed:
                for qq in (q, lax.div(near[0], 2)):
                    block = self.block(zz, qq)
                    cp.send(self.pairs[2], block, block, near[1], z)
            cp.sent(self.pairs[2], self.view(6 * self.part))

        def third(self):
            cp.got(self.pairs[2], self.view(6 * self.part))
            for zz in zed:
                block = self.ref.at[at(zz * self.rows, self.rows, 16), self.mine]
                cp.send(self.pairs[3], block, block, core, z)
            cp.sent(self.pairs[3], self.view(3 * self.rows))

        def ready(self):
            cp.got(self.pairs[3], self.view(3 * self.rows))
            self.load.wait()

    wk, wq, lat = Weight(s.wk, wk_in), Weight(s.wq, wq_in), Weight(s.lat, lat_in)
    wv = Weight(s.wv, wv_in)
    wo, wu, wd = Weight(s.wo, wo_in), Weight(s.wu, wu_in), Weight(s.wd, wd_in)
    for weight in (wk, wq, lat, wv, wo, wu, wd):
        weight.start()
    load_cot = cp.local(cot_in, s.cot)

    cp.got(small_pair, s.small.at[0 : zs - 1])
    s.small[z] = s.small_own[...]
    for row, ref in enumerate(smalls):
        size = ref.shape[1]
        for zz in range(zs):
            s.vec[row : row + 1, zz * size : (zz + 1) * size] = s.small[zz, row : row + 1, 0:size]
    vec = s.vec
    gain_lat, bias_lat = vec[0:1, :], vec[1:2, :]

    load_feats.wait()

    @pl.loop(0, p.rows_in // 64)
    def _(i):
        rows = at(i * 64, 64)
        normed, _ = ln_parts(s.feats[rows, :].astype(FULL))
        s.nin[rows, :] = (normed * vec[2:3, 0 : p.din] + vec[3:4, 0 : p.din]).astype(LOW)

    wk.first()
    wq.first()
    lat.first()

    @pl.loop(0, p.din // 128)
    def _(i):
        tile = at(i * 128, 128)
        s.nin_t[tile, :] = s.nin[:, tile].T

    wk.second()
    wq.second()
    lat.second()
    wv.first()
    wk.third()
    wq.third()
    lat.third()
    wk.ready()

    @pl.loop(0, p.seqs)
    def _(i):
        rows = at(i * p.slots, p.slots)
        low = matmul(s.nin[rows, :], s.wk[...]).astype(LOW)
        s.keys[rows, :] = low
        s.keys_t[:, rows] = low.T

    wv.second()
    lat.ready()

    @pl.loop(0, p.lat // 64)
    def _(i):
        rows = at(i * 64, 64)
        normed, _ = ln_parts(s.lat[rows, :].astype(FULL))
        s.nlat[rows, :] = (normed * gain_lat + bias_lat).astype(LOW)

    wq.ready()
    queries = matmul(s.nlat[...], s.wq[...])
    lane_q = lanes(p.lat, p.qk)
    for head in range(H):
        inside = (lane_q >= head * p.head) & (lane_q < (head + 1) * p.head)
        s.qmask[head * p.lat : (head + 1) * p.lat, :] = jnp.where(inside, queries, 0.0).astype(LOW)

    score_scale = 1.0 / math.sqrt(p.head)
    start_slot = c * p.slots
    s.stat[...] = jnp.zeros_like(s.stat)
    lane_stat = lanes(p.lat, 128)

    @pl.loop(0, p.seqs * H)
    def _(i):
        seq, head = lax.div(i, H), lax.rem(i, H)
        raw = matmul_nt(
            s.qmask[at(head * p.lat, p.lat), :], s.keys[at(seq * p.slots, p.slots), :]
        )
        valid = start_slot + lanes(p.lat, p.slots) < lengths[seq]
        scores = jnp.where(valid, raw * score_scale, -1e30)
        s.scores[at(i * p.lat, p.lat), :] = scores
        top = jnp.max(scores, axis=-1, keepdims=True)
        s.stat[...] = jnp.where(lane_stat == i, top, s.stat[...])

    s.stat_t[...] = s.stat[...].T
    s.max_own[...] = s.stat_t[0 : 2 * H, :]
    max_pair = cp.group()
    for peer in plane:
        cp.send(max_pair, s.max_own, s.max_in.at[c], peer, z)
    cp.sent(max_pair, s.max_in.at[0 : ctx - 1])

    wv.third()
    wo.first()
    wv.ready()

    @pl.loop(0, p.vd // 256)
    def _(i):
        tile = at(i * 256, 256)
        s.values[:, tile] = matmul(s.nin[...], s.wv[:, tile]).astype(LOW)

    cp.got(max_pair, s.max_in.at[0 : ctx - 1])
    s.max_in[c] = s.max_own[...]
    top = s.max_in[0]
    for i in range(1, ctx):
        top = jnp.maximum(top, s.max_in[i])
    s.max_all[...] = top
    s.stat_t[0 : 2 * H, :] = top
    max_columns = s.stat_t[...].T
    s.stat[...] = jnp.zeros_like(s.stat)

    def window(head):
        low_lane = pl.multiple_of(lax.div(head * p.vhead, 128) * 128, 128)
        return pl.ds(low_lane, 256), head * p.vhead - low_lane

    def mask_of(rows, low_lane):
        lane = lanes(rows, 256)
        return ((lane >= low_lane) & (lane < low_lane + p.vhead)).astype(FULL)

    def partial(seq):
        s.numer[...] = jnp.zeros_like(s.numer)

        @pl.loop(0, H)
        def _(head):
            i = seq * H + head
            top = jnp.sum(jnp.where(lane_stat == i, max_columns, 0.0), axis=-1, keepdims=True)
            weights = jnp.exp(s.scores[at(i * p.lat, p.lat), :] - top)
            total = jnp.sum(weights, axis=-1, keepdims=True)
            s.stat[...] = jnp.where(lane_stat == i, total, s.stat[...])
            cols, low_lane = window(head)
            part = s.values[at(seq * p.slots, p.slots), cols] * mask_of(p.slots, low_lane).astype(LOW)
            s.numer[:, cols] += matmul(weights.astype(LOW), part)

        s.stat_t[...] = s.stat[...].T
        s.sums[seq] = s.stat_t[at(seq * H, H), :]

    partial(other)
    s.numer_low[...] = s.numer[...].astype(LOW)
    pair_pair = cp.group()
    sums_pair = cp.group()
    cp.send(pair_pair, s.numer_low, s.numer_in, core, z)
    cp.send(sums_pair, s.sums.at[other], s.sums_in, core, z)
    cp.sent(pair_pair, s.numer_low)
    cp.sent(sums_pair, s.sums_in)
    partial(h)
    wo.second()

    cp.got(pair_pair, s.numer_in)
    cp.got(sums_pair, s.sums_in)
    quarter = p.lat // 4
    s.chip[...] = (s.numer[...] + s.numer_in[...].astype(FULL)).astype(LOW)
    s.chip_sums[...] = s.sums[h] + s.sums_in[...]
    chip_pair = cp.group()
    chip_sums_pair = cp.group()
    for peer in chips:
        peer_chip = lax.div(peer, 2)
        cp.send(chip_pair, s.chip.at[at(peer_chip * quarter, quarter), :], s.chip_in.at[q], peer, z)
        cp.send(chip_sums_pair, s.chip_sums, s.chip_sums_in.at[q], peer, z)
    cp.sent(chip_pair, s.chip_in.at[0:3])
    cp.sent(chip_sums_pair, s.chip_sums_in.at[0:3])
    wu.first()
    wo.third()

    cp.got(chip_sums_pair, s.chip_sums_in.at[0:3])
    s.chip_sums_in[q] = s.chip_sums[...]
    sums = s.chip_sums_in
    inverse = 1.0 / ((sums[0] + sums[1]) + (sums[2] + sums[3]))
    s.stats[h, 0:H, :] = inverse
    s.stat_t[0:H, :] = inverse
    s.stat[...] = s.stat_t[...].T
    s.scale[...] = jnp.zeros_like(s.scale)
    own_quarter = s.stat[at(q * quarter, quarter), :]
    for head in range(H):
        low_lane = head * p.vhead // 128 * 128
        lane = lanes(quarter, 256) + low_lane
        inside = (lane >= head * p.vhead) & (lane < (head + 1) * p.vhead)
        cols = slice(low_lane, low_lane + 256)
        s.scale[:, cols] = jnp.where(inside, own_quarter[:, head : head + 1], s.scale[:, cols])
    cp.got(chip_pair, s.chip_in.at[0:3])
    s.chip_in[q] = s.chip[at(q * quarter, quarter), :]
    numer = s.chip_in
    added = (numer[0].astype(FULL) + numer[1].astype(FULL)) + (numer[2].astype(FULL) + numer[3].astype(FULL))
    own_rows = at(h * p.lat + q * quarter, quarter)
    s.att[own_rows, :] = (added * s.scale[...]).astype(LOW)
    att_pair = cp.group()
    for peer in chips:
        cp.send(att_pair, s.att.at[own_rows, :], s.att.at[own_rows, :], peer, z)
    cp.sent(att_pair, s.att.at[0 : 3 * quarter, :])
    wu.second()
    wd.first()
    wo.ready()
    own = at(h * p.lat, p.lat)
    cp.got(att_pair, s.att.at[0 : 3 * quarter, :])

    def share(ref):
        pair = cp.group()
        cp.send(pair, ref.at[own, :], ref.at[own, :], core, z)
        cp.sent(pair, ref.at[0 : p.lat, :])
        return pair

    att_share = share(s.att)
    tiles = p.dl // 256

    @pl.loop(0, tiles)
    def _(i):
        tile = at(i * 256, 256)
        s.hid[:, tile] = s.lat[:, tile].astype(FULL) + matmul(s.att[own, :], s.wo[:, tile])

    wu.third()
    wd.second()
    gain_mlp, bias_mlp = vec[4:5, :], vec[5:6, :]

    @pl.loop(0, p.lat // 64)
    def _(i):
        normed, _ = ln_parts(s.hid[at(i * 64, 64), :])
        s.mid[at(h * p.lat + i * 64, 64), :] = (normed * gain_mlp + bias_mlp).astype(LOW)

    mid_share = share(s.mid)
    wu.ready()
    load_cot.wait()

    @pl.loop(0, tiles)
    def _(i):
        tile = at(i * 256, 256)
        up = matmul(s.mid[own, :], s.wu[:, tile])
        cdf = 0.5 * (1.0 + lax.erf(up * (1.0 / math.sqrt(2.0))))
        density = jnp.exp(-0.5 * up * up) * (1.0 / math.sqrt(2.0 * math.pi))
        s.act[own, tile] = (up * cdf).astype(LOW)
        s.slope[:, tile] = cdf + up * density

    act_share = share(s.act)
    wd.third()
    wd.ready()

    @pl.loop(0, tiles)
    def _(i):
        tile = at(i * 256, 256)
        dact = matmul_nt(s.cot[own, :], s.wd[tile, :])
        s.dup[own, tile] = (dact * s.slope[:, tile]).astype(LOW)

    dup_share = share(s.dup)

    @pl.loop(0, tiles)
    def _(i):
        tile = at(i * 256, 256)
        s.dmid[:, tile] = matmul_nt(s.dup[own, :], s.wu[tile, :])

    s.vs[...] = jnp.zeros_like(s.vs)

    @pl.loop(0, p.lat // 64)
    def _(i):
        rows = at(i * 64, 64)
        full_rows = at(h * p.lat + i * 64, 64)
        normed, scale = ln_parts(s.hid[rows, :])
        grad = s.dmid[rows, :]
        s.vs[0:1, :] += columns_sum(grad * normed)
        s.vs[1:2, :] += columns_sum(grad)
        total = s.cot[full_rows, :].astype(FULL) + ln_grad(grad, gain_mlp, normed, scale)
        s.dhid[full_rows, :] = total.astype(LOW)

    dhid_share = share(s.dhid)

    @pl.loop(0, tiles)
    def _(i):
        tile = at(i * 256, 256)
        s.datt[own, tile] = matmul_nt(s.dhid[own, :], s.wo[tile, :]).astype(LOW)

    datt_share = share(s.datt)
    s.stat[...] = jnp.zeros_like(s.stat)

    @pl.loop(0, H)
    def _(head):
        cols, low_lane = window(head)
        product = s.datt[own, cols].astype(FULL) * s.att[own, cols].astype(FULL)
        delta = jnp.sum(product * mask_of(p.lat, low_lane), axis=-1, keepdims=True)
        s.stat[...] = jnp.where(lane_stat == head, delta, s.stat[...])

    s.stat_t[...] = s.stat[...].T
    s.stats[h, H : 2 * H, :] = s.stat_t[0:H, :]
    stats_pair = cp.group()
    cp.send(stats_pair, s.stats.at[h], s.stats.at[h], core, z)
    cp.sent(stats_pair, s.stats.at[0])

    @pl.loop(0, tiles)
    def _(i):
        tile = at(i * 256, 256)
        s.res[:, tile] = (s.hid[:, tile] + matmul(s.act[own, :], s.wd[:, tile])).astype(LOW)

    res_pair = cp.group()
    cp.send(res_pair, s.res, res_out.at[own, :], core, z)
    cp.sent(res_pair, s.res)
    stores = [cp.local(s.res, res_out.at[own, :])]

    half_cols = at(h * (p.dl // 2), p.dl // 2)

    class Reduce:
        def __init__(self, left, right, grads, arrive, final, out):
            self.left, self.right, self.out = left, right, out
            self.grads, self.arrive, self.final = grads, arrive, final
            self.part = self.final.shape[0]
            self.rows = self.part * 4
            self.pairs = [cp.group() for _ in range(3)]

        def product(self):
            @pl.loop(0, self.grads.shape[0] // 256)
            def _(i):
                rows = at(i * 256, 256)
                self.grads[rows, :] = matmul_tn(self.left[:, rows], self.right[:, half_cols]).astype(LOW)

        def block(self, zz):
            return self.grads.at[at(zz * self.rows + q * self.part, self.part, 16), :]

        def scatter(self):
            for peer in zed:
                cp.send(self.pairs[0], self.block(peer), self.arrive.at[z], c, peer)
            cp.sent(self.pairs[0], self.arrive.at[0 : zs - 1])

        def add(self):
            cp.got(self.pairs[0], self.arrive.at[0 : zs - 1])
            self.arrive[z] = self.grads[at(z * self.rows + q * self.part, self.part, 16), :]
            total = self.arrive[0].astype(FULL)
            for zz in range(1, zs):
                total = total + self.arrive[zz].astype(FULL)
            self.final[...] = total.astype(LOW)
            here = self.out.at[at(q * self.part, self.part, 16), half_cols]
            for peer in chips:
                cp.send(self.pairs[1], self.final, here, peer, z)
            cp.sent(self.pairs[1], self.arrive.at[0:3])
            self.store = cp.local(self.final, here)

        def spread(self):
            cp.got(self.pairs[1], self.arrive.at[0:3])
            self.store.wait()
            block = self.out.at[:, half_cols]
            cp.send(self.pairs[2], block, block, core, z)
            cp.sent(self.pairs[2], block)

        def done(self):
            cp.got(self.pairs[2], self.out.at[:, half_cols])

    down = Reduce(s.act, s.cot, s.dwd, s.zd, s.fd, gd)
    upper = Reduce(s.mid, s.dup, s.dwu, s.zu, s.fu, gu)
    outer = Reduce(s.att, s.dhid, s.dwo, s.zo, s.fo, go)
    latents = Reduce(s.att, s.dhid, s.dlat, s.zl, s.fl, gl)

    cp.got(act_share, s.act.at[0 : p.lat, :])
    down.product()
    down.scatter()
    cp.got(mid_share, s.mid.at[0 : p.lat, :])
    cp.got(dup_share, s.dup.at[0 : p.lat, :])
    upper.product()
    upper.scatter()
    cp.got(att_share, s.att.at[0 : p.lat, :])
    cp.got(dhid_share, s.dhid.at[0 : p.lat, :])
    outer.product()
    outer.scatter()
    s.dlat[...] = (
        s.dhid[0 : p.lat, half_cols].astype(FULL) + s.dhid[p.lat : 2 * p.lat, half_cols].astype(FULL)
    ).astype(LOW)
    latents.scatter()
    cp.got(datt_share, s.datt.at[0 : p.lat, :])
    cp.got(stats_pair, s.stats.at[0])

    s.dq_t[...] = jnp.zeros_like(s.dq_t)
    sublane = lax.broadcasted_iota(jnp.int32, (p.slots, p.lat), 0)

    @pl.loop(0, p.seqs)
    def _(seq):
        slots = at(seq * p.slots, p.slots)
        latent_rows = at(seq * p.lat, p.lat)
        s.numer[...] = jnp.zeros_like(s.numer)
        s.dk_sum[...] = jnp.zeros_like(s.dk_sum)

        @pl.loop(0, H)
        def _(head):
            heads = at(head * p.lat, p.lat)
            cols, low_lane = window(head)
            raw = matmul_nt(s.keys[slots, :], s.qmask[heads, :])
            valid = start_slot + sublane < lengths[seq]
            top = s.max_all[pl.ds(seq * H + head, 1), :]
            inverse = s.stats[seq, pl.ds(head, 1), :]
            delta = s.stats[seq, pl.ds(H + head, 1), :]
            probs = jnp.exp(jnp.where(valid, raw * score_scale, -1e30) - top) * inverse
            grad = s.datt[latent_rows, cols] * mask_of(p.lat, low_lane).astype(LOW)
            dprobs = matmul_nt(s.values[slots, cols], grad)
            dscores = (probs * (dprobs - delta)).astype(LOW)
            s.numer[:, cols] += matmul(probs.astype(LOW), grad)
            s.dk_sum[...] += matmul(dscores, s.qmask[heads, :])
            block = at(head * p.head, p.head)
            s.dq_t[block, :] += matmul(s.keys_t[block, slots], dscores)

        s.dkeys[slots, :] = (s.dk_sum[...] * score_scale).astype(LOW)
        s.dvalues[slots, :] = s.numer[...].astype(LOW)

    s.dq[...] = (s.dq_t[...] * score_scale).T.astype(LOW)
    qhalf = p.qk // 2
    dq_pairs = [cp.group() for _ in range(4)]
    cp.send(dq_pairs[0], s.dq.at[:, at(other * qhalf, qhalf)], s.dq_in1, core, z)
    cp.sent(dq_pairs[0], s.dq_in1)

    def weight_grads(side):
        kcols = at(side * qhalf, qhalf)
        vcols = at(side * (p.vd // 2), p.vd // 2)

        @pl.loop(0, p.din // 256)
        def _(i):
            rows = at(i * 256, 256)
            s.swk[side, rows, :] = matmul(s.nin_t[rows, :], s.dkeys[:, kcols]).astype(LOW)
            s.swv[side, rows, :] = matmul(s.nin_t[rows, :], s.dvalues[:, vcols]).astype(LOW)

    weight_grads(other)
    kv_pairs = [[cp.group() for _ in range(4)] for _ in range(2)]
    for pairs, send, arrive in ((kv_pairs[0], s.swk, s.rwk), (kv_pairs[1], s.swv, s.rwv)):
        cp.send(pairs[0], send.at[other], arrive, core, z)
        cp.sent(pairs[0], arrive)
    weight_grads(h)

    down.add()
    upper.add()
    outer.add()
    latents.add()
    cp.got(dq_pairs[0], s.dq_in1)
    s.dq_chip[...] = (
        s.dq[:, at(h * qhalf, qhalf)].astype(FULL) + s.dq_in1[...].astype(FULL)
    ).astype(LOW)
    for peer in chips:
        cp.send(dq_pairs[1], s.dq_chip, s.dq_in2.at[q], peer, z)
    cp.sent(dq_pairs[1], s.dq_in2.at[0:3])

    kv = (
        (kv_pairs[0], s.swk, s.rwk, s.cwk, s.pwk_in, s.pwk, s.zwk_in, s.fwk, gk, qhalf),
        (kv_pairs[1], s.swv, s.rwv, s.cwv, s.pwv_in, s.pwv, s.zwv_in, s.fwv, gv, p.vd // 2),
    )
    zrows = p.din // zs
    vpart = zrows // 4
    for pairs, send, arrive, chip, plane_in, plane_sum, z_in, final, out, width in kv:
        cp.got(pairs[0], arrive)

        @pl.loop(0, zs)
        def _(zz):
            rows = at(zz * zrows, zrows)
            chip[zz] = (send[h, rows, :].astype(FULL) + arrive[rows, :].astype(FULL)).astype(LOW)

        for peer in chips:
            rows = at(lax.div(peer, 2) * vpart, vpart)
            cp.send(pairs[1], chip.at[:, rows, :], plane_in.at[q], peer, z)
        cp.sent(pairs[1], plane_in.at[0:3])

    @pl.loop(0, p.rows_in // 64)
    def _(i):
        rows = at(i * 64, 64)
        grad = matmul_nt(s.dkeys[rows, :], s.wk[...]) + matmul_nt(s.dvalues[rows, :], s.wv[...])
        normed, scale = ln_parts(s.feats[rows, :].astype(FULL))
        s.vs[2:3, 0 : p.din] += columns_sum(grad * normed)
        s.vs[3:4, 0 : p.din] += columns_sum(grad)
        s.bgrad[rows, :] = ln_grad(grad, vec[2:3, 0 : p.din], normed, scale).astype(LOW)

    stores.append(cp.local(s.bgrad, byte_out))
    vs_pairs = [cp.group() for _ in range(3)]
    cp.send(vs_pairs[0], s.vs, s.vs_in1, core, z)
    cp.sent(vs_pairs[0], s.vs)

    cp.got(dq_pairs[1], s.dq_in2.at[0:3])
    s.dq_in2[q] = s.dq_chip[...]
    parts = s.dq_in2
    s.dq_plane[...] = (
        (parts[0].astype(FULL) + parts[1].astype(FULL)) + (parts[2].astype(FULL) + parts[3].astype(FULL))
    ).astype(LOW)
    for peer in zed:
        cp.send(dq_pairs[2], s.dq_plane, s.dq_in3.at[z], c, peer)
    cp.sent(dq_pairs[2], s.dq_in3.at[0 : zs - 1])

    cp.got(vs_pairs[0], s.vs_in1)
    s.vs_chip[...] = s.vs[...] + s.vs_in1[...]
    for peer in chips:
        cp.send(vs_pairs[1], s.vs_chip, s.vs_in2.at[q], peer, z)
    cp.sent(vs_pairs[1], s.vs_in2.at[0:3])

    for pairs, send, arrive, chip, plane_in, plane_sum, z_in, final, out, width in kv:
        cp.got(pairs[1], plane_in.at[0:3])
        for zz in range(zs):
            plane_in[q, zz] = chip[zz, at(q * vpart, vpart, 16), :]
        parts = plane_in
        for zz in range(zs):
            plane_sum[zz] = (
                (parts[0, zz].astype(FULL) + parts[1, zz].astype(FULL))
                + (parts[2, zz].astype(FULL) + parts[3, zz].astype(FULL))
            ).astype(LOW)
        for peer in zed:
            cp.send(pairs[2], plane_sum.at[peer], z_in.at[z], c, peer)
        cp.sent(pairs[2], z_in.at[0 : zs - 1])

    cp.got(vs_pairs[1], s.vs_in2.at[0:3])
    s.vs_in2[q] = s.vs_chip[...]
    parts = s.vs_in2
    total = (parts[0] + parts[1]) + (parts[2] + parts[3])
    row_ids = lax.broadcasted_iota(jnp.int32, (8, p.dl), 0)
    s.vs_plane[...] = jnp.where(row_ids < 2, s.vs_chip[...], total)
    for peer in zed:
        cp.send(vs_pairs[2], s.vs_plane, s.vs_in3.at[z], c, peer)
    cp.sent(vs_pairs[2], s.vs_in3.at[0 : zs - 1])

    reduces = (down, upper, outer, latents)
    for reduce in reduces:
        reduce.spread()

    cp.got(dq_pairs[2], s.dq_in3.at[0 : zs - 1])
    s.dq_in3[z] = s.dq_plane[...]
    parts = s.dq_in3
    total = parts[0].astype(FULL)
    for zz in range(1, zs):
        total = total + parts[zz].astype(FULL)
    own_half = at(h * qhalf, qhalf)
    s.dq_all[:, own_half] = total.astype(LOW)
    cp.send(dq_pairs[3], s.dq_all.at[:, own_half], s.dq_all.at[:, own_half], core, z)
    cp.sent(dq_pairs[3], s.dq_in1)

    for pairs, send, arrive, chip, plane_in, plane_sum, z_in, final, out, width in kv:
        cp.got(pairs[2], z_in.at[0 : zs - 1])
        z_in[z] = plane_sum[z]
        total = z_in[0].astype(FULL)
        for zz in range(1, zs):
            total = total + z_in[zz].astype(FULL)
        final[...] = total.astype(LOW)
        here = out.at[at(q * vpart, vpart, 16), at(h * width, width)]
        for peer in plane:
            cp.send(pairs[3], final, here, peer, z)
        cp.sent(pairs[3], send.at[0, 0 : (ctx - 1) * vpart, :])
        stores.append(cp.local(final, here))

    cp.got(dq_pairs[3], s.dq_in1)

    @pl.loop(0, tiles)
    def _(i):
        tile = at(i * 256, 256)
        s.gq[tile, :] = matmul_tn(s.nlat[:, tile], s.dq_all[...])
        s.dmid[:, tile] = matmul_nt(s.dq_all[...], s.wq[tile, :])

    stores.append(cp.local(s.gq.at[at(z * (p.dl // zs), p.dl // zs, 16), :], gq_out))
    cp.got(vs_pairs[2], s.vs_in3.at[0 : zs - 1])
    s.vs_in3[z] = s.vs_plane[...]
    total = s.vs_in3[0]
    for zz in range(1, zs):
        total = total + s.vs_in3[zz]
    s.vs_all[...] = total
    s.vs_all[4:6, :] = jnp.zeros((2, p.dl), FULL)

    @pl.loop(0, p.lat // 64)
    def _(i):
        rows = at(i * 64, 64)
        normed, scale = ln_parts(s.lat[rows, :].astype(FULL))
        grad = s.dmid[rows, :]
        s.vs_all[4:5, :] += columns_sum(grad * normed)
        s.vs_all[5:6, :] += columns_sum(grad)
        s.slope[rows, :] = ln_grad(grad, gain_lat, normed, scale)

    stores.append(cp.local(s.slope.at[at(z * (p.lat // zs), p.lat // zs, 16), :], glat_out))
    stores.append(cp.local(s.vs_all, vec_out))
    for reduce in reduces:
        reduce.done()
    cp.got(res_pair, s.res)
    for pairs, send, *_ in kv:
        cp.got(pairs[3], send.at[0, 0 : (ctx - 1) * vpart, :])
    for store in stores:
        store.wait()
    cp.drain()


def finish_kernel(p, res, byte, go, gu, gd, gv, gk, gl, gq, glat, vec, *outs):
    z = lax.axis_index("wshard")
    outs[0][...] = res[...]
    outs[1][...] = byte[...]
    outs[2][...] = glat[...] + gl[...].astype(FULL)
    for out, row in ((3, 4), (4, 5), (5, 2), (6, 3), (11, 0), (12, 1)):
        size = outs[out].shape[1]
        picked = vec[row : row + 1, 0:size]
        for zz in range(1, p.zs):
            picked = jnp.where(z == zz, vec[row : row + 1, zz * size : (zz + 1) * size], picked)
        outs[out][...] = picked
    outs[7][...] = gq[...]
    for out, source in ((8, gk), (9, gv), (10, go), (13, gu), (14, gd)):
        outs[out][...] = source[...].astype(FULL)


def fused(*args):
    (byte_feats, lengths, latent, *smalls, cot) = (args[0], args[1], args[2], *args[3:7], args[11], args[12], args[15])
    w_query, w_key, w_value, w_output = args[7:11]
    w_up, w_down = args[13:15]
    seqs, slots, din = byte_feats.shape
    ctx, zs = lax.axis_size("ctx"), lax.axis_size("wshard")
    feats = byte_feats.reshape(seqs * slots, din)
    cot_flat = cot.reshape(-1, cot.shape[-1])
    smalls = [small.reshape(1, -1) for small in smalls]
    p = Plan(ctx, zs, feats, latent, w_query, w_key, w_value, w_output, cot_flat)
    table = scratch_table(p)
    anywhere = pl.BlockSpec(memory_space=pl.ANY)
    in_vmem = pl.BlockSpec(memory_space=pltpu.VMEM)
    struct = jax.ShapeDtypeStruct
    made = pl.pallas_call(
        functools.partial(fused_kernel, p, tuple(table)),
        out_shape=(
            struct(cot_flat.shape, LOW),
            struct(feats.shape, LOW),
            struct(w_output.shape, LOW),
            struct(w_up.shape, LOW),
            struct(w_down.shape, LOW),
            struct(w_value.shape, LOW),
            struct(w_key.shape, LOW),
            struct(latent.shape, LOW),
            struct(w_query.shape, FULL),
            struct(latent.shape, FULL),
            struct((8, p.dl), FULL),
        ),
        in_specs=[pl.BlockSpec(memory_space=pltpu.SMEM)] + [anywhere] * 8 + [in_vmem] * 6 + [anywhere],
        out_specs=(anywhere,) * 11,
        scratch_shapes=[pltpu.VMEM(shape, kind) for shape, kind in table.values()]
        + [pltpu.SemaphoreType.DMA((SEMS,))],
        compiler_params=pltpu.CompilerParams(
            collective_id=0, has_side_effects=True, vmem_limit_bytes=67043328
        ),
        name="block",
    )(lengths, feats, latent, w_query, w_key, w_value, w_output, w_up, w_down, *smalls, cot_flat)
    shapes = (
        (cot_flat.shape, LOW),
        (feats.shape, LOW),
        (latent.shape, FULL),
        *((smalls[i].shape, FULL) for i in range(4)),
        *((w.shape, FULL) for w in (w_query, w_key, w_value, w_output)),
        *((smalls[i].shape, FULL) for i in (4, 5)),
        *((w.shape, FULL) for w in (w_up, w_down)),
    )
    outs = pl.pallas_call(
        functools.partial(finish_kernel, p),
        out_shape=tuple(struct(shape, kind) for shape, kind in shapes),
        in_specs=[in_vmem] * 11,
        out_specs=(in_vmem,) * 15,
        compiler_params=pltpu.CompilerParams(vmem_limit_bytes=60 * 2**20),
        name="finish",
    )(*made)
    return tuple(
        out.reshape(-1) if out.shape[0] == 1 else out
        for out in (outs[0].reshape(cot.shape), outs[1].reshape(byte_feats.shape), *outs[2:])
    )


def shards(*args):
    if lax.axis_size("ctx") == 8 and lax.axis_size("wshard") == 4 and args[0].shape[0] == 2:
        return fused(*args)
    return plain(*args)


def solution(mesh):
    sharded, plain = P("wshard", None), P("wshard")
    return jax.shard_map(
        shards,
        mesh=mesh,
        in_specs=(
            P("wshard", "ctx", None),
            plain,
            sharded,
            plain,
            plain,
            plain,
            plain,
            sharded,
            sharded,
            sharded,
            sharded,
            plain,
            plain,
            sharded,
            sharded,
            P("wshard", None, None),
        ),
        out_specs=(
            P("wshard", None, None),
            P("wshard", "ctx", None),
            sharded,
            plain,
            plain,
            plain,
            plain,
            sharded,
            sharded,
            sharded,
            sharded,
            plain,
            plain,
            sharded,
            sharded,
        ),
        check_vma=False,
    )
```

```python
import functools
import math
import types

import jax
import jax.numpy as jnp
from jax import lax
from jax.experimental import pallas as pl
from jax.experimental.pallas import tpu as pltpu
from jax.sharding import PartitionSpec as P

H = 8
LOW = jnp.bfloat16
FULL = jnp.float32


def layer_norm(values, gain, offset):
    center = jnp.mean(values, axis=-1, keepdims=True)
    centred = values - center
    variance = jnp.mean(centred * centred, axis=-1, keepdims=True)
    return centred * lax.rsqrt(variance + 1e-05) * gain + offset


def exact_gelu(values):
    return jax.nn.gelu(values, approximate=False)


def matmul(left, right):
    return jnp.dot(left, right, preferred_element_type=FULL)


def matmul_tn(left, right):
    return lax.dot_general(left, right, (((0,), (0,)), ((), ())), preferred_element_type=FULL)


def matmul_nt(left, right):
    return lax.dot_general(left, right, (((1,), (1,)), ((), ())), preferred_element_type=FULL)


def gather(shard):
    return lax.all_gather(shard, "wshard", axis=0, tiled=True)


def scatter(total):
    return lax.psum_scatter(
        total.astype(LOW), "wshard", scatter_dimension=0, tiled=True
    ).astype(FULL)


SEMS = 224


def own_part(total, shard):
    size = shard.shape[0]
    return lax.dynamic_slice_in_dim(total, lax.axis_index("wshard") * size, size, 0)


def plain(
    byte_feats,
    lengths,
    latent_array,
    lat_gain,
    lat_bias,
    in_gain,
    in_bias,
    w_query,
    w_key,
    w_value,
    w_output,
    mlp_gain,
    mlp_bias,
    w_up,
    w_down,
    cotangent,
):
    seqs, slots, width = byte_feats.shape
    gain_in, bias_in = gather(in_gain).astype(FULL), gather(in_bias).astype(FULL)
    key_w, value_w = gather(w_key), gather(w_value)
    latent = gather(latent_array).astype(FULL)
    gain_lat, bias_lat = gather(lat_gain).astype(FULL), gather(lat_bias).astype(FULL)
    query_w = gather(w_query)
    gain_mlp, bias_mlp = gather(mlp_gain).astype(FULL), gather(mlp_bias).astype(FULL)
    output_w, up_w, down_w = gather(w_output), gather(w_up), gather(w_down)

    features = byte_feats.reshape(seqs * slots, width).astype(FULL)
    normed_in, in_back = jax.vjp(layer_norm, features, gain_in, bias_in)
    input_low = normed_in.astype(LOW)
    keys = matmul(input_low, key_w).astype(LOW)
    values = matmul(input_low, value_w).astype(LOW)
    normed_lat, lat_back = jax.vjp(layer_norm, latent, gain_lat, bias_lat)
    lat_low = normed_lat.astype(LOW)
    rows = lat_low.shape[0]
    queries = matmul(lat_low, query_w).astype(LOW)
    score_scale = 1.0 / math.sqrt(queries.shape[1] // H)
    qheads = queries.reshape(rows, H, -1)
    kheads = keys.reshape(seqs, slots, H, -1)
    vheads = values.reshape(seqs, slots, H, -1)

    scores = jnp.einsum("lhd,mkhd->mhlk", qheads, kheads, preferred_element_type=FULL) * score_scale
    slot_ids = lax.axis_index("ctx") * slots + lax.iota(jnp.int32, slots)
    valid = (slot_ids[None, :] < lengths[:, None])[:, None, None, :]
    scores = jnp.where(valid, scores, -1e30)
    highest = lax.pmax(jnp.max(scores, axis=-1), "ctx")
    weights = jnp.where(valid, jnp.exp(scores - highest[..., None]), 0.0)
    total = lax.psum(jnp.sum(weights, axis=-1), "ctx")
    numer = jnp.einsum("mhlk,mkhe->mlhe", weights.astype(LOW), vheads, preferred_element_type=FULL)
    numer = lax.psum(numer.astype(LOW), "ctx").astype(FULL)
    attended = numer / jnp.transpose(total, (0, 2, 1))[..., None]
    attended = attended.reshape(seqs * rows, -1)

    att_low = attended.astype(LOW)
    hidden = jnp.tile(latent, (seqs, 1)) + matmul(att_low, output_w)
    normed_mid, mid_back = jax.vjp(layer_norm, hidden, gain_mlp, bias_mlp)
    mid_low = normed_mid.astype(LOW)
    upward = matmul(mid_low, up_w)
    activated, gelu_back = jax.vjp(exact_gelu, upward)
    act_low = activated.astype(LOW)
    result = hidden + matmul(act_low, down_w)
    dout_low = cotangent.reshape(seqs * rows, -1)
    grad_down = scatter(matmul_tn(act_low, dout_low))
    (grad_upward,) = gelu_back(matmul_nt(dout_low, down_w))
    up_low = grad_upward.astype(LOW)
    grad_up = scatter(matmul_tn(mid_low, up_low))
    dhid_norm, grad_gmlp, grad_bmlp = mid_back(matmul_nt(up_low, up_w))
    dhidden = dout_low.astype(FULL) + dhid_norm
    dhid_low = dhidden.astype(LOW)
    grad_output = scatter(matmul_tn(att_low, dhid_low))
    grad_hidden = scatter(jnp.sum(dhidden.reshape(seqs, rows, -1), axis=0))
    grad_att = matmul_nt(dhid_low, output_w).astype(LOW)

    grad_heads = grad_att.reshape(seqs, rows, H, -1)
    delta = jnp.sum(
        grad_heads.astype(FULL) * attended.reshape(seqs, rows, H, -1), axis=-1
    ).transpose(0, 2, 1)
    probs = weights / total[..., None]
    dprobs = jnp.einsum("mlhe,mkhe->mhlk", grad_heads, vheads, preferred_element_type=FULL)
    dscores = (probs * (dprobs - delta[..., None])).astype(LOW)
    dquery = jnp.einsum("mhlk,mkhd->lhd", dscores, kheads, preferred_element_type=FULL) * score_scale
    dkeys = jnp.einsum("mhlk,lhd->mkhd", dscores, qheads, preferred_element_type=FULL) * score_scale
    dvalues = jnp.einsum("mhlk,mlhe->mkhe", probs.astype(LOW), grad_heads, preferred_element_type=FULL)
    dkeys = dkeys.astype(LOW).reshape(seqs * slots, -1)
    dvalues = dvalues.astype(LOW).reshape(seqs * slots, -1)

    dquery = lax.psum(dquery.reshape(rows, -1).astype(LOW), ("ctx", "wshard"))
    grad_query = matmul_tn(
        lax.dynamic_slice_in_dim(
            lat_low, lax.axis_index("wshard") * w_query.shape[0], w_query.shape[0], 1
        ),
        dquery,
    )
    dlat_norm, grad_glat, grad_blat = lat_back(matmul_nt(dquery, query_w))
    grad_latent = grad_hidden + own_part(dlat_norm, latent_array)

    dnorm_in = matmul_nt(dkeys, key_w) + matmul_nt(dvalues, value_w)
    dfeatures, grad_gin, grad_bin = in_back(dnorm_in)
    grad_key = lax.psum(scatter(matmul_tn(input_low, dkeys)).astype(LOW), "ctx").astype(FULL)
    grad_value = lax.psum(scatter(matmul_tn(input_low, dvalues)).astype(LOW), "ctx").astype(FULL)
    in_sums = lax.psum(jnp.concatenate([grad_gin, grad_bin]), ("ctx", "wshard"))
    grad_gin, grad_bin = jnp.split(in_sums, 2)
    mlp_sums = lax.psum(jnp.concatenate([grad_gmlp, grad_bmlp]), "wshard")
    grad_gmlp, grad_bmlp = jnp.split(mlp_sums, 2)
    return (
        result.astype(LOW).reshape(seqs, rows, -1),
        dfeatures.astype(LOW).reshape(seqs, slots, width),
        grad_latent,
        own_part(grad_glat, lat_gain),
        own_part(grad_blat, lat_bias),
        own_part(grad_gin, in_gain),
        own_part(grad_bin, in_bias),
        grad_query,
        grad_key,
        grad_value,
        grad_output,
        own_part(grad_gmlp, mlp_gain),
        own_part(grad_bmlp, mlp_bias),
        grad_up,
        grad_down,
    )


def ln_parts(values):
    centred = values - jnp.mean(values, axis=-1, keepdims=True)
    scale = lax.rsqrt(jnp.mean(centred * centred, axis=-1, keepdims=True) + 1e-05)
    return centred * scale, scale


def ln_grad(cotangent, gain, normed, scale):
    scaled = cotangent * gain
    first = jnp.mean(scaled, axis=-1, keepdims=True)
    second = jnp.mean(scaled * normed, axis=-1, keepdims=True)
    return scale * (scaled - first - normed * second)


def lanes(rows, columns):
    return lax.broadcasted_iota(jnp.int32, (rows, columns), 1)


def columns_sum(values):
    return jnp.sum(values, axis=0, keepdims=True)


class Plan:
    def __init__(self, ctx, zs, feats, latent, w_query, w_key, w_value, w_output, cot):
        self.ctx, self.zs = ctx, zs
        self.rows_in, self.din = feats.shape
        self.lat = latent.shape[0] * zs
        self.dl = latent.shape[1]
        self.qk, self.vd = w_key.shape[1], w_value.shape[1]
        self.seqs = cot.shape[0] // self.lat
        self.slots = self.rows_in // self.seqs
        self.head, self.vhead = self.qk // H, self.vd // H


def scratch_table(p):
    both = p.seqs * p.lat
    half = p.dl // 2
    part = p.dl // p.zs // 4
    vpart = p.din // p.zs // 4
    return dict(
        wk=((p.din, p.qk), LOW),
        wq=((p.dl, p.qk), LOW),
        lat=((p.lat, p.dl), LOW),
        wv=((p.din, p.vd), LOW),
        wo=((p.vd, p.dl), LOW),
        wu=((p.dl, p.dl), LOW),
        wd=((p.dl, p.dl), LOW),
        small_own=((8, 384), FULL),
        small=((p.zs, 8, 384), FULL),
        vec=((8, p.dl), FULL),
        feats=((p.rows_in, p.din), LOW),
        nin=((p.rows_in, p.din), LOW),
        nin_t=((p.din, p.rows_in), LOW),
        keys=((p.rows_in, p.qk), LOW),
        keys_t=((p.qk, p.rows_in), LOW),
        values=((p.rows_in, p.vd), LOW),
        nlat=((p.lat, p.dl), LOW),
        qmask=((H * p.lat, p.qk), LOW),
        scores=((p.seqs * H * p.lat, p.slots), FULL),
        stat=((p.lat, 128), FULL),
        stat_t=((128, p.lat), FULL),
        max_own=((2 * H, p.lat), FULL),
        max_in=((p.ctx, 2 * H, p.lat), FULL),
        max_all=((2 * H, p.lat), FULL),
        numer=((p.lat, p.vd), FULL),
        numer_low=((p.lat, p.vd), LOW),
        numer_in=((p.lat, p.vd), LOW),
        sums=((2, H, p.lat), FULL),
        sums_in=((H, p.lat), FULL),
        chip=((p.lat, p.vd), LOW),
        chip_in=((4, p.lat // 4, p.vd), LOW),
        chip_sums=((H, p.lat), FULL),
        chip_sums_in=((4, H, p.lat), FULL),
        scale=((p.lat // 4, p.vd), FULL),
        att=((both, p.vd), LOW),
        mid=((both, p.dl), LOW),
        act=((both, p.dl), LOW),
        dup=((both, p.dl), LOW),
        dhid=((both, p.dl), LOW),
        datt=((both, p.vd), LOW),
        cot=((both, p.dl), LOW),
        hid=((p.lat, p.dl), FULL),
        slope=((p.lat, p.dl), FULL),
        dmid=((p.lat, p.dl), FULL),
        res=((p.lat, p.dl), LOW),
        stats=((2, 2 * H, p.lat), FULL),
        dwo=((p.vd, half), LOW),
        dwu=((p.dl, half), LOW),
        dwd=((p.dl, half), LOW),
        dlat=((p.lat, half), LOW),
        zo=((p.zs, part, half), LOW),
        zu=((p.zs, part, half), LOW),
        zd=((p.zs, part, half), LOW),
        zl=((p.zs, p.lat // p.zs // 4, half), LOW),
        fo=((part, half), LOW),
        fu=((part, half), LOW),
        fd=((part, half), LOW),
        fl=((p.lat // p.zs // 4, half), LOW),
        dkeys=((p.rows_in, p.qk), LOW),
        dvalues=((p.rows_in, p.vd), LOW),
        dk_sum=((p.slots, p.qk), FULL),
        dq_t=((p.qk, p.lat), FULL),
        dq=((p.lat, p.qk), LOW),
        dq_in1=((p.lat, p.qk // 2), LOW),
        dq_chip=((p.lat, p.qk // 2), LOW),
        dq_in2=((4, p.lat, p.qk // 2), LOW),
        dq_plane=((p.lat, p.qk // 2), LOW),
        dq_in3=((p.zs, p.lat, p.qk // 2), LOW),
        dq_all=((p.lat, p.qk), LOW),
        bgrad=((p.rows_in, p.din), LOW),
        swk=((2, p.din, p.qk // 2), LOW),
        swv=((2, p.din, p.vd // 2), LOW),
        rwk=((p.din, p.qk // 2), LOW),
        rwv=((p.din, p.vd // 2), LOW),
        cwk=((p.zs, p.din // p.zs, p.qk // 2), LOW),
        cwv=((p.zs, p.din // p.zs, p.vd // 2), LOW),
        pwk_in=((4, p.zs, vpart, p.qk // 2), LOW),
        pwv_in=((4, p.zs, vpart, p.vd // 2), LOW),
        pwk=((p.zs, vpart, p.qk // 2), LOW),
        pwv=((p.zs, vpart, p.vd // 2), LOW),
        zwk_in=((p.zs, vpart, p.qk // 2), LOW),
        zwv_in=((p.zs, vpart, p.vd // 2), LOW),
        fwk=((vpart, p.qk // 2), LOW),
        fwv=((vpart, p.vd // 2), LOW),
        vs=((8, p.dl), FULL),
        vs_in1=((8, p.dl), FULL),
        vs_chip=((8, p.dl), FULL),
        vs_in2=((4, 8, p.dl), FULL),
        vs_plane=((8, p.dl), FULL),
        vs_in3=((p.zs, 8, p.dl), FULL),
        vs_all=((8, p.dl), FULL),
        gq=((p.dl, p.qk), FULL),
    )


class Copies:
    def __init__(self, sems):
        self.sems, self.used, self.open = sems, 0, []

    def new(self):
        self.used += 1
        return self.sems.at[self.used - 1]

    def group(self):
        return (self.new(), self.new())

    def send(self, pair, src, dst, ctx, z):
        pltpu.make_async_remote_copy(
            src_ref=src,
            dst_ref=dst,
            send_sem=pair[0],
            recv_sem=pair[1],
            device_id=(ctx, z),
            device_id_type=pl.DeviceIdType.MESH,
        ).start()

    def local(self, src, dst):
        copy = pltpu.make_async_copy(src, dst, self.new())
        copy.start()
        return copy

    def got(self, pair, view):
        pltpu.make_async_copy(view, view, pair[1]).wait()

    def sent(self, pair, view):
        self.open.append((pair[0], view))

    def drain(self):
        for sem, view in self.open:
            pltpu.make_async_copy(view, view, sem).wait()


def at(start, size, step=None):
    return pl.ds(pl.multiple_of(start, step or size), size)


def fused_kernel(p, names, *refs):
    ins, refs = refs[:16], refs[16:]
    lengths, feats_in, lat_in, wq_in, wk_in, wv_in, wo_in, wu_in, wd_in = ins[:9]
    smalls, cot_in = ins[9:15], ins[15]
    outs, refs = refs[:11], refs[11:]
    res_out, byte_out, go, gu, gd, gv, gk, gl, gq_out, glat_out, vec_out = outs
    sems = refs[-1]
    s = types.SimpleNamespace(**dict(zip(names, refs[:-1])))
    cp = Copies(sems)
    ctx, zs = p.ctx, p.zs
    c, z = lax.axis_index("ctx"), lax.axis_index("wshard")
    h, q = lax.rem(c, 2), lax.div(c, 2)
    x, y = lax.rem(q, 2), lax.div(q, 2)
    other = 1 - h
    core = c + 1 - 2 * h
    chips = (c + 2 - 4 * x, c + 4 - 8 * y, c + 6 - 4 * x - 8 * y)
    near = (chips[0] * (1 - h) + chips[1] * h, chips[1] * (1 - h) + chips[0] * h)
    zed = [lax.rem(z + j, zs) for j in range(1, zs)]
    plane = [lax.rem(c + j, ctx) for j in range(1, ctx)]

    barrier = pltpu.get_barrier_semaphore()
    for peer in plane:
        pl.semaphore_signal(barrier, inc=1, device_id=(peer, z), device_id_type=pl.DeviceIdType.MESH)
    for peer in zed:
        pl.semaphore_signal(barrier, inc=1, device_id=(c, peer), device_id_type=pl.DeviceIdType.MESH)
    pl.semaphore_wait(barrier, ctx - 1 + zs - 1)

    load_feats = cp.local(feats_in, s.feats)
    for row, ref in enumerate(smalls):
        s.small_own[row : row + 1, 0 : ref.shape[0]] = ref[...].reshape(1, -1).astype(FULL)
    small_pair = cp.group()
    for peer in zed:
        cp.send(small_pair, s.small_own, s.small.at[z], c, peer)
    cp.sent(small_pair, s.small.at[0 : zs - 1])

    class Weight:
        def __init__(self, ref, source, cuts):
            self.ref, self.source, self.cuts = ref, source, cuts
            self.rows, cols = source.shape
            self.part, self.cols = self.rows // cuts, cols // 2
            self.slot = q if cuts == 4 else lax.rem(x + y, 2)
            self.mine = at(h * self.cols, self.cols)
            self.pairs = [cp.group() for _ in range(4)]

        def view(self, rows):
            return self.ref.at[pl.ds(0, rows), pl.ds(0, self.cols)]

        def block(self, zz, qq):
            return self.ref.at[at(zz * self.rows + qq * self.part, self.part, 16), self.mine]

        def start(self):
            for peer in zed:
                cp.send(
                    self.pairs[0],
                    self.source.at[at(self.slot * self.part, self.part, 16), self.mine],
                    self.block(z, self.slot),
                    c,
                    peer,
                )
            cp.sent(self.pairs[0], self.view(3 * self.part))
            self.load = cp.local(self.source, self.ref.at[at(z * self.rows, self.rows, 16), :])

        def first(self):
            cp.got(self.pairs[0], self.view(3 * self.part))
            for zz in zed:
                block = self.block(zz, self.slot)
                cp.send(self.pairs[1], block, block, near[0], z)
            cp.sent(self.pairs[1], self.view(3 * self.part))

        def second(self):
            cp.got(self.pairs[1], self.view(3 * self.part))
            for zz in zed:
                for qq in (q, lax.div(near[0], 2)):
                    block = self.block(zz, qq)
                    cp.send(self.pairs[2], block, block, near[1], z)
            cp.sent(self.pairs[2], self.view(6 * self.part))

        def third(self):
            if self.cuts == 4:
                cp.got(self.pairs[2], self.view(6 * self.part))
            else:
                cp.got(self.pairs[1], self.view(3 * self.part))
            for zz in zed:
                block = self.ref.at[at(zz * self.rows, self.rows, 16), self.mine]
                cp.send(self.pairs[3], block, block, core, z)
            cp.sent(self.pairs[3], self.view(3 * self.rows))

        def ready(self):
            cp.got(self.pairs[3], self.view(3 * self.rows))
            self.load.wait()

    wk, wq, lat = Weight(s.wk, wk_in, 4), Weight(s.wq, wq_in, 4), Weight(s.lat, lat_in, 4)
    wv, wo = Weight(s.wv, wv_in, 4), Weight(s.wo, wo_in, 4)
    wu, wd = Weight(s.wu, wu_in, 2), Weight(s.wd, wd_in, 2)
    for weight in (wk, wq, lat, wv, wo, wu, wd):
        weight.start()
    load_cot = cp.local(cot_in, s.cot)

    cp.got(small_pair, s.small.at[0 : zs - 1])
    s.small[z] = s.small_own[...]
    for row, ref in enumerate(smalls):
        size = ref.shape[0]
        for zz in range(zs):
            s.vec[row : row + 1, zz * size : (zz + 1) * size] = s.small[zz, row : row + 1, 0:size]
    vec = s.vec
    gain_lat, bias_lat = vec[0:1, :], vec[1:2, :]

    load_feats.wait()

    @pl.loop(0, p.rows_in // 64)
    def _(i):
        rows = at(i * 64, 64)
        normed, _ = ln_parts(s.feats[rows, :].astype(FULL))
        s.nin[rows, :] = (normed * vec[2:3, 0 : p.din] + vec[3:4, 0 : p.din]).astype(LOW)

    wk.first()
    wq.first()
    lat.first()

    @pl.loop(0, p.din // 128)
    def _(i):
        tile = at(i * 128, 128)
        s.nin_t[tile, :] = s.nin[:, tile].T

    wk.second()
    wq.second()
    lat.second()
    wk.third()
    wq.third()
    lat.third()
    wk.ready()

    @pl.loop(0, p.seqs)
    def _(i):
        rows = at(i * p.slots, p.slots)
        low = matmul(s.nin[rows, :], s.wk[...]).astype(LOW)
        s.keys[rows, :] = low
        s.keys_t[:, rows] = low.T

    wv.first()
    lat.ready()

    @pl.loop(0, p.lat // 64)
    def _(i):
        rows = at(i * 64, 64)
        normed, _ = ln_parts(s.lat[rows, :].astype(FULL))
        s.nlat[rows, :] = (normed * gain_lat + bias_lat).astype(LOW)

    wq.ready()
    queries = matmul(s.nlat[...], s.wq[...])
    lane_q = lanes(p.lat, p.qk)
    for head in range(H):
        inside = (lane_q >= head * p.head) & (lane_q < (head + 1) * p.head)
        s.qmask[head * p.lat : (head + 1) * p.lat, :] = jnp.where(inside, queries, 0.0).astype(LOW)

    wv.second()
    score_scale = 1.0 / math.sqrt(p.head)
    start_slot = c * p.slots
    s.stat[...] = jnp.zeros_like(s.stat)
    lane_stat = lanes(p.lat, 128)

    @pl.loop(0, p.seqs * H)
    def _(i):
        seq, head = lax.div(i, H), lax.rem(i, H)
        raw = matmul_nt(
            s.qmask[at(head * p.lat, p.lat), :], s.keys[at(seq * p.slots, p.slots), :]
        )
        valid = start_slot + lanes(p.lat, p.slots) < lengths[seq]
        scores = jnp.where(valid, raw * score_scale, -1e30)
        s.scores[at(i * p.lat, p.lat), :] = scores
        top = jnp.max(scores, axis=-1, keepdims=True)
        s.stat[...] = jnp.where(lane_stat == i, top, s.stat[...])

    s.stat_t[...] = s.stat[...].T
    s.max_own[...] = s.stat_t[0 : 2 * H, :]
    max_pair = cp.group()
    for peer in plane:
        cp.send(max_pair, s.max_own, s.max_in.at[c], peer, z)
    cp.sent(max_pair, s.max_in.at[0 : ctx - 1])

    wv.third()
    wo.first()
    wv.ready()

    @pl.loop(0, p.vd // 256)
    def _(i):
        tile = at(i * 256, 256)
        s.values[:, tile] = matmul(s.nin[...], s.wv[:, tile]).astype(LOW)

    wo.second()
    cp.got(max_pair, s.max_in.at[0 : ctx - 1])
    s.max_in[c] = s.max_own[...]
    top = s.max_in[0]
    for i in range(1, ctx):
        top = jnp.maximum(top, s.max_in[i])
    s.max_all[...] = top
    s.stat_t[0 : 2 * H, :] = top
    max_columns = s.stat_t[...].T
    s.stat[...] = jnp.zeros_like(s.stat)

    def window(head):
        low_lane = pl.multiple_of(lax.div(head * p.vhead, 128) * 128, 128)
        return pl.ds(low_lane, 256), head * p.vhead - low_lane

    def mask_of(rows, low_lane):
        lane = lanes(rows, 256)
        return ((lane >= low_lane) & (lane < low_lane + p.vhead)).astype(FULL)

    def partial(seq):
        s.numer[...] = jnp.zeros_like(s.numer)

        @pl.loop(0, H)
        def _(head):
            i = seq * H + head
            top = jnp.sum(jnp.where(lane_stat == i, max_columns, 0.0), axis=-1, keepdims=True)
            weights = jnp.exp(s.scores[at(i * p.lat, p.lat), :] - top)
            total = jnp.sum(weights, axis=-1, keepdims=True)
            s.stat[...] = jnp.where(lane_stat == i, total, s.stat[...])
            cols, low_lane = window(head)
            part = s.values[at(seq * p.slots, p.slots), cols] * mask_of(p.slots, low_lane).astype(LOW)
            s.numer[:, cols] += matmul(weights.astype(LOW), part)

        s.stat_t[...] = s.stat[...].T
        s.sums[seq] = s.stat_t[at(seq * H, H), :]

    partial(other)
    s.numer_low[...] = s.numer[...].astype(LOW)
    pair_pair = cp.group()
    sums_pair = cp.group()
    cp.send(pair_pair, s.numer_low, s.numer_in, core, z)
    cp.send(sums_pair, s.sums.at[other], s.sums_in, core, z)
    cp.sent(pair_pair, s.numer_low)
    cp.sent(sums_pair, s.sums_in)
    partial(h)

    cp.got(pair_pair, s.numer_in)
    cp.got(sums_pair, s.sums_in)
    quarter = p.lat // 4
    s.chip[...] = (s.numer[...] + s.numer_in[...].astype(FULL)).astype(LOW)
    s.chip_sums[...] = s.sums[h] + s.sums_in[...]
    chip_pair = cp.group()
    chip_sums_pair = cp.group()
    for peer in chips:
        peer_chip = lax.div(peer, 2)
        cp.send(chip_pair, s.chip.at[at(peer_chip * quarter, quarter), :], s.chip_in.at[q], peer, z)
        cp.send(chip_sums_pair, s.chip_sums, s.chip_sums_in.at[q], peer, z)
    cp.sent(chip_pair, s.chip_in.at[0:3])
    cp.sent(chip_sums_pair, s.chip_sums_in.at[0:3])
    wu.first()
    wo.third()

    cp.got(chip_sums_pair, s.chip_sums_in.at[0:3])
    s.chip_sums_in[q] = s.chip_sums[...]
    sums = s.chip_sums_in
    inverse = 1.0 / ((sums[0] + sums[1]) + (sums[2] + sums[3]))
    s.stats[h, 0:H, :] = inverse
    s.stat_t[0:H, :] = inverse
    s.stat[...] = s.stat_t[...].T
    s.scale[...] = jnp.zeros_like(s.scale)
    own_quarter = s.stat[at(q * quarter, quarter), :]
    for head in range(H):
        low_lane = head * p.vhead // 128 * 128
        lane = lanes(quarter, 256) + low_lane
        inside = (lane >= head * p.vhead) & (lane < (head + 1) * p.vhead)
        cols = slice(low_lane, low_lane + 256)
        s.scale[:, cols] = jnp.where(inside, own_quarter[:, head : head + 1], s.scale[:, cols])
    cp.got(chip_pair, s.chip_in.at[0:3])
    s.chip_in[q] = s.chip[at(q * quarter, quarter), :]
    numer = s.chip_in
    added = (numer[0].astype(FULL) + numer[1].astype(FULL)) + (numer[2].astype(FULL) + numer[3].astype(FULL))
    own_rows = at(h * p.lat + q * quarter, quarter)
    s.att[own_rows, :] = (added * s.scale[...]).astype(LOW)
    att_pair = cp.group()
    for peer in chips:
        cp.send(att_pair, s.att.at[own_rows, :], s.att.at[own_rows, :], peer, z)
    cp.sent(att_pair, s.att.at[0 : 3 * quarter, :])
    wo.ready()
    own = at(h * p.lat, p.lat)
    cp.got(att_pair, s.att.at[0 : 3 * quarter, :])

    def share(ref):
        pair = cp.group()
        cp.send(pair, ref.at[own, :], ref.at[own, :], core, z)
        cp.sent(pair, ref.at[0 : p.lat, :])
        return pair

    att_share = share(s.att)
    wd.first()
    tiles = p.dl // 256

    @pl.loop(0, tiles)
    def _(i):
        tile = at(i * 256, 256)
        s.hid[:, tile] = s.lat[:, tile].astype(FULL) + matmul(s.att[own, :], s.wo[:, tile])

    wu.third()
    gain_mlp, bias_mlp = vec[4:5, :], vec[5:6, :]

    @pl.loop(0, p.lat // 64)
    def _(i):
        normed, _ = ln_parts(s.hid[at(i * 64, 64), :])
        s.mid[at(h * p.lat + i * 64, 64), :] = (normed * gain_mlp + bias_mlp).astype(LOW)

    mid_share = share(s.mid)
    wu.ready()
    load_cot.wait()

    @pl.loop(0, tiles)
    def _(i):
        tile = at(i * 256, 256)
        up = matmul(s.mid[own, :], s.wu[:, tile])
        cdf = 0.5 * (1.0 + lax.erf(up * (1.0 / math.sqrt(2.0))))
        density = jnp.exp(-0.5 * up * up) * (1.0 / math.sqrt(2.0 * math.pi))
        s.act[own, tile] = (up * cdf).astype(LOW)
        s.slope[:, tile] = cdf + up * density

    half_cols = at(h * (p.dl // 2), p.dl // 2)

    class Reduce:
        def __init__(self, left, right, grads, arrive, final, out):
            self.left, self.right, self.out = left, right, out
            self.grads, self.arrive, self.final = grads, arrive, final
            self.part = self.final.shape[0]
            self.rows = self.part * 4
            self.pairs = [cp.group() for _ in range(3)]

        def product(self):
            @pl.loop(0, self.grads.shape[0] // 256)
            def _(i):
                rows = at(i * 256, 256)
                self.grads[rows, :] = matmul_tn(self.left[:, rows], self.right[:, half_cols]).astype(LOW)

        def block(self, zz):
            return self.grads.at[at(zz * self.rows + q * self.part, self.part, 16), :]

        def scatter(self):
            for peer in zed:
                cp.send(self.pairs[0], self.block(peer), self.arrive.at[z], c, peer)
            cp.sent(self.pairs[0], self.arrive.at[0 : zs - 1])

        def add(self):
            cp.got(self.pairs[0], self.arrive.at[0 : zs - 1])
            self.arrive[z] = self.grads[at(z * self.rows + q * self.part, self.part, 16), :]
            total = self.arrive[0].astype(FULL)
            for zz in range(1, zs):
                total = total + self.arrive[zz].astype(FULL)
            self.final[...] = total.astype(LOW)
            here = self.out.at[at(q * self.part, self.part, 16), half_cols]
            for peer in chips:
                cp.send(self.pairs[1], self.final, here, peer, z)
            cp.sent(self.pairs[1], self.arrive.at[0:3])
            self.store = cp.local(self.final, here)

        def spread(self):
            cp.got(self.pairs[1], self.arrive.at[0:3])
            self.store.wait()
            block = self.out.at[:, half_cols]
            cp.send(self.pairs[2], block, block, core, z)
            cp.sent(self.pairs[2], block)

        def done(self):
            cp.got(self.pairs[2], self.out.at[:, half_cols])

    down = Reduce(s.act, s.cot, s.dwd, s.zd, s.fd, gd)
    upper = Reduce(s.mid, s.dup, s.dwu, s.zu, s.fu, gu)
    outer = Reduce(s.att, s.dhid, s.dwo, s.zo, s.fo, go)
    latents = Reduce(s.att, s.dhid, s.dlat, s.zl, s.fl, gl)

    act_share = share(s.act)
    wd.third()
    cp.got(act_share, s.act.at[0 : p.lat, :])
    down.product()
    down.scatter()
    wd.ready()

    @pl.loop(0, tiles)
    def _(i):
        tile = at(i * 256, 256)
        dact = matmul_nt(s.cot[own, :], s.wd[tile, :])
        s.dup[own, tile] = (dact * s.slope[:, tile]).astype(LOW)

    dup_share = share(s.dup)

    @pl.loop(0, tiles)
    def _(i):
        tile = at(i * 256, 256)
        s.dmid[:, tile] = matmul_nt(s.dup[own, :], s.wu[tile, :])

    s.vs[...] = jnp.zeros_like(s.vs)

    @pl.loop(0, p.lat // 64)
    def _(i):
        rows = at(i * 64, 64)
        full_rows = at(h * p.lat + i * 64, 64)
        normed, scale = ln_parts(s.hid[rows, :])
        grad = s.dmid[rows, :]
        s.vs[0:1, :] += columns_sum(grad * normed)
        s.vs[1:2, :] += columns_sum(grad)
        total = s.cot[full_rows, :].astype(FULL) + ln_grad(grad, gain_mlp, normed, scale)
        s.dhid[full_rows, :] = total.astype(LOW)

    dhid_share = share(s.dhid)

    @pl.loop(0, tiles)
    def _(i):
        tile = at(i * 256, 256)
        s.datt[own, tile] = matmul_nt(s.dhid[own, :], s.wo[tile, :]).astype(LOW)

    datt_share = share(s.datt)
    s.stat[...] = jnp.zeros_like(s.stat)

    @pl.loop(0, H)
    def _(head):
        cols, low_lane = window(head)
        product = s.datt[own, cols].astype(FULL) * s.att[own, cols].astype(FULL)
        delta = jnp.sum(product * mask_of(p.lat, low_lane), axis=-1, keepdims=True)
        s.stat[...] = jnp.where(lane_stat == head, delta, s.stat[...])

    s.stat_t[...] = s.stat[...].T
    s.stats[h, H : 2 * H, :] = s.stat_t[0:H, :]
    stats_pair = cp.group()
    cp.send(stats_pair, s.stats.at[h], s.stats.at[h], core, z)
    cp.sent(stats_pair, s.stats.at[0])

    cp.got(mid_share, s.mid.at[0 : p.lat, :])
    cp.got(dup_share, s.dup.at[0 : p.lat, :])
    upper.product()
    upper.scatter()
    down.add()
    cp.got(datt_share, s.datt.at[0 : p.lat, :])
    cp.got(stats_pair, s.stats.at[0])

    s.dq_t[...] = jnp.zeros_like(s.dq_t)
    sublane = lax.broadcasted_iota(jnp.int32, (p.slots, p.lat), 0)

    @pl.loop(0, p.seqs)
    def _(seq):
        slots = at(seq * p.slots, p.slots)
        latent_rows = at(seq * p.lat, p.lat)
        s.numer[...] = jnp.zeros_like(s.numer)
        s.dk_sum[...] = jnp.zeros_like(s.dk_sum)

        @pl.loop(0, H)
        def _(head):
            heads = at(head * p.lat, p.lat)
            cols, low_lane = window(head)
            raw = matmul_nt(s.keys[slots, :], s.qmask[heads, :])
            valid = start_slot + sublane < lengths[seq]
            top = s.max_all[pl.ds(seq * H + head, 1), :]
            inverse = s.stats[seq, pl.ds(head, 1), :]
            delta = s.stats[seq, pl.ds(H + head, 1), :]
            probs = jnp.exp(jnp.where(valid, raw * score_scale, -1e30) - top) * inverse
            grad = s.datt[latent_rows, cols] * mask_of(p.lat, low_lane).astype(LOW)
            dprobs = matmul_nt(s.values[slots, cols], grad)
            dscores = (probs * (dprobs - delta)).astype(LOW)
            s.numer[:, cols] += matmul(probs.astype(LOW), grad)
            s.dk_sum[...] += matmul(dscores, s.qmask[heads, :])
            block = at(head * p.head, p.head)
            s.dq_t[block, :] += matmul(s.keys_t[block, slots], dscores)

        s.dkeys[slots, :] = (s.dk_sum[...] * score_scale).astype(LOW)
        s.dvalues[slots, :] = s.numer[...].astype(LOW)

    s.dq[...] = (s.dq_t[...] * score_scale).T.astype(LOW)
    qhalf = p.qk // 2
    dq_pairs = [cp.group() for _ in range(4)]
    cp.send(dq_pairs[0], s.dq.at[:, at(other * qhalf, qhalf)], s.dq_in1, core, z)
    cp.sent(dq_pairs[0], s.dq_in1)

    def weight_grads(side):
        kcols = at(side * qhalf, qhalf)
        vcols = at(side * (p.vd // 2), p.vd // 2)

        @pl.loop(0, p.din // 256)
        def _(i):
            rows = at(i * 256, 256)
            s.swk[side, rows, :] = matmul(s.nin_t[rows, :], s.dkeys[:, kcols]).astype(LOW)
            s.swv[side, rows, :] = matmul(s.nin_t[rows, :], s.dvalues[:, vcols]).astype(LOW)

    weight_grads(other)
    zrows = p.din // zs
    vpart = zrows // 4

    class Local:
        def __init__(self, grads, arrive, chip, plane_in, plane, z_in, final, out):
            self.grads, self.arrive, self.chip, self.plane_in = grads, arrive, chip, plane_in
            self.plane, self.z_in, self.final, self.out = plane, z_in, final, out
            self.width = final.shape[1]
            self.pairs = [cp.group() for _ in range(4)]
            self.chunks = [cp.group() for _ in range(zs)]

        def pair(self):
            cp.send(self.pairs[0], self.grads.at[other], self.arrive, core, z)
            cp.sent(self.pairs[0], self.arrive)

        def chunk(self, i, zz):
            rows = at(zz * zrows, zrows)
            total = self.grads[h, rows, :].astype(FULL) + self.arrive[rows, :].astype(FULL)
            self.chip[zz] = total.astype(LOW)
            for peer in chips:
                rows = at(lax.div(peer, 2) * vpart, vpart)
                cp.send(self.chunks[i], self.chip.at[zz, rows, :], self.plane_in.at[q, zz], peer, z)
            cp.sent(self.chunks[i], self.plane_in.at[0, 0:3])

        def add(self, i, zz):
            cp.got(self.chunks[i], self.plane_in.at[0, 0:3])
            self.plane_in[q, zz] = self.chip[zz, at(q * vpart, vpart, 16), :]
            parts = [self.plane_in[qq, zz].astype(FULL) for qq in range(4)]
            self.plane[zz] = ((parts[0] + parts[1]) + (parts[2] + parts[3])).astype(LOW)
            if i < zs - 1:
                cp.send(self.pairs[1], self.plane.at[zz], self.z_in.at[z], c, zz)
            else:
                cp.sent(self.pairs[1], self.z_in.at[0 : zs - 1])

        def finish(self):
            cp.got(self.pairs[1], self.z_in.at[0 : zs - 1])
            self.z_in[z] = self.plane[z]
            total = self.z_in[0].astype(FULL)
            for zz in range(1, zs):
                total = total + self.z_in[zz].astype(FULL)
            self.final[...] = total.astype(LOW)
            here = self.out.at[at(q * vpart, vpart, 16), at(h * self.width, self.width)]
            for peer in chips:
                cp.send(self.pairs[2], self.final, here, peer, z)
            cp.sent(self.pairs[2], self.z_in.at[0:3])
            self.store = cp.local(self.final, here)

        def spread(self):
            cp.got(self.pairs[2], self.z_in.at[0:3])
            self.store.wait()
            block = self.out.at[:, at(h * self.width, self.width)]
            cp.send(self.pairs[3], block, block, core, z)
            cp.sent(self.pairs[3], block)

        def done(self):
            cp.got(self.pairs[3], self.out.at[:, at(h * self.width, self.width)])

    key_grads = Local(s.swk, s.rwk, s.cwk, s.pwk_in, s.pwk, s.zwk_in, s.fwk, gk)
    value_grads = Local(s.swv, s.rwv, s.cwv, s.pwv_in, s.pwv, s.zwv_in, s.fwv, gv)
    kv = (value_grads, key_grads)
    for grads in kv:
        grads.pair()
    weight_grads(h)
    cp.got(dq_pairs[0], s.dq_in1)
    s.dq_chip[...] = (
        s.dq[:, at(h * qhalf, qhalf)].astype(FULL) + s.dq_in1[...].astype(FULL)
    ).astype(LOW)
    for peer in chips:
        cp.send(dq_pairs[1], s.dq_chip, s.dq_in2.at[q], peer, z)
    cp.sent(dq_pairs[1], s.dq_in2.at[0:3])
    for grads in kv:
        cp.got(grads.pairs[0], grads.arrive)
    order = [*zed, z]
    for i, zz in enumerate(order):
        for grads in kv:
            grads.chunk(i, zz)

    cp.got(att_share, s.att.at[0 : p.lat, :])
    cp.got(dhid_share, s.dhid.at[0 : p.lat, :])
    outer.product()
    outer.scatter()
    s.dlat[...] = (
        s.dhid[0 : p.lat, half_cols].astype(FULL) + s.dhid[p.lat : 2 * p.lat, half_cols].astype(FULL)
    ).astype(LOW)
    latents.scatter()
    down.spread()

    def byte_part(part):
        @pl.loop(part * 2, part * 2 + 2)
        def _(i):
            rows = at(i * 64, 64)
            grad = matmul_nt(s.dkeys[rows, :], s.wk[...]) + matmul_nt(s.dvalues[rows, :], s.wv[...])
            normed, scale = ln_parts(s.feats[rows, :].astype(FULL))
            s.vs[2:3, 0 : p.din] += columns_sum(grad * normed)
            s.vs[3:4, 0 : p.din] += columns_sum(grad)
            s.bgrad[rows, :] = ln_grad(grad, vec[2:3, 0 : p.din], normed, scale).astype(LOW)

    for i, zz in enumerate(order):
        for grads in kv:
            grads.add(i, zz)
        byte_part(i)

    stores = [cp.local(s.bgrad, byte_out)]
    vs_pairs = [cp.group() for _ in range(3)]
    cp.send(vs_pairs[0], s.vs, s.vs_in1, core, z)
    cp.sent(vs_pairs[0], s.vs)
    cp.got(dq_pairs[1], s.dq_in2.at[0:3])
    s.dq_in2[q] = s.dq_chip[...]
    parts = s.dq_in2
    s.dq_plane[...] = (
        (parts[0].astype(FULL) + parts[1].astype(FULL)) + (parts[2].astype(FULL) + parts[3].astype(FULL))
    ).astype(LOW)
    for peer in zed:
        cp.send(dq_pairs[2], s.dq_plane, s.dq_in3.at[z], c, peer)
    cp.sent(dq_pairs[2], s.dq_in3.at[0 : zs - 1])
    cp.got(vs_pairs[0], s.vs_in1)
    s.vs_chip[...] = s.vs[...] + s.vs_in1[...]
    for peer in chips:
        cp.send(vs_pairs[1], s.vs_chip, s.vs_in2.at[q], peer, z)
    cp.sent(vs_pairs[1], s.vs_in2.at[0:3])
    upper.add()

    @pl.loop(0, tiles)
    def _(i):
        tile = at(i * 256, 256)
        s.res[:, tile] = (s.hid[:, tile] + matmul(s.act[own, :], s.wd[:, tile])).astype(LOW)

    res_pair = cp.group()
    cp.send(res_pair, s.res, res_out.at[own, :], core, z)
    cp.sent(res_pair, s.res)
    stores.append(cp.local(s.res, res_out.at[own, :]))

    for grads in kv:
        grads.finish()
    cp.got(vs_pairs[1], s.vs_in2.at[0:3])
    s.vs_in2[q] = s.vs_chip[...]
    parts = s.vs_in2
    total = (parts[0] + parts[1]) + (parts[2] + parts[3])
    row_ids = lax.broadcasted_iota(jnp.int32, (8, p.dl), 0)
    s.vs_plane[...] = jnp.where(row_ids < 2, s.vs_chip[...], total)
    for peer in zed:
        cp.send(vs_pairs[2], s.vs_plane, s.vs_in3.at[z], c, peer)
    cp.sent(vs_pairs[2], s.vs_in3.at[0 : zs - 1])
    cp.got(dq_pairs[2], s.dq_in3.at[0 : zs - 1])
    s.dq_in3[z] = s.dq_plane[...]
    parts = s.dq_in3
    total = parts[0].astype(FULL)
    for zz in range(1, zs):
        total = total + parts[zz].astype(FULL)
    own_half = at(h * qhalf, qhalf)
    s.dq_all[:, own_half] = total.astype(LOW)
    cp.send(dq_pairs[3], s.dq_all.at[:, own_half], s.dq_all.at[:, own_half], core, z)
    cp.sent(dq_pairs[3], s.dq_in1)
    outer.add()
    latents.add()
    upper.spread()
    reduces = (down, upper, outer, latents)
    for grads in kv:
        grads.spread()
    cp.got(dq_pairs[3], s.dq_in1)

    @pl.loop(0, tiles)
    def _(i):
        tile = at(i * 256, 256)
        s.gq[tile, :] = matmul_tn(s.nlat[:, tile], s.dq_all[...])
        s.dmid[:, tile] = matmul_nt(s.dq_all[...], s.wq[tile, :])

    stores.append(cp.local(s.gq.at[at(z * (p.dl // zs), p.dl // zs, 16), :], gq_out))
    cp.got(vs_pairs[2], s.vs_in3.at[0 : zs - 1])
    s.vs_in3[z] = s.vs_plane[...]
    total = s.vs_in3[0]
    for zz in range(1, zs):
        total = total + s.vs_in3[zz]
    s.vs_all[...] = total
    s.vs_all[4:6, :] = jnp.zeros((2, p.dl), FULL)

    @pl.loop(0, p.lat // 64)
    def _(i):
        rows = at(i * 64, 64)
        normed, scale = ln_parts(s.lat[rows, :].astype(FULL))
        grad = s.dmid[rows, :]
        s.vs_all[4:5, :] += columns_sum(grad * normed)
        s.vs_all[5:6, :] += columns_sum(grad)
        s.slope[rows, :] = ln_grad(grad, gain_lat, normed, scale)

    stores.append(cp.local(s.slope.at[at(z * (p.lat // zs), p.lat // zs, 16), :], glat_out))
    stores.append(cp.local(s.vs_all, vec_out))
    outer.spread()
    latents.spread()
    for reduce in (*reduces, *kv):
        reduce.done()
    cp.got(res_pair, s.res)
    for store in stores:
        store.wait()
    cp.drain()


def finish_kernel(p, res, byte, go, gu, gd, gv, gk, gl, gq, glat, vec, *outs):
    z = lax.axis_index("wshard")
    outs[0][...] = res[...]
    outs[1][...] = byte[...]
    outs[2][...] = glat[...] + gl[...].astype(FULL)
    for out, row in ((3, 4), (4, 5), (5, 2), (6, 3), (11, 0), (12, 1)):
        size = outs[out].shape[0]
        picked = vec[row : row + 1, 0:size]
        for zz in range(1, p.zs):
            picked = jnp.where(z == zz, vec[row : row + 1, zz * size : (zz + 1) * size], picked)
        outs[out][...] = picked.reshape(size)
    outs[7][...] = gq[...]
    for out, source in ((8, gk), (9, gv), (10, go), (13, gu), (14, gd)):
        outs[out][...] = source[...].astype(FULL)


def fused(*args):
    (byte_feats, lengths, latent, *smalls, cot) = (args[0], args[1], args[2], *args[3:7], args[11], args[12], args[15])
    w_query, w_key, w_value, w_output = args[7:11]
    w_up, w_down = args[13:15]
    seqs, slots, din = byte_feats.shape
    ctx, zs = lax.axis_size("ctx"), lax.axis_size("wshard")
    feats = byte_feats.reshape(seqs * slots, din)
    cot_flat = cot.reshape(-1, cot.shape[-1])
    p = Plan(ctx, zs, feats, latent, w_query, w_key, w_value, w_output, cot_flat)
    table = scratch_table(p)
    anywhere = pl.BlockSpec(memory_space=pl.ANY)
    in_vmem = pl.BlockSpec(memory_space=pltpu.VMEM)
    struct = jax.ShapeDtypeStruct
    made = pl.pallas_call(
        functools.partial(fused_kernel, p, tuple(table)),
        out_shape=(
            struct(cot_flat.shape, LOW),
            struct(feats.shape, LOW),
            struct(w_output.shape, LOW),
            struct(w_up.shape, LOW),
            struct(w_down.shape, LOW),
            struct(w_value.shape, LOW),
            struct(w_key.shape, LOW),
            struct(latent.shape, LOW),
            struct(w_query.shape, FULL),
            struct(latent.shape, FULL),
            struct((8, p.dl), FULL),
        ),
        in_specs=[pl.BlockSpec(memory_space=pltpu.SMEM)] + [anywhere] * 8 + [in_vmem] * 6 + [anywhere],
        out_specs=(anywhere,) * 11,
        scratch_shapes=[pltpu.VMEM(shape, kind) for shape, kind in table.values()]
        + [pltpu.SemaphoreType.DMA((SEMS,))],
        compiler_params=pltpu.CompilerParams(
            collective_id=0, has_side_effects=True, vmem_limit_bytes=67043328
        ),
        name="block",
    )(lengths, feats, latent, w_query, w_key, w_value, w_output, w_up, w_down, *smalls, cot_flat)
    shapes = (
        (cot_flat.shape, LOW),
        (feats.shape, LOW),
        (latent.shape, FULL),
        *((smalls[i].shape, FULL) for i in range(4)),
        *((w.shape, FULL) for w in (w_query, w_key, w_value, w_output)),
        *((smalls[i].shape, FULL) for i in (4, 5)),
        *((w.shape, FULL) for w in (w_up, w_down)),
    )
    outs = pl.pallas_call(
        functools.partial(finish_kernel, p),
        out_shape=tuple(struct(shape, kind) for shape, kind in shapes),
        in_specs=[in_vmem] * 11,
        out_specs=(in_vmem,) * 15,
        compiler_params=pltpu.CompilerParams(vmem_limit_bytes=60 * 2**20),
        name="finish",
    )(*made)
    return (outs[0].reshape(cot.shape), outs[1].reshape(byte_feats.shape), *outs[2:])


def shards(*args):
    if lax.axis_size("ctx") == 8 and lax.axis_size("wshard") == 4 and args[0].shape[0] == 2:
        return fused(*args)
    return plain(*args)


def solution(mesh):
    sharded, plain = P("wshard", None), P("wshard")
    return jax.shard_map(
        shards,
        mesh=mesh,
        in_specs=(
            P("wshard", "ctx", None),
            plain,
            sharded,
            plain,
            plain,
            plain,
            plain,
            sharded,
            sharded,
            sharded,
            sharded,
            plain,
            plain,
            sharded,
            sharded,
            P("wshard", None, None),
        ),
        out_specs=(
            P("wshard", None, None),
            P("wshard", "ctx", None),
            sharded,
            plain,
            plain,
            plain,
            plain,
            sharded,
            sharded,
            sharded,
            sharded,
            plain,
            plain,
            sharded,
            sharded,
        ),
        check_vma=False,
    )
```

```python
import functools
import math
import types

import jax
import jax.numpy as jnp
from jax import lax
from jax.experimental import pallas as pl
from jax.experimental.pallas import tpu as pltpu
from jax.sharding import PartitionSpec as P

H = 8
LOW = jnp.bfloat16
FULL = jnp.float32


def layer_norm(values, gain, offset):
    center = jnp.mean(values, axis=-1, keepdims=True)
    centred = values - center
    variance = jnp.mean(centred * centred, axis=-1, keepdims=True)
    return centred * lax.rsqrt(variance + 1e-05) * gain + offset


def exact_gelu(values):
    return jax.nn.gelu(values, approximate=False)


def matmul(left, right):
    return jnp.dot(left, right, preferred_element_type=FULL)


def matmul_tn(left, right):
    return lax.dot_general(left, right, (((0,), (0,)), ((), ())), preferred_element_type=FULL)


def matmul_nt(left, right):
    return lax.dot_general(left, right, (((1,), (1,)), ((), ())), preferred_element_type=FULL)


def gather(shard):
    return lax.all_gather(shard, "wshard", axis=0, tiled=True)


def scatter(total):
    return lax.psum_scatter(
        total.astype(LOW), "wshard", scatter_dimension=0, tiled=True
    ).astype(FULL)


SEMS = 256


def own_part(total, shard):
    size = shard.shape[0]
    return lax.dynamic_slice_in_dim(total, lax.axis_index("wshard") * size, size, 0)


def plain(
    byte_feats,
    lengths,
    latent_array,
    lat_gain,
    lat_bias,
    in_gain,
    in_bias,
    w_query,
    w_key,
    w_value,
    w_output,
    mlp_gain,
    mlp_bias,
    w_up,
    w_down,
    cotangent,
):
    seqs, slots, width = byte_feats.shape
    gain_in, bias_in = gather(in_gain).astype(FULL), gather(in_bias).astype(FULL)
    key_w, value_w = gather(w_key), gather(w_value)
    latent = gather(latent_array).astype(FULL)
    gain_lat, bias_lat = gather(lat_gain).astype(FULL), gather(lat_bias).astype(FULL)
    query_w = gather(w_query)
    gain_mlp, bias_mlp = gather(mlp_gain).astype(FULL), gather(mlp_bias).astype(FULL)
    output_w, up_w, down_w = gather(w_output), gather(w_up), gather(w_down)

    features = byte_feats.reshape(seqs * slots, width).astype(FULL)
    normed_in, in_back = jax.vjp(layer_norm, features, gain_in, bias_in)
    input_low = normed_in.astype(LOW)
    keys = matmul(input_low, key_w).astype(LOW)
    values = matmul(input_low, value_w).astype(LOW)
    normed_lat, lat_back = jax.vjp(layer_norm, latent, gain_lat, bias_lat)
    lat_low = normed_lat.astype(LOW)
    rows = lat_low.shape[0]
    queries = matmul(lat_low, query_w).astype(LOW)
    score_scale = 1.0 / math.sqrt(queries.shape[1] // H)
    qheads = queries.reshape(rows, H, -1)
    kheads = keys.reshape(seqs, slots, H, -1)
    vheads = values.reshape(seqs, slots, H, -1)

    scores = jnp.einsum("lhd,mkhd->mhlk", qheads, kheads, preferred_element_type=FULL) * score_scale
    slot_ids = lax.axis_index("ctx") * slots + lax.iota(jnp.int32, slots)
    valid = (slot_ids[None, :] < lengths[:, None])[:, None, None, :]
    scores = jnp.where(valid, scores, -1e30)
    highest = lax.pmax(jnp.max(scores, axis=-1), "ctx")
    weights = jnp.where(valid, jnp.exp(scores - highest[..., None]), 0.0)
    total = lax.psum(jnp.sum(weights, axis=-1), "ctx")
    numer = jnp.einsum("mhlk,mkhe->mlhe", weights.astype(LOW), vheads, preferred_element_type=FULL)
    numer = lax.psum(numer.astype(LOW), "ctx").astype(FULL)
    attended = numer / jnp.transpose(total, (0, 2, 1))[..., None]
    attended = attended.reshape(seqs * rows, -1)

    att_low = attended.astype(LOW)
    hidden = jnp.tile(latent, (seqs, 1)) + matmul(att_low, output_w)
    normed_mid, mid_back = jax.vjp(layer_norm, hidden, gain_mlp, bias_mlp)
    mid_low = normed_mid.astype(LOW)
    upward = matmul(mid_low, up_w)
    activated, gelu_back = jax.vjp(exact_gelu, upward)
    act_low = activated.astype(LOW)
    result = hidden + matmul(act_low, down_w)
    dout_low = cotangent.reshape(seqs * rows, -1)
    grad_down = scatter(matmul_tn(act_low, dout_low))
    (grad_upward,) = gelu_back(matmul_nt(dout_low, down_w))
    up_low = grad_upward.astype(LOW)
    grad_up = scatter(matmul_tn(mid_low, up_low))
    dhid_norm, grad_gmlp, grad_bmlp = mid_back(matmul_nt(up_low, up_w))
    dhidden = dout_low.astype(FULL) + dhid_norm
    dhid_low = dhidden.astype(LOW)
    grad_output = scatter(matmul_tn(att_low, dhid_low))
    grad_hidden = scatter(jnp.sum(dhidden.reshape(seqs, rows, -1), axis=0))
    grad_att = matmul_nt(dhid_low, output_w).astype(LOW)

    grad_heads = grad_att.reshape(seqs, rows, H, -1)
    delta = jnp.sum(
        grad_heads.astype(FULL) * attended.reshape(seqs, rows, H, -1), axis=-1
    ).transpose(0, 2, 1)
    probs = weights / total[..., None]
    dprobs = jnp.einsum("mlhe,mkhe->mhlk", grad_heads, vheads, preferred_element_type=FULL)
    dscores = (probs * (dprobs - delta[..., None])).astype(LOW)
    dquery = jnp.einsum("mhlk,mkhd->lhd", dscores, kheads, preferred_element_type=FULL) * score_scale
    dkeys = jnp.einsum("mhlk,lhd->mkhd", dscores, qheads, preferred_element_type=FULL) * score_scale
    dvalues = jnp.einsum("mhlk,mlhe->mkhe", probs.astype(LOW), grad_heads, preferred_element_type=FULL)
    dkeys = dkeys.astype(LOW).reshape(seqs * slots, -1)
    dvalues = dvalues.astype(LOW).reshape(seqs * slots, -1)

    dquery = lax.psum(dquery.reshape(rows, -1).astype(LOW), ("ctx", "wshard"))
    grad_query = matmul_tn(
        lax.dynamic_slice_in_dim(
            lat_low, lax.axis_index("wshard") * w_query.shape[0], w_query.shape[0], 1
        ),
        dquery,
    )
    dlat_norm, grad_glat, grad_blat = lat_back(matmul_nt(dquery, query_w))
    grad_latent = grad_hidden + own_part(dlat_norm, latent_array)

    dnorm_in = matmul_nt(dkeys, key_w) + matmul_nt(dvalues, value_w)
    dfeatures, grad_gin, grad_bin = in_back(dnorm_in)
    grad_key = lax.psum(scatter(matmul_tn(input_low, dkeys)).astype(LOW), "ctx").astype(FULL)
    grad_value = lax.psum(scatter(matmul_tn(input_low, dvalues)).astype(LOW), "ctx").astype(FULL)
    in_sums = lax.psum(jnp.concatenate([grad_gin, grad_bin]), ("ctx", "wshard"))
    grad_gin, grad_bin = jnp.split(in_sums, 2)
    mlp_sums = lax.psum(jnp.concatenate([grad_gmlp, grad_bmlp]), "wshard")
    grad_gmlp, grad_bmlp = jnp.split(mlp_sums, 2)
    return (
        result.astype(LOW).reshape(seqs, rows, -1),
        dfeatures.astype(LOW).reshape(seqs, slots, width),
        grad_latent,
        own_part(grad_glat, lat_gain),
        own_part(grad_blat, lat_bias),
        own_part(grad_gin, in_gain),
        own_part(grad_bin, in_bias),
        grad_query,
        grad_key,
        grad_value,
        grad_output,
        own_part(grad_gmlp, mlp_gain),
        own_part(grad_bmlp, mlp_bias),
        grad_up,
        grad_down,
    )


def ln_parts(values):
    centred = values - jnp.mean(values, axis=-1, keepdims=True)
    scale = lax.rsqrt(jnp.mean(centred * centred, axis=-1, keepdims=True) + 1e-05)
    return centred * scale, scale


def ln_grad(cotangent, gain, normed, scale):
    scaled = cotangent * gain
    first = jnp.mean(scaled, axis=-1, keepdims=True)
    second = jnp.mean(scaled * normed, axis=-1, keepdims=True)
    return scale * (scaled - first - normed * second)


def lanes(rows, columns):
    return lax.broadcasted_iota(jnp.int32, (rows, columns), 1)


def columns_sum(values):
    return jnp.sum(values, axis=0, keepdims=True)


class Plan:
    def __init__(self, ctx, zs, feats, latent, w_query, w_key, w_value, w_output, cot):
        self.ctx, self.zs = ctx, zs
        self.rows_in, self.din = feats.shape
        self.lat = latent.shape[0] * zs
        self.dl = latent.shape[1]
        self.qk, self.vd = w_key.shape[1], w_value.shape[1]
        self.seqs = cot.shape[0] // self.lat
        self.slots = self.rows_in // self.seqs
        self.head, self.vhead = self.qk // H, self.vd // H


def scratch_table(p):
    both = p.seqs * p.lat
    half = p.dl // 2
    part = p.dl // p.zs // 4
    vpart = p.din // p.zs // 4
    return dict(
        wk=((p.din, p.qk), LOW),
        wq=((p.dl, p.qk), LOW),
        lat=((p.lat, p.dl), LOW),
        wv=((p.din, p.vd), LOW),
        wo=((p.vd, p.dl), LOW),
        wu=((p.dl, p.dl), LOW),
        wd=((p.dl, p.dl), LOW),
        small_own=((8, 384), FULL),
        small=((p.zs, 8, 384), FULL),
        vec=((8, p.dl), FULL),
        feats=((p.rows_in, p.din), LOW),
        nin=((p.rows_in, p.din), LOW),
        nin_t=((p.din, p.rows_in), LOW),
        keys=((p.rows_in, p.qk), LOW),
        keys_t=((p.qk, p.rows_in), LOW),
        values=((p.rows_in, p.vd), LOW),
        nlat=((p.lat, p.dl), LOW),
        qmask=((H * p.lat, p.qk), LOW),
        scores=((p.seqs * H * max(p.lat, p.slots), max(p.lat, p.slots)), FULL),
        stat=((p.lat, 128), FULL),
        stat_t=((128, p.lat), FULL),
        max_t=((p.lat, 128), FULL),
        max_own=((2 * H, p.lat), FULL),
        max_in=((p.ctx, 2 * H, p.lat), FULL),
        max_all=((2 * H, p.lat), FULL),
        numer=((p.lat, p.vd), FULL),
        numer_low=((p.lat, p.vd), LOW),
        numer_in=((p.lat, p.vd), LOW),
        sums=((2, H, p.lat), FULL),
        sums_in=((H, p.lat), FULL),
        chip=((p.lat, p.vd), LOW),
        chip_in=((4, p.lat // 4, p.vd), LOW),
        chip_sums=((H, p.lat), FULL),
        chip_sums_in=((4, H, p.lat), FULL),
        scale=((p.lat // 4, p.vd), FULL),
        att=((both, p.vd), LOW),
        mid=((both, p.dl), LOW),
        act=((both, p.dl), LOW),
        dup=((both, p.dl), LOW),
        dhid=((both, p.dl), LOW),
        datt=((both, p.vd), LOW),
        cot=((both, p.dl), LOW),
        hid=((p.lat, p.dl), FULL),
        slope=((p.lat, p.dl), FULL),
        dmid=((p.lat, p.dl), FULL),
        res=((p.lat, p.dl), LOW),
        stats=((2, 2 * H, p.lat), FULL),
        dwo=((p.vd, half), LOW),
        dwu=((p.dl, half), LOW),
        dwd=((p.dl, half), LOW),
        dlat=((p.lat, half), LOW),
        zo=((p.zs, part, half), LOW),
        zu=((p.zs, part, half), LOW),
        zd=((p.zs, part, half), LOW),
        zl=((p.zs, p.lat // p.zs // 4, half), LOW),
        fo=((part, half), LOW),
        fu=((part, half), LOW),
        fd=((part, half), LOW),
        fl=((p.lat // p.zs // 4, half), LOW),
        dkeys=((p.rows_in, p.qk), LOW),
        dvalues=((p.rows_in, p.vd), LOW),
        dk_sum=((p.slots, p.qk), FULL),
        dq_t=((p.qk, p.lat), FULL),
        dq=((p.lat, p.qk), LOW),
        dq_in1=((p.lat, p.qk // 2), LOW),
        dq_chip=((p.lat, p.qk // 2), LOW),
        dq_in2=((4, p.lat, p.qk // 2), LOW),
        dq_plane=((p.lat, p.qk // 2), LOW),
        dq_in3=((p.zs, p.lat, p.qk // 2), LOW),
        dq_all=((p.lat, p.qk), LOW),
        bgrad=((p.rows_in, p.din), LOW),
        swk=((2, p.din, p.qk // 2), LOW),
        swv=((2, p.din, p.vd // 2), LOW),
        rwk=((p.din, p.qk // 2), LOW),
        rwv=((p.din, p.vd // 2), LOW),
        cwk=((p.zs, p.din // p.zs, p.qk // 2), LOW),
        cwv=((p.zs, p.din // p.zs, p.vd // 2), LOW),
        pwk_in=((4, p.zs, vpart, p.qk // 2), LOW),
        pwv_in=((4, p.zs, vpart, p.vd // 2), LOW),
        pwk=((p.zs, vpart, p.qk // 2), LOW),
        pwv=((p.zs, vpart, p.vd // 2), LOW),
        zwk_in=((p.zs, vpart, p.qk // 2), LOW),
        zwv_in=((p.zs, vpart, p.vd // 2), LOW),
        fwk=((vpart, p.qk // 2), LOW),
        fwv=((vpart, p.vd // 2), LOW),
        vs=((8, p.dl), FULL),
        vs_in1=((8, p.dl), FULL),
        vs_chip=((8, p.dl), FULL),
        vs_in2=((4, 8, p.dl), FULL),
        vs_plane=((8, p.dl), FULL),
        vs_in3=((p.zs, 8, p.dl), FULL),
        vs_all=((8, p.dl), FULL),
        gq=((p.dl, p.qk), FULL),
    )


class Copies:
    def __init__(self, sems):
        self.sems, self.used, self.open = sems, 0, []

    def new(self):
        self.used += 1
        return self.sems.at[self.used - 1]

    def group(self):
        return (self.new(), self.new())

    def send(self, pair, src, dst, ctx, z):
        pltpu.make_async_remote_copy(
            src_ref=src,
            dst_ref=dst,
            send_sem=pair[0],
            recv_sem=pair[1],
            device_id=(ctx, z),
            device_id_type=pl.DeviceIdType.MESH,
        ).start()

    def local(self, src, dst):
        copy = pltpu.make_async_copy(src, dst, self.new())
        copy.start()
        return copy

    def got(self, pair, view):
        pltpu.make_async_copy(view, view, pair[1]).wait()

    def sent(self, pair, view, when=None):
        self.open.append((pair[0], view, when))

    def drain(self):
        for sem, view, when in self.open:
            wait = pltpu.make_async_copy(view, view, sem).wait
            if when is None:
                wait()
            else:
                pl.when(when)(wait)


def at(start, size, step=None):
    return pl.ds(pl.multiple_of(start, step or size), size)


def fused_kernel(p, names, *refs):
    ins, refs = refs[:16], refs[16:]
    lengths, feats_in, lat_in, wq_in, wk_in, wv_in, wo_in, wu_in, wd_in = ins[:9]
    smalls, cot_in = ins[9:15], ins[15]
    outs, refs = refs[:11], refs[11:]
    res_out, byte_out, go, gu, gd, gv, gk, gl, gq_out, glat_out, vec_out = outs
    sems = refs[-1]
    s = types.SimpleNamespace(**dict(zip(names, refs[:-1])))
    cp = Copies(sems)
    ctx, zs = p.ctx, p.zs
    c, z = lax.axis_index("ctx"), lax.axis_index("wshard")
    h, q = lax.rem(c, 2), lax.div(c, 2)
    x, y = lax.rem(q, 2), lax.div(q, 2)
    other = 1 - h
    core = c + 1 - 2 * h
    chips = (c + 2 - 4 * x, c + 4 - 8 * y, c + 6 - 4 * x - 8 * y)
    near = (chips[0] * (1 - h) + chips[1] * h, chips[1] * (1 - h) + chips[0] * h)
    zed = [lax.rem(z + j, zs) for j in range(1, zs)]
    plane = [lax.rem(c + j, ctx) for j in range(1, ctx)]

    barrier = pltpu.get_barrier_semaphore()
    for peer in plane:
        pl.semaphore_signal(barrier, inc=1, device_id=(peer, z), device_id_type=pl.DeviceIdType.MESH)
    for peer in zed:
        pl.semaphore_signal(barrier, inc=1, device_id=(c, peer), device_id_type=pl.DeviceIdType.MESH)
    pl.semaphore_wait(barrier, ctx - 1 + zs - 1)

    load_feats = cp.local(feats_in, s.feats)
    for row, ref in enumerate(smalls):
        s.small_own[row : row + 1, 0 : ref.shape[0]] = ref[...].reshape(1, -1).astype(FULL)
    small_pair = cp.group()
    for peer in zed:
        cp.send(small_pair, s.small_own, s.small.at[z], c, peer)
    cp.sent(small_pair, s.small.at[0 : zs - 1])

    class Weight:
        def __init__(self, ref, source, cuts, line):
            self.ref, self.source, self.cuts, self.line = ref, source, cuts, line
            if line:
                self.up = [cp.group() for _ in range(zs - 1)]
                self.down = [cp.group() for _ in range(zs - 1)]
            self.rows, cols = source.shape
            self.part, self.cols = self.rows // cuts, cols // 2
            self.slot = q if cuts == 4 else lax.rem(x + y, 2)
            self.mine = at(h * self.cols, self.cols)
            self.pairs = [cp.group() for _ in range(4)]

        def view(self, rows):
            return self.ref.at[pl.ds(0, rows), pl.ds(0, self.cols)]

        def block(self, zz, qq):
            return self.ref.at[at(zz * self.rows + qq * self.part, self.part, 16), self.mine]

        def hop(self, i):
            one = self.view(self.part)

            def forward(pair, source, dest, when):
                @pl.when(when)
                def _():
                    cp.send(pair, source, self.block(dest[0], self.slot), c, dest[1])

                cp.sent(pair, one, when)

            if i == 0:
                mine = self.source.at[at(self.slot * self.part, self.part, 16), self.mine]
                forward(self.up[0], mine, (z, z + 1), z < zs - 1)
                forward(self.down[0], mine, (z, z - 1), z > 0)
                self.load = cp.local(self.source, self.ref.at[at(z * self.rows, self.rows, 16), :])
                return

            @pl.when(z >= i)
            def _():
                cp.got(self.up[i - 1], one)

            if i < zs - 1:
                block = self.block(lax.rem(z + zs - i, zs), self.slot)
                forward(self.up[i], block, (lax.rem(z + zs - i, zs), z + 1), (z >= i) & (z < zs - 1))

            @pl.when(z + i < zs)
            def _():
                cp.got(self.down[i - 1], one)

            if i < zs - 1:
                block = self.block(lax.rem(z + i, zs), self.slot)
                forward(self.down[i], block, (lax.rem(z + i, zs), z - 1), (z + i < zs) & (z > 0))

        def start(self):
            for peer in zed:
                cp.send(
                    self.pairs[0],
                    self.source.at[at(self.slot * self.part, self.part, 16), self.mine],
                    self.block(z, self.slot),
                    c,
                    peer,
                )
            cp.sent(self.pairs[0], self.view(3 * self.part))
            self.load = cp.local(self.source, self.ref.at[at(z * self.rows, self.rows, 16), :])

        def first(self):
            if self.line:
                self.hop(zs - 1)
            else:
                cp.got(self.pairs[0], self.view(3 * self.part))
            for zz in zed:
                block = self.block(zz, self.slot)
                cp.send(self.pairs[1], block, block, near[0], z)
            cp.sent(self.pairs[1], self.view(3 * self.part))

        def second(self):
            cp.got(self.pairs[1], self.view(3 * self.part))
            for zz in zed:
                for qq in (q, lax.div(near[0], 2)):
                    block = self.block(zz, qq)
                    cp.send(self.pairs[2], block, block, near[1], z)
            cp.sent(self.pairs[2], self.view(6 * self.part))

        def third(self):
            if self.cuts == 4:
                cp.got(self.pairs[2], self.view(6 * self.part))
            else:
                cp.got(self.pairs[1], self.view(3 * self.part))
            for zz in zed:
                block = self.ref.at[at(zz * self.rows, self.rows, 16), self.mine]
                cp.send(self.pairs[3], block, block, core, z)
            cp.sent(self.pairs[3], self.view(3 * self.rows))

        def ready(self):
            cp.got(self.pairs[3], self.view(3 * self.rows))
            self.load.wait()

    wk, wq, lat = Weight(s.wk, wk_in, 4, False), Weight(s.wq, wq_in, 4, False), Weight(s.lat, lat_in, 4, False)
    wv, wo = Weight(s.wv, wv_in, 4, False), Weight(s.wo, wo_in, 4, True)
    wu, wd = Weight(s.wu, wu_in, 4, True), Weight(s.wd, wd_in, 2, True)
    for weight in (wk, wq, lat, wv):
        weight.start()
    wo.hop(0)
    load_cot = cp.local(cot_in, s.cot)

    cp.got(small_pair, s.small.at[0 : zs - 1])
    s.small[z] = s.small_own[...]
    for row, ref in enumerate(smalls):
        size = ref.shape[0]
        for zz in range(zs):
            s.vec[row : row + 1, zz * size : (zz + 1) * size] = s.small[zz, row : row + 1, 0:size]
    vec = s.vec
    gain_lat, bias_lat = vec[0:1, :], vec[1:2, :]

    half_cols = at(h * (p.dl // 2), p.dl // 2)
    own = at(h * p.lat, p.lat)
    tiles = p.dl // 256
    quarter = p.lat // 4
    own_rows = at(h * p.lat + q * quarter, quarter)
    score_scale = 1.0 / math.sqrt(p.head)
    start_slot = c * p.slots
    lane_stat = lanes(p.lat, 128)
    gain_mlp, bias_mlp = vec[4:5, :], vec[5:6, :]
    qhalf, vhalf = p.qk // 2, p.vd // 2
    zrows = p.din // zs
    vpart = zrows // 4
    order = [*zed, z]

    def window(head):
        low_lane = pl.multiple_of(lax.div(head * p.vhead, 128) * 128, 128)
        return pl.ds(low_lane, 256), head * p.vhead - low_lane

    def mask_of(rows, low_lane):
        lane = lanes(rows, 256)
        return ((lane >= low_lane) & (lane < low_lane + p.vhead)).astype(FULL)

    def normed_bytes():
        load_feats.wait()

        @pl.loop(0, p.rows_in // 64)
        def _(i):
            rows = at(i * 64, 64)
            normed, _ = ln_parts(s.feats[rows, :].astype(FULL))
            s.nin[rows, :] = (normed * vec[2:3, 0 : p.din] + vec[3:4, 0 : p.din]).astype(LOW)

    def turned_bytes():
        @pl.loop(0, p.din // 128)
        def _(i):
            tile = at(i * 128, 128)
            s.nin_t[tile, :] = s.nin[:, tile].T

    def make_keys():
        @pl.loop(0, p.seqs)
        def _(i):
            rows = at(i * p.slots, p.slots)
            low = matmul(s.nin[rows, :], s.wk[...]).astype(LOW)
            s.keys[rows, :] = low
            s.keys_t[:, rows] = low.T

    def normed_latents():
        @pl.loop(0, p.lat // 64)
        def _(i):
            rows = at(i * 64, 64)
            normed, _ = ln_parts(s.lat[rows, :].astype(FULL))
            s.nlat[rows, :] = (normed * gain_lat + bias_lat).astype(LOW)

    def make_queries():
        queries = matmul(s.nlat[...], s.wq[...])
        lane_q = lanes(p.lat, p.qk)
        for head in range(H):
            inside = (lane_q >= head * p.head) & (lane_q < (head + 1) * p.head)
            s.qmask[head * p.lat : (head + 1) * p.lat, :] = jnp.where(inside, queries, 0.0).astype(LOW)

    max_pair = cp.group()

    def make_scores():
        s.stat[...] = jnp.zeros_like(s.stat)
        for seq in range(p.seqs):

            @pl.loop(0, H)
            def _(head):
                raw = matmul_nt(
                    s.qmask[at(head * p.lat, p.lat), :], s.keys[seq * p.slots : (seq + 1) * p.slots, :]
                )
                valid = lanes(p.lat, p.slots) < lengths[seq] - start_slot
                scores = jnp.where(valid, raw * score_scale, -1e30)
                s.scores[at((seq * H + head) * p.lat, p.lat), :] = scores
                top = jnp.max(scores, axis=-1, keepdims=True)
                s.stat[...] = jnp.where(lanes(p.lat, 128) == seq * H + head, top, s.stat[...])

        s.stat_t[...] = s.stat[...].T
        s.max_own[...] = s.stat_t[0 : 2 * H, :]
        for peer in plane:
            cp.send(max_pair, s.max_own, s.max_in.at[c], peer, z)
        cp.sent(max_pair, s.max_in.at[0 : ctx - 1])

    def make_values():
        @pl.loop(0, p.vd // 256)
        def _(i):
            tile = at(i * 256, 256)
            s.values[:, tile] = matmul(s.nin[...], s.wv[:, tile]).astype(LOW)

    def get_max():
        cp.got(max_pair, s.max_in.at[0 : ctx - 1])
        s.max_in[c] = s.max_own[...]
        top = s.max_in[0]
        for i in range(1, ctx):
            top = jnp.maximum(top, s.max_in[i])
        s.max_all[...] = top
        s.stat_t[0 : 2 * H, :] = top
        s.max_t[...] = s.stat_t[...].T
        s.stat[...] = jnp.zeros_like(s.stat)

    def partial(seq):
        s.numer[...] = jnp.zeros_like(s.numer)

        @pl.loop(0, H)
        def _(head):
            i = seq * H + head
            lane = lanes(p.lat, 128)
            top = jnp.sum(jnp.where(lane == i, s.max_t[...], 0.0), axis=-1, keepdims=True)
            weights = jnp.exp(s.scores[at(i * p.lat, p.lat), :] - top)
            total = jnp.sum(weights, axis=-1, keepdims=True)
            s.stat[...] = jnp.where(lane == i, total, s.stat[...])
            cols, low_lane = window(head)
            part = s.values[at(seq * p.slots, p.slots), cols] * mask_of(p.slots, low_lane).astype(LOW)
            s.numer[:, cols] += matmul(weights.astype(LOW), part)

        s.stat_t[...] = s.stat[...].T
        s.sums[seq] = s.stat_t[at(seq * H, H), :]

    pair_pair, sums_pair = cp.group(), cp.group()
    chip_sums_pair = cp.group()
    chip_pairs, att_pairs = [cp.group() for _ in range(2)], [cp.group() for _ in range(2)]
    near_chip = [lax.div(near[0], 2), lax.div(near[1], 2)]

    def partial_other():
        partial(other)
        s.numer_low[...] = s.numer[...].astype(LOW)
        cp.send(sums_pair, s.sums.at[other], s.sums_in, core, z)
        cp.send(pair_pair, s.numer_low, s.numer_in, core, z)
        cp.sent(pair_pair, s.numer_low)
        cp.sent(sums_pair, s.sums_in)

    def partial_own():
        partial(h)

    def chip_numer():
        cp.got(sums_pair, s.sums_in)
        s.chip_sums[...] = s.sums[h] + s.sums_in[...]
        for peer in chips:
            cp.send(chip_sums_pair, s.chip_sums, s.chip_sums_in.at[q], peer, z)
        cp.sent(chip_sums_pair, s.chip_sums_in.at[0:3])
        cp.got(pair_pair, s.numer_in)
        s.chip[...] = (s.numer[...] + s.numer_in[...].astype(FULL)).astype(LOW)
        for slot, qq in enumerate((3 - q, near_chip[0])):
            rows = at(qq * quarter, quarter)
            cp.send(chip_pairs[0], s.chip.at[rows, :], s.chip_in.at[slot], near[0], z)
        cp.sent(chip_pairs[0], s.chip_in.at[0:2])

    def chip_pass():
        cp.got(chip_pairs[0], s.chip_in.at[0:2])
        rows = at(near_chip[1] * quarter, quarter)
        s.chip_in[3] = (s.chip[rows, :].astype(FULL) + s.chip_in[0].astype(FULL)).astype(LOW)
        cp.send(chip_pairs[1], s.chip_in.at[3], s.chip_in.at[2], near[1], z)
        cp.sent(chip_pairs[1], s.chip_in.at[3])

    def turned_weights():
        for seq in range(p.seqs):

            @pl.loop(0, H)
            def _(head):
                i = seq * H + head
                raw = matmul_nt(
                    s.keys[seq * p.slots : (seq + 1) * p.slots, :], s.qmask[at(head * p.lat, p.lat), :]
                )
                slot = lax.broadcasted_iota(jnp.int32, (p.slots, p.lat), 0)
                masked = jnp.where(slot < lengths[seq] - start_slot, raw * score_scale, -1e30)
                s.scores[at(i * p.slots, p.slots), :] = jnp.exp(masked - s.max_all[pl.ds(i, 1), :])

    def make_scale():
        cp.got(chip_sums_pair, s.chip_sums_in.at[0:3])
        s.chip_sums_in[q] = s.chip_sums[...]
        sums = s.chip_sums_in
        inverse = 1.0 / ((sums[0] + sums[1]) + (sums[2] + sums[3]))
        s.stats[h, 0:H, :] = inverse
        s.stat_t[0:H, :] = inverse
        s.stat[...] = s.stat_t[...].T
        s.scale[...] = jnp.zeros_like(s.scale)
        own_quarter = s.stat[at(q * quarter, quarter), :]
        for head in range(H):
            low_lane = head * p.vhead // 128 * 128
            lane = lanes(quarter, 256) + low_lane
            inside = (lane >= head * p.vhead) & (lane < (head + 1) * p.vhead)
            cols = slice(low_lane, low_lane + 256)
            s.scale[:, cols] = jnp.where(inside, own_quarter[:, head : head + 1], s.scale[:, cols])

    def make_att():
        cp.got(chip_pairs[1], s.chip_in.at[2])
        own_numer = s.chip[at(q * quarter, quarter), :].astype(FULL)
        added = own_numer + (s.chip_in[1].astype(FULL) + s.chip_in[2].astype(FULL))
        s.att[own_rows, :] = (added * s.scale[...]).astype(LOW)
        cp.send(att_pairs[0], s.att.at[own_rows, :], s.att.at[own_rows, :], near[0], z)
        cp.sent(att_pairs[0], s.att.at[0:quarter, :])

    def att_pass():
        cp.got(att_pairs[0], s.att.at[0:quarter, :])
        for qq in (q, near_chip[0]):
            rows = at(h * p.lat + qq * quarter, quarter)
            cp.send(att_pairs[1], s.att.at[rows, :], s.att.at[rows, :], near[1], z)
        cp.sent(att_pairs[1], s.att.at[0 : 2 * quarter, :])

    shares = {}

    def share(ref):
        pair = cp.group()
        cp.send(pair, ref.at[own, :], ref.at[own, :], core, z)
        cp.sent(pair, ref.at[0 : p.lat, :])
        shares[id(ref)] = pair

    def shared(ref):
        cp.got(shares.pop(id(ref)), ref.at[0 : p.lat, :])

    def get_att():
        cp.got(att_pairs[1], s.att.at[0 : 2 * quarter, :])
        share(s.att)

    def make_hidden():
        @pl.loop(0, tiles)
        def _(i):
            tile = at(i * 256, 256)
            s.hid[:, tile] = s.lat[:, tile].astype(FULL) + matmul(s.att[own, :], s.wo[:, tile])

    def make_mid():
        @pl.loop(0, p.lat // 64)
        def _(i):
            normed, _ = ln_parts(s.hid[at(i * 64, 64), :])
            s.mid[at(h * p.lat + i * 64, 64), :] = (normed * gain_mlp + bias_mlp).astype(LOW)

        share(s.mid)

    def make_act():
        load_cot.wait()

        @pl.loop(0, tiles)
        def _(i):
            tile = at(i * 256, 256)
            up = matmul(s.mid[own, :], s.wu[:, tile])
            cdf = 0.5 * (1.0 + lax.erf(up * (1.0 / math.sqrt(2.0))))
            density = jnp.exp(-0.5 * up * up) * (1.0 / math.sqrt(2.0 * math.pi))
            s.act[own, tile] = (up * cdf).astype(LOW)
            s.slope[:, tile] = cdf + up * density

        share(s.act)

    class Reduce:
        def __init__(self, left, right, grads, arrive, final, out):
            self.left, self.right, self.out = left, right, out
            self.grads, self.arrive, self.final = grads, arrive, final
            self.part = self.final.shape[0]
            self.rows = self.part * 4
            self.pairs = [cp.group() for _ in range(4)]

        def product(self):
            @pl.loop(0, self.grads.shape[0] // 256)
            def _(i):
                rows = at(i * 256, 256)
                self.grads[rows, :] = matmul_tn(self.left[:, rows], self.right[:, half_cols]).astype(LOW)

        def block(self, zz):
            return self.grads.at[at(zz * self.rows + q * self.part, self.part, 16), :]

        def scatter(self):
            for peer in zed:
                cp.send(self.pairs[0], self.block(peer), self.arrive.at[z], c, peer)
            cp.sent(self.pairs[0], self.arrive.at[0 : zs - 1])

        def add(self):
            cp.got(self.pairs[0], self.arrive.at[0 : zs - 1])
            self.arrive[z] = self.grads[at(z * self.rows + q * self.part, self.part, 16), :]
            total = self.arrive[0].astype(FULL)
            for zz in range(1, zs):
                total = total + self.arrive[zz].astype(FULL)
            self.final[...] = total.astype(LOW)
            here = self.out.at[at(q * self.part, self.part, 16), half_cols]
            cp.send(self.pairs[1], self.final, here, near[0], z)
            cp.sent(self.pairs[1], self.final)
            self.store = cp.local(self.final, here)

        def spread(self):
            cp.got(self.pairs[1], self.final)
            here = self.out.at[at(q * self.part, self.part, 16), half_cols]
            there = self.out.at[at(near_chip[0] * self.part, self.part, 16), half_cols]
            cp.send(self.pairs[2], self.final, here, near[1], z)
            cp.send(self.pairs[2], there, there, near[1], z)
            cp.sent(self.pairs[2], self.arrive.at[0:2])

        def halve(self):
            cp.got(self.pairs[2], self.arrive.at[0:2])
            self.store.wait()
            block = self.out.at[:, half_cols]
            cp.send(self.pairs[3], block, block, core, z)
            cp.sent(self.pairs[3], block)

        def done(self):
            cp.got(self.pairs[3], self.out.at[:, half_cols])

    down = Reduce(s.act, s.cot, s.dwd, s.zd, s.fd, gd)
    upper = Reduce(s.mid, s.dup, s.dwu, s.zu, s.fu, gu)
    outer = Reduce(s.att, s.dhid, s.dwo, s.zo, s.fo, go)
    latents = Reduce(s.att, s.dhid, s.dlat, s.zl, s.fl, gl)
    reduces = (down, upper, outer, latents)

    def down_grads():
        shared(s.act)
        down.product()
        down.scatter()

    def upper_grads():
        shared(s.mid)
        shared(s.dup)
        upper.product()
        upper.scatter()

    def outer_grads():
        shared(s.att)
        shared(s.dhid)
        outer.product()
        outer.scatter()
        s.dlat[...] = (
            s.dhid[0 : p.lat, half_cols].astype(FULL) + s.dhid[p.lat : 2 * p.lat, half_cols].astype(FULL)
        ).astype(LOW)
        latents.scatter()

    def make_dup():
        @pl.loop(0, tiles)
        def _(i):
            tile = at(i * 256, 256)
            dact = matmul_nt(s.cot[own, :], s.wd[tile, :])
            s.dup[own, tile] = (dact * s.slope[:, tile]).astype(LOW)

        share(s.dup)

    def make_dmid():
        @pl.loop(0, tiles)
        def _(i):
            tile = at(i * 256, 256)
            s.dmid[:, tile] = matmul_nt(s.dup[own, :], s.wu[tile, :])

    def make_dhid():
        s.vs[...] = jnp.zeros_like(s.vs)

        @pl.loop(0, p.lat // 64)
        def _(i):
            rows = at(i * 64, 64)
            full_rows = at(h * p.lat + i * 64, 64)
            normed, scale = ln_parts(s.hid[rows, :])
            grad = s.dmid[rows, :]
            s.vs[0:1, :] += columns_sum(grad * normed)
            s.vs[1:2, :] += columns_sum(grad)
            total = s.cot[full_rows, :].astype(FULL) + ln_grad(grad, gain_mlp, normed, scale)
            s.dhid[full_rows, :] = total.astype(LOW)

        share(s.dhid)

    stats_pairs = [cp.group() for _ in range(2)]

    def share_inverse():
        cp.send(stats_pairs[0], s.stats.at[h, 0:H], s.stats.at[h, 0:H], core, z)
        cp.sent(stats_pairs[0], s.stats.at[0, 0:H])

    def make_datt():
        @pl.loop(0, tiles)
        def _(i):
            tile = at(i * 256, 256)
            s.datt[own, tile] = matmul_nt(s.dhid[own, :], s.wo[tile, :]).astype(LOW)

        share(s.datt)

    def make_delta():
        s.stat[...] = jnp.zeros_like(s.stat)

        @pl.loop(0, H)
        def _(head):
            cols, low_lane = window(head)
            product = s.datt[own, cols].astype(FULL) * s.att[own, cols].astype(FULL)
            delta = jnp.sum(product * mask_of(p.lat, low_lane), axis=-1, keepdims=True)
            s.stat[...] = jnp.where(lanes(p.lat, 128) == head, delta, s.stat[...])

        s.stat_t[...] = s.stat[...].T
        s.stats[h, H : 2 * H, :] = s.stat_t[0:H, :]
        cp.send(stats_pairs[1], s.stats.at[h, H : 2 * H], s.stats.at[h, H : 2 * H], core, z)
        cp.sent(stats_pairs[1], s.stats.at[0, 0:H])

    def values_grad(seq):
        latent_rows = at(seq * p.lat, p.lat)
        s.numer[...] = jnp.zeros_like(s.numer)

        @pl.loop(0, H)
        def _(head):
            cols, low_lane = window(head)
            inverse = s.stats[seq, pl.ds(head, 1), :]
            probs = s.scores[at((seq * H + head) * p.slots, p.slots), :] * inverse
            grad = s.datt[latent_rows, cols] * mask_of(p.lat, low_lane).astype(LOW)
            s.numer[:, cols] += matmul(probs.astype(LOW), grad)

        s.dvalues[at(seq * p.slots, p.slots), :] = s.numer[...].astype(LOW)

    def scores_grad(seq):
        slots = at(seq * p.slots, p.slots)
        latent_rows = at(seq * p.lat, p.lat)
        s.dk_sum[...] = jnp.zeros_like(s.dk_sum)

        @pl.loop(0, H)
        def _(head):
            heads = at(head * p.lat, p.lat)
            cols, low_lane = window(head)
            inverse = s.stats[seq, pl.ds(head, 1), :]
            delta = s.stats[seq, pl.ds(H + head, 1), :]
            probs = s.scores[at((seq * H + head) * p.slots, p.slots), :] * inverse
            grad = s.datt[latent_rows, cols] * mask_of(p.lat, low_lane).astype(LOW)
            dprobs = matmul_nt(s.values[slots, cols], grad)
            dscores = (probs * (dprobs - delta)).astype(LOW)
            s.dk_sum[...] += matmul(dscores, s.qmask[heads, :])
            block = at(head * p.head, p.head)
            s.dq_t[block, :] += matmul(s.keys_t[block, slots], dscores)

        s.dkeys[slots, :] = (s.dk_sum[...] * score_scale).astype(LOW)

    def weight_grads(ref, grad, width, side):
        cols = at(side * width, width)

        @pl.loop(0, p.din // 256)
        def _(i):
            rows = at(i * 256, 256)
            ref[side, rows, :] = matmul(s.nin_t[rows, :], grad[:, cols]).astype(LOW)

    class Local:
        def __init__(self, grads, arrive, chip, plane_in, plane, z_in, final, out):
            self.grads, self.arrive, self.chip, self.plane_in = grads, arrive, chip, plane_in
            self.plane, self.z_in, self.final, self.out = plane, z_in, final, out
            self.width = final.shape[1]
            self.pairs = [cp.group() for _ in range(5)]
            self.firsts = [cp.group() for _ in range(zs // 2)]
            self.seconds = [cp.group() for _ in range(zs // 2)]
            self.mine = at(h * self.width, self.width)

        def pair(self):
            cp.send(self.pairs[0], self.grads.at[other], self.arrive, core, z)
            cp.sent(self.pairs[0], self.arrive)

        def rows(self, qq):
            return at(qq * vpart, vpart, 16)

        def chunk(self, i):
            for zz in order[2 * i : 2 * i + 2]:
                rows = at(zz * zrows, zrows)
                total = self.grads[h, rows, :].astype(FULL) + self.arrive[rows, :].astype(FULL)
                self.chip[zz] = total.astype(LOW)
                for slot, qq in enumerate((3 - q, near_chip[0])):
                    cp.send(
                        self.firsts[i],
                        self.chip.at[zz, self.rows(qq), :],
                        self.plane_in.at[slot, zz],
                        near[0],
                        z,
                    )
            cp.sent(self.firsts[i], self.plane_in.at[0])

        def middle(self, i):
            cp.got(self.firsts[i], self.plane_in.at[0])
            for zz in order[2 * i : 2 * i + 2]:
                mine = self.chip[zz, self.rows(near_chip[1]), :].astype(FULL)
                self.plane_in[3, zz] = (mine + self.plane_in[0, zz].astype(FULL)).astype(LOW)
                cp.send(self.seconds[i], self.plane_in.at[3, zz], self.plane_in.at[2, zz], near[1], z)
            cp.sent(self.seconds[i], self.plane_in.at[0, 0:2])

        def add(self, i):
            cp.got(self.seconds[i], self.plane_in.at[0, 0:2])
            for zz in order[2 * i : 2 * i + 2]:
                mine = self.chip[zz, self.rows(q), :].astype(FULL)
                parts = self.plane_in[1, zz].astype(FULL) + self.plane_in[2, zz].astype(FULL)
                self.plane[zz] = (mine + parts).astype(LOW)
                if zz is not order[-1]:
                    cp.send(self.pairs[1], self.plane.at[zz], self.z_in.at[z], c, zz)
            if i == zs // 2 - 1:
                cp.sent(self.pairs[1], self.z_in.at[0 : zs - 1])

        def finish(self):
            cp.got(self.pairs[1], self.z_in.at[0 : zs - 1])
            self.z_in[z] = self.plane[z]
            total = self.z_in[0].astype(FULL)
            for zz in range(1, zs):
                total = total + self.z_in[zz].astype(FULL)
            self.final[...] = total.astype(LOW)
            here = self.out.at[self.rows(q), self.mine]
            cp.send(self.pairs[2], self.final, here, near[0], z)
            cp.sent(self.pairs[2], self.final)
            self.store = cp.local(self.final, here)

        def spread(self):
            cp.got(self.pairs[2], self.final)
            here = self.out.at[self.rows(q), self.mine]
            there = self.out.at[self.rows(near_chip[0]), self.mine]
            cp.send(self.pairs[3], self.final, here, near[1], z)
            cp.send(self.pairs[3], there, there, near[1], z)
            cp.sent(self.pairs[3], self.z_in.at[0:2])

        def halve(self):
            cp.got(self.pairs[3], self.z_in.at[0:2])
            self.store.wait()
            block = self.out.at[:, self.mine]
            cp.send(self.pairs[4], block, block, core, z)
            cp.sent(self.pairs[4], block)

        def done(self):
            cp.got(self.pairs[4], self.out.at[:, self.mine])

    key_grads = Local(s.swk, s.rwk, s.cwk, s.pwk_in, s.pwk, s.zwk_in, s.fwk, gk)
    value_grads = Local(s.swv, s.rwv, s.cwv, s.pwv_in, s.pwv, s.zwv_in, s.fwv, gv)
    def byte_part(part):
        @pl.loop(part * 2, part * 2 + 2)
        def _(i):
            rows = at(i * 64, 64)
            grad = matmul_nt(s.dkeys[rows, :], s.wk[...]) + matmul_nt(s.dvalues[rows, :], s.wv[...])
            normed, scale = ln_parts(s.feats[rows, :].astype(FULL))
            s.vs[2:3, 0 : p.din] += columns_sum(grad * normed)
            s.vs[3:4, 0 : p.din] += columns_sum(grad)
            s.bgrad[rows, :] = ln_grad(grad, vec[2:3, 0 : p.din], normed, scale).astype(LOW)

    kv = (value_grads, key_grads)
    dq_pairs = [cp.group() for _ in range(5)]
    vs_pairs = [cp.group() for _ in range(3)]
    res_pair = cp.group()
    stores = []
    own_half = at(h * qhalf, qhalf)

    def values_own():
        values_grad(h)

    def values_other():
        cp.got(stats_pairs[0], s.stats.at[0, 0:H])
        shared(s.datt)
        values_grad(other)

    def value_weights():
        weight_grads(s.swv, s.dvalues, vhalf, other)
        value_grads.pair()

    def value_weights_own():
        weight_grads(s.swv, s.dvalues, vhalf, h)

    def value_chunks():
        cp.got(value_grads.pairs[0], value_grads.arrive)
        for i in range(zs // 2):
            value_grads.chunk(i)

    def scores_own():
        s.dq_t[...] = jnp.zeros_like(s.dq_t)
        scores_grad(h)

    def scores_other():
        cp.got(stats_pairs[1], s.stats.at[0, 0:H])
        scores_grad(other)
        s.dq[...] = (s.dq_t[...] * score_scale).T.astype(LOW)
        cp.send(dq_pairs[0], s.dq.at[:, at(other * qhalf, qhalf)], s.dq_in1, core, z)
        cp.sent(dq_pairs[0], s.dq_in1)

    def key_weights():
        weight_grads(s.swk, s.dkeys, qhalf, other)
        key_grads.pair()
        weight_grads(s.swk, s.dkeys, qhalf, h)

    def dq_chip():
        cp.got(dq_pairs[0], s.dq_in1)
        s.dq_chip[...] = (s.dq[:, own_half].astype(FULL) + s.dq_in1[...].astype(FULL)).astype(LOW)
        cp.send(dq_pairs[1], s.dq_chip, s.dq_in2.at[0], near[0], z)
        cp.sent(dq_pairs[1], s.dq_chip)

    def dq_pass():
        cp.got(dq_pairs[1], s.dq_chip)
        s.dq_in2[2] = (s.dq_chip[...].astype(FULL) + s.dq_in2[0].astype(FULL)).astype(LOW)
        cp.send(dq_pairs[4], s.dq_in2.at[2], s.dq_in2.at[1], near[1], z)
        cp.sent(dq_pairs[4], s.dq_chip)

    def key_chunks():
        cp.got(key_grads.pairs[0], key_grads.arrive)
        for i in range(zs // 2):
            key_grads.chunk(i)

    def byte_store():
        stores.append(cp.local(s.bgrad, byte_out))
        cp.send(vs_pairs[0], s.vs, s.vs_in1, core, z)
        cp.sent(vs_pairs[0], s.vs)

    def dq_plane():
        cp.got(dq_pairs[4], s.dq_chip)
        s.dq_plane[...] = (s.dq_in2[1].astype(FULL) + s.dq_in2[2].astype(FULL)).astype(LOW)
        for peer in zed:
            cp.send(dq_pairs[2], s.dq_plane, s.dq_in3.at[z], c, peer)
        cp.sent(dq_pairs[2], s.dq_in3.at[0 : zs - 1])

    def vs_chip():
        cp.got(vs_pairs[0], s.vs_in1)
        s.vs_chip[...] = s.vs[...] + s.vs_in1[...]
        for peer in chips:
            cp.send(vs_pairs[1], s.vs_chip, s.vs_in2.at[q], peer, z)
        cp.sent(vs_pairs[1], s.vs_in2.at[0:3])

    def make_result():
        @pl.loop(0, tiles)
        def _(i):
            tile = at(i * 256, 256)
            s.res[:, tile] = (s.hid[:, tile] + matmul(s.act[own, :], s.wd[:, tile])).astype(LOW)

        cp.send(res_pair, s.res, res_out.at[own, :], core, z)
        cp.sent(res_pair, s.res)
        stores.append(cp.local(s.res, res_out.at[own, :]))

    def vs_plane():
        cp.got(vs_pairs[1], s.vs_in2.at[0:3])
        s.vs_in2[q] = s.vs_chip[...]
        parts = s.vs_in2
        total = (parts[0] + parts[1]) + (parts[2] + parts[3])
        row_ids = lax.broadcasted_iota(jnp.int32, (8, p.dl), 0)
        s.vs_plane[...] = jnp.where(row_ids < 2, s.vs_chip[...], total)
        for peer in zed:
            cp.send(vs_pairs[2], s.vs_plane, s.vs_in3.at[z], c, peer)
        cp.sent(vs_pairs[2], s.vs_in3.at[0 : zs - 1])

    def dq_total():
        cp.got(dq_pairs[2], s.dq_in3.at[0 : zs - 1])
        s.dq_in3[z] = s.dq_plane[...]
        parts = s.dq_in3
        total = parts[0].astype(FULL)
        for zz in range(1, zs):
            total = total + parts[zz].astype(FULL)
        s.dq_all[:, own_half] = total.astype(LOW)
        cp.send(dq_pairs[3], s.dq_all.at[:, own_half], s.dq_all.at[:, own_half], core, z)
        cp.sent(dq_pairs[3], s.dq_in1)

    def query_grads():
        cp.got(dq_pairs[3], s.dq_in1)

        @pl.loop(0, tiles)
        def _(i):
            tile = at(i * 256, 256)
            s.gq[tile, :] = matmul_tn(s.nlat[:, tile], s.dq_all[...])
            s.dmid[:, tile] = matmul_nt(s.dq_all[...], s.wq[tile, :])

        stores.append(cp.local(s.gq.at[at(z * (p.dl // zs), p.dl // zs, 16), :], gq_out))

    def latent_grads():
        cp.got(vs_pairs[2], s.vs_in3.at[0 : zs - 1])
        s.vs_in3[z] = s.vs_plane[...]
        total = s.vs_in3[0]
        for zz in range(1, zs):
            total = total + s.vs_in3[zz]
        s.vs_all[...] = total
        s.vs_all[4:6, :] = jnp.zeros((2, p.dl), FULL)

        @pl.loop(0, p.lat // 64)
        def _(i):
            rows = at(i * 64, 64)
            normed, scale = ln_parts(s.lat[rows, :].astype(FULL))
            grad = s.dmid[rows, :]
            s.vs_all[4:5, :] += columns_sum(grad * normed)
            s.vs_all[5:6, :] += columns_sum(grad)
            s.slope[rows, :] = ln_grad(grad, gain_lat, normed, scale)

        stores.append(cp.local(s.slope.at[at(z * (p.lat // zs), p.lat // zs, 16), :], glat_out))
        stores.append(cp.local(s.vs_all, vec_out))

    wq.first()
    wk.first()
    normed_bytes()
    lat.first()
    lat.second()
    turned_bytes()
    wk.second()
    wq.second()
    wk.third()
    wq.third()
    wk.ready()
    wv.first()
    wo.hop(1)
    make_keys()
    wq.ready()
    lat.third()
    wu.hop(0)
    lat.ready()
    normed_latents()
    make_queries()
    wo.hop(2)
    wv.second()
    make_scores()
    wd.hop(0)
    wo.first()
    wv.third()
    get_max()
    wu.hop(1)
    wv.ready()
    make_values()
    wo.second()
    wu.hop(2)
    partial_other()
    partial_own()
    chip_numer()
    wd.hop(1)
    wu.first()
    wo.third()
    turned_weights()
    chip_pass()
    wu.second()
    wd.hop(2)
    make_scale()
    make_att()
    att_pass()
    wu.third()
    share_inverse()
    wo.ready()
    wd.first()
    get_att()
    make_hidden()
    make_mid()
    wu.ready()
    make_act()
    wd.third()
    down_grads()
    wd.ready()
    make_dup()
    make_dmid()
    make_dhid()
    make_datt()
    make_delta()
    values_own()
    values_other()
    value_weights()
    down.add()
    upper_grads()
    value_weights_own()
    value_chunks()
    scores_own()
    scores_other()
    value_grads.middle(0)
    value_grads.middle(1)
    dq_chip()
    key_weights()
    value_grads.add(0)
    down.spread()
    value_grads.add(1)
    key_chunks()
    outer_grads()
    down.halve()
    key_grads.middle(0)
    dq_pass()
    upper.add()
    key_grads.middle(1)
    byte_part(0)
    byte_part(1)
    byte_part(2)
    byte_part(3)
    byte_store()
    key_grads.add(0)
    key_grads.add(1)
    dq_plane()
    upper.spread()
    value_grads.finish()
    value_grads.spread()
    make_result()
    vs_chip()
    outer.add()
    upper.halve()
    key_grads.finish()
    value_grads.halve()
    latents.add()
    vs_plane()
    outer.spread()
    key_grads.spread()
    dq_total()
    latents.spread()
    query_grads()
    key_grads.halve()
    outer.halve()
    latents.halve()
    latent_grads()
    for part in (*reduces, *kv):
        part.done()
    cp.got(res_pair, s.res)
    for store in stores:
        store.wait()
    cp.drain()


def finish_kernel(p, res, byte, go, gu, gd, gv, gk, gl, gq, glat, vec, *outs):
    z = lax.axis_index("wshard")
    outs[0][...] = res[...]
    outs[1][...] = byte[...]
    outs[2][...] = glat[...] + gl[...].astype(FULL)
    for out, row in ((3, 4), (4, 5), (5, 2), (6, 3), (11, 0), (12, 1)):
        size = outs[out].shape[0]
        picked = vec[row : row + 1, 0:size]
        for zz in range(1, p.zs):
            picked = jnp.where(z == zz, vec[row : row + 1, zz * size : (zz + 1) * size], picked)
        outs[out][...] = picked.reshape(size)
    outs[7][...] = gq[...]
    for out, source in ((8, gk), (9, gv), (10, go), (13, gu), (14, gd)):
        outs[out][...] = source[...].astype(FULL)


def fused(*args):
    (byte_feats, lengths, latent, *smalls, cot) = (args[0], args[1], args[2], *args[3:7], args[11], args[12], args[15])
    w_query, w_key, w_value, w_output = args[7:11]
    w_up, w_down = args[13:15]
    seqs, slots, din = byte_feats.shape
    ctx, zs = lax.axis_size("ctx"), lax.axis_size("wshard")
    feats = byte_feats.reshape(seqs * slots, din)
    cot_flat = cot.reshape(-1, cot.shape[-1])
    p = Plan(ctx, zs, feats, latent, w_query, w_key, w_value, w_output, cot_flat)
    table = scratch_table(p)
    anywhere = pl.BlockSpec(memory_space=pl.ANY)
    in_vmem = pl.BlockSpec(memory_space=pltpu.VMEM)
    struct = jax.ShapeDtypeStruct
    made = pl.pallas_call(
        functools.partial(fused_kernel, p, tuple(table)),
        out_shape=(
            struct(cot_flat.shape, LOW),
            struct(feats.shape, LOW),
            struct(w_output.shape, LOW),
            struct(w_up.shape, LOW),
            struct(w_down.shape, LOW),
            struct(w_value.shape, LOW),
            struct(w_key.shape, LOW),
            struct(latent.shape, LOW),
            struct(w_query.shape, FULL),
            struct(latent.shape, FULL),
            struct((8, p.dl), FULL),
        ),
        in_specs=[pl.BlockSpec(memory_space=pltpu.SMEM)] + [anywhere] * 8 + [in_vmem] * 6 + [anywhere],
        out_specs=(anywhere,) * 11,
        scratch_shapes=[pltpu.VMEM(shape, kind) for shape, kind in table.values()]
        + [pltpu.SemaphoreType.DMA((SEMS,))],
        compiler_params=pltpu.CompilerParams(
            collective_id=0, has_side_effects=True, vmem_limit_bytes=67043328
        ),
        name="block",
    )(lengths, feats, latent, w_query, w_key, w_value, w_output, w_up, w_down, *smalls, cot_flat)
    shapes = (
        (cot_flat.shape, LOW),
        (feats.shape, LOW),
        (latent.shape, FULL),
        *((smalls[i].shape, FULL) for i in range(4)),
        *((w.shape, FULL) for w in (w_query, w_key, w_value, w_output)),
        *((smalls[i].shape, FULL) for i in (4, 5)),
        *((w.shape, FULL) for w in (w_up, w_down)),
    )
    outs = pl.pallas_call(
        functools.partial(finish_kernel, p),
        out_shape=tuple(struct(shape, kind) for shape, kind in shapes),
        in_specs=[in_vmem] * 11,
        out_specs=(in_vmem,) * 15,
        compiler_params=pltpu.CompilerParams(vmem_limit_bytes=60 * 2**20),
        name="finish",
    )(*made)
    return (outs[0].reshape(cot.shape), outs[1].reshape(byte_feats.shape), *outs[2:])


def shards(*args):
    if lax.axis_size("ctx") == 8 and lax.axis_size("wshard") == 4 and args[0].shape[0] == 2:
        return fused(*args)
    return plain(*args)


def solution(mesh):
    sharded, plain = P("wshard", None), P("wshard")
    return jax.shard_map(
        shards,
        mesh=mesh,
        in_specs=(
            P("wshard", "ctx", None),
            plain,
            sharded,
            plain,
            plain,
            plain,
            plain,
            sharded,
            sharded,
            sharded,
            sharded,
            plain,
            plain,
            sharded,
            sharded,
            P("wshard", None, None),
        ),
        out_specs=(
            P("wshard", None, None),
            P("wshard", "ctx", None),
            sharded,
            plain,
            plain,
            plain,
            plain,
            sharded,
            sharded,
            sharded,
            sharded,
            plain,
            plain,
            sharded,
            sharded,
        ),
        check_vma=False,
    )
```

```python
import functools
import math
import types

import jax
import jax.numpy as jnp
from jax import lax
from jax.experimental import pallas as pl
from jax.experimental.pallas import tpu as pltpu
from jax.sharding import PartitionSpec as P

H = 8
LOW = jnp.bfloat16
FULL = jnp.float32


def layer_norm(values, gain, offset):
    center = jnp.mean(values, axis=-1, keepdims=True)
    centred = values - center
    variance = jnp.mean(centred * centred, axis=-1, keepdims=True)
    return centred * lax.rsqrt(variance + 1e-05) * gain + offset


def exact_gelu(values):
    return jax.nn.gelu(values, approximate=False)


def matmul(left, right):
    return jnp.dot(left, right, preferred_element_type=FULL)


def matmul_tn(left, right):
    return lax.dot_general(left, right, (((0,), (0,)), ((), ())), preferred_element_type=FULL)


def matmul_nt(left, right):
    return lax.dot_general(left, right, (((1,), (1,)), ((), ())), preferred_element_type=FULL)


def gather(shard):
    return lax.all_gather(shard, "wshard", axis=0, tiled=True)


def scatter(total):
    return lax.psum_scatter(
        total.astype(LOW), "wshard", scatter_dimension=0, tiled=True
    ).astype(FULL)


SEMS = 256


def own_part(total, shard):
    size = shard.shape[0]
    return lax.dynamic_slice_in_dim(total, lax.axis_index("wshard") * size, size, 0)


def plain(
    byte_feats,
    lengths,
    latent_array,
    lat_gain,
    lat_bias,
    in_gain,
    in_bias,
    w_query,
    w_key,
    w_value,
    w_output,
    mlp_gain,
    mlp_bias,
    w_up,
    w_down,
    cotangent,
):
    seqs, slots, width = byte_feats.shape
    gain_in, bias_in = gather(in_gain).astype(FULL), gather(in_bias).astype(FULL)
    key_w, value_w = gather(w_key), gather(w_value)
    latent = gather(latent_array).astype(FULL)
    gain_lat, bias_lat = gather(lat_gain).astype(FULL), gather(lat_bias).astype(FULL)
    query_w = gather(w_query)
    gain_mlp, bias_mlp = gather(mlp_gain).astype(FULL), gather(mlp_bias).astype(FULL)
    output_w, up_w, down_w = gather(w_output), gather(w_up), gather(w_down)

    features = byte_feats.reshape(seqs * slots, width).astype(FULL)
    normed_in, in_back = jax.vjp(layer_norm, features, gain_in, bias_in)
    input_low = normed_in.astype(LOW)
    keys = matmul(input_low, key_w).astype(LOW)
    values = matmul(input_low, value_w).astype(LOW)
    normed_lat, lat_back = jax.vjp(layer_norm, latent, gain_lat, bias_lat)
    lat_low = normed_lat.astype(LOW)
    rows = lat_low.shape[0]
    queries = matmul(lat_low, query_w).astype(LOW)
    score_scale = 1.0 / math.sqrt(queries.shape[1] // H)
    qheads = queries.reshape(rows, H, -1)
    kheads = keys.reshape(seqs, slots, H, -1)
    vheads = values.reshape(seqs, slots, H, -1)

    scores = jnp.einsum("lhd,mkhd->mhlk", qheads, kheads, preferred_element_type=FULL) * score_scale
    slot_ids = lax.axis_index("ctx") * slots + lax.iota(jnp.int32, slots)
    valid = (slot_ids[None, :] < lengths[:, None])[:, None, None, :]
    scores = jnp.where(valid, scores, -1e30)
    highest = lax.pmax(jnp.max(scores, axis=-1), "ctx")
    weights = jnp.where(valid, jnp.exp(scores - highest[..., None]), 0.0)
    total = lax.psum(jnp.sum(weights, axis=-1), "ctx")
    numer = jnp.einsum("mhlk,mkhe->mlhe", weights.astype(LOW), vheads, preferred_element_type=FULL)
    numer = lax.psum(numer.astype(LOW), "ctx").astype(FULL)
    attended = numer / jnp.transpose(total, (0, 2, 1))[..., None]
    attended = attended.reshape(seqs * rows, -1)

    att_low = attended.astype(LOW)
    hidden = jnp.tile(latent, (seqs, 1)) + matmul(att_low, output_w)
    normed_mid, mid_back = jax.vjp(layer_norm, hidden, gain_mlp, bias_mlp)
    mid_low = normed_mid.astype(LOW)
    upward = matmul(mid_low, up_w)
    activated, gelu_back = jax.vjp(exact_gelu, upward)
    act_low = activated.astype(LOW)
    result = hidden + matmul(act_low, down_w)
    dout_low = cotangent.reshape(seqs * rows, -1)
    grad_down = scatter(matmul_tn(act_low, dout_low))
    (grad_upward,) = gelu_back(matmul_nt(dout_low, down_w))
    up_low = grad_upward.astype(LOW)
    grad_up = scatter(matmul_tn(mid_low, up_low))
    dhid_norm, grad_gmlp, grad_bmlp = mid_back(matmul_nt(up_low, up_w))
    dhidden = dout_low.astype(FULL) + dhid_norm
    dhid_low = dhidden.astype(LOW)
    grad_output = scatter(matmul_tn(att_low, dhid_low))
    grad_hidden = scatter(jnp.sum(dhidden.reshape(seqs, rows, -1), axis=0))
    grad_att = matmul_nt(dhid_low, output_w).astype(LOW)

    grad_heads = grad_att.reshape(seqs, rows, H, -1)
    delta = jnp.sum(
        grad_heads.astype(FULL) * attended.reshape(seqs, rows, H, -1), axis=-1
    ).transpose(0, 2, 1)
    probs = weights / total[..., None]
    dprobs = jnp.einsum("mlhe,mkhe->mhlk", grad_heads, vheads, preferred_element_type=FULL)
    dscores = (probs * (dprobs - delta[..., None])).astype(LOW)
    dquery = jnp.einsum("mhlk,mkhd->lhd", dscores, kheads, preferred_element_type=FULL) * score_scale
    dkeys = jnp.einsum("mhlk,lhd->mkhd", dscores, qheads, preferred_element_type=FULL) * score_scale
    dvalues = jnp.einsum("mhlk,mlhe->mkhe", probs.astype(LOW), grad_heads, preferred_element_type=FULL)
    dkeys = dkeys.astype(LOW).reshape(seqs * slots, -1)
    dvalues = dvalues.astype(LOW).reshape(seqs * slots, -1)

    dquery = lax.psum(dquery.reshape(rows, -1).astype(LOW), ("ctx", "wshard"))
    grad_query = matmul_tn(
        lax.dynamic_slice_in_dim(
            lat_low, lax.axis_index("wshard") * w_query.shape[0], w_query.shape[0], 1
        ),
        dquery,
    )
    dlat_norm, grad_glat, grad_blat = lat_back(matmul_nt(dquery, query_w))
    grad_latent = grad_hidden + own_part(dlat_norm, latent_array)

    dnorm_in = matmul_nt(dkeys, key_w) + matmul_nt(dvalues, value_w)
    dfeatures, grad_gin, grad_bin = in_back(dnorm_in)
    grad_key = lax.psum(scatter(matmul_tn(input_low, dkeys)).astype(LOW), "ctx").astype(FULL)
    grad_value = lax.psum(scatter(matmul_tn(input_low, dvalues)).astype(LOW), "ctx").astype(FULL)
    in_sums = lax.psum(jnp.concatenate([grad_gin, grad_bin]), ("ctx", "wshard"))
    grad_gin, grad_bin = jnp.split(in_sums, 2)
    mlp_sums = lax.psum(jnp.concatenate([grad_gmlp, grad_bmlp]), "wshard")
    grad_gmlp, grad_bmlp = jnp.split(mlp_sums, 2)
    return (
        result.astype(LOW).reshape(seqs, rows, -1),
        dfeatures.astype(LOW).reshape(seqs, slots, width),
        grad_latent,
        own_part(grad_glat, lat_gain),
        own_part(grad_blat, lat_bias),
        own_part(grad_gin, in_gain),
        own_part(grad_bin, in_bias),
        grad_query,
        grad_key,
        grad_value,
        grad_output,
        own_part(grad_gmlp, mlp_gain),
        own_part(grad_bmlp, mlp_bias),
        grad_up,
        grad_down,
    )


def ln_parts(values):
    centred = values - jnp.mean(values, axis=-1, keepdims=True)
    scale = lax.rsqrt(jnp.mean(centred * centred, axis=-1, keepdims=True) + 1e-05)
    return centred * scale, scale


def ln_grad(cotangent, gain, normed, scale):
    scaled = cotangent * gain
    first = jnp.mean(scaled, axis=-1, keepdims=True)
    second = jnp.mean(scaled * normed, axis=-1, keepdims=True)
    return scale * (scaled - first - normed * second)


def lanes(rows, columns):
    return lax.broadcasted_iota(jnp.int32, (rows, columns), 1)


def columns_sum(values):
    return jnp.sum(values, axis=0, keepdims=True)


class Plan:
    def __init__(self, ctx, zs, feats, latent, w_query, w_key, w_value, w_output, cot):
        self.ctx, self.zs = ctx, zs
        self.rows_in, self.din = feats.shape
        self.lat = latent.shape[0] * zs
        self.dl = latent.shape[1]
        self.qk, self.vd = w_key.shape[1], w_value.shape[1]
        self.seqs = cot.shape[0] // self.lat
        self.slots = self.rows_in // self.seqs
        self.head, self.vhead = self.qk // H, self.vd // H


def scratch_table(p):
    both = p.seqs * p.lat
    half = p.dl // 2
    part = p.dl // p.zs // 4
    vpart = p.din // p.zs // 4
    return dict(
        wk=((p.din, p.qk), LOW),
        wq=((p.dl, p.qk), LOW),
        lat=((p.lat, p.dl), LOW),
        wv=((p.din, p.vd), LOW),
        wo=((p.vd, p.dl), LOW),
        wu=((p.dl, p.dl), LOW),
        wd=((p.dl, p.dl), LOW),
        small_own=((8, 384), FULL),
        small=((p.zs, 8, 384), FULL),
        vec=((8, p.dl), FULL),
        feats=((p.rows_in, p.din), LOW),
        nin=((p.rows_in, p.din), LOW),
        nin_t=((p.din, p.rows_in), LOW),
        keys=((p.rows_in, p.qk), LOW),
        keys_t=((p.qk, p.rows_in), LOW),
        values=((p.rows_in, p.vd), LOW),
        nlat=((p.lat, p.dl), LOW),
        qmask=((H * p.lat, p.qk), LOW),
        scores=((p.seqs * H * max(p.lat, p.slots), max(p.lat, p.slots)), FULL),
        stat=((p.lat, 128), FULL),
        stat_t=((128, p.lat), FULL),
        max_t=((p.lat, 128), FULL),
        max_own=((2 * H, p.lat), FULL),
        max_in=((p.ctx, 2 * H, p.lat), FULL),
        max_all=((2 * H, p.lat), FULL),
        numer=((p.lat, p.vd), FULL),
        numer_low=((p.lat, p.vd), LOW),
        numer_in=((p.lat, p.vd), LOW),
        sums=((2, H, p.lat), FULL),
        sums_in=((H, p.lat), FULL),
        chip=((p.lat, p.vd), LOW),
        chip_in=((4, p.lat // 4, p.vd), LOW),
        chip_sums=((H, p.lat), FULL),
        chip_sums_in=((4, H, p.lat), FULL),
        scale=((p.lat // 4, p.vd), FULL),
        att=((both, p.vd), LOW),
        mid=((both, p.dl), LOW),
        act=((both, p.dl), LOW),
        dup=((both, p.dl), LOW),
        dhid=((both, p.dl), LOW),
        datt=((both, p.vd), LOW),
        cot=((both, p.dl), LOW),
        hid=((p.lat, p.dl), FULL),
        slope=((p.lat, p.dl), FULL),
        dmid=((p.lat, p.dl), FULL),
        res=((p.lat, p.dl), LOW),
        stats=((2, 2 * H, p.lat), FULL),
        dwo=((p.vd, half), LOW),
        dwu=((p.dl, half), LOW),
        dwd=((p.dl, half), LOW),
        dlat=((p.lat, half), LOW),
        zo=((p.zs, part, half), LOW),
        zu=((p.zs, part, half), LOW),
        zd=((p.zs, part, half), LOW),
        zl=((p.zs, p.lat // p.zs // 4, half), LOW),
        fo=((part, half), LOW),
        fu=((part, half), LOW),
        fd=((part, half), LOW),
        fl=((p.lat // p.zs // 4, half), LOW),
        dkeys=((p.rows_in, p.qk), LOW),
        dvalues=((p.rows_in, p.vd), LOW),
        dk_sum=((p.slots, p.qk), FULL),
        dq_t=((p.qk, p.lat), FULL),
        dq=((p.lat, p.qk), LOW),
        dq_in1=((p.lat, p.qk // 2), LOW),
        dq_chip=((p.lat, p.qk // 2), LOW),
        dq_in2=((4, p.lat, p.qk // 2), LOW),
        dq_plane=((p.lat, p.qk // 2), LOW),
        dq_in3=((p.zs, p.lat, p.qk // 2), LOW),
        dq_all=((p.lat, p.qk), LOW),
        bgrad=((p.rows_in, p.din), LOW),
        swk=((2, p.din, p.qk // 2), LOW),
        swv=((2, p.din, p.vd // 2), LOW),
        rwk=((p.din, p.qk // 2), LOW),
        rwv=((p.din, p.vd // 2), LOW),
        cwk=((p.zs, p.din // p.zs, p.qk // 2), LOW),
        cwv=((p.zs, p.din // p.zs, p.vd // 2), LOW),
        pwk_in=((4, p.zs, vpart, p.qk // 2), LOW),
        pwv_in=((4, p.zs, vpart, p.vd // 2), LOW),
        pwk=((p.zs, vpart, p.qk // 2), LOW),
        pwv=((p.zs, vpart, p.vd // 2), LOW),
        zwk_in=((p.zs, vpart, p.qk // 2), LOW),
        zwv_in=((p.zs, vpart, p.vd // 2), LOW),
        fwk=((vpart, p.qk // 2), LOW),
        fwv=((vpart, p.vd // 2), LOW),
        vs=((8, p.dl), FULL),
        vs_in1=((8, p.dl), FULL),
        vs_chip=((8, p.dl), FULL),
        vs_in2=((4, 8, p.dl), FULL),
        vs_plane=((8, p.dl), FULL),
        vs_in3=((p.zs, 8, p.dl), FULL),
        vs_all=((8, p.dl), FULL),
        gq=((p.dl, p.qk), FULL),
    )


class Copies:
    def __init__(self, sems):
        self.sems, self.used, self.open = sems, 0, []

    def new(self):
        self.used += 1
        return self.sems.at[self.used - 1]

    def group(self):
        return (self.new(), self.new())

    def send(self, pair, src, dst, ctx, z):
        pltpu.make_async_remote_copy(
            src_ref=src,
            dst_ref=dst,
            send_sem=pair[0],
            recv_sem=pair[1],
            device_id=(ctx, z),
            device_id_type=pl.DeviceIdType.MESH,
        ).start()

    def local(self, src, dst):
        copy = pltpu.make_async_copy(src, dst, self.new())
        copy.start()
        return copy

    def got(self, pair, view):
        pltpu.make_async_copy(view, view, pair[1]).wait()

    def sent(self, pair, view, when=None):
        self.open.append((pair[0], view, when))

    def drain(self):
        for sem, view, when in self.open:
            wait = pltpu.make_async_copy(view, view, sem).wait
            if when is None:
                wait()
            else:
                pl.when(when)(wait)


def at(start, size, step=None):
    return pl.ds(pl.multiple_of(start, step or size), size)


def fused_kernel(p, names, *refs):
    ins, refs = refs[:16], refs[16:]
    lengths, feats_in, lat_in, wq_in, wk_in, wv_in, wo_in, wu_in, wd_in = ins[:9]
    smalls, cot_in = ins[9:15], ins[15]
    outs, refs = refs[:11], refs[11:]
    res_out, byte_out, go, gu, gd, gv, gk, gl, gq_out, glat_out, vec_out = outs
    sems = refs[-1]
    s = types.SimpleNamespace(**dict(zip(names, refs[:-1])))
    cp = Copies(sems)
    ctx, zs = p.ctx, p.zs
    c, z = lax.axis_index("ctx"), lax.axis_index("wshard")
    h, q = lax.rem(c, 2), lax.div(c, 2)
    x, y = lax.rem(q, 2), lax.div(q, 2)
    other = 1 - h
    core = c + 1 - 2 * h
    chips = (c + 2 - 4 * x, c + 4 - 8 * y, c + 6 - 4 * x - 8 * y)
    near = (chips[0] * (1 - h) + chips[1] * h, chips[1] * (1 - h) + chips[0] * h)
    zed = [lax.rem(z + j, zs) for j in range(1, zs)]
    plane = [lax.rem(c + j, ctx) for j in range(1, ctx)]

    barrier = pltpu.get_barrier_semaphore()
    for peer in plane:
        pl.semaphore_signal(barrier, inc=1, device_id=(peer, z), device_id_type=pl.DeviceIdType.MESH)
    for peer in zed:
        pl.semaphore_signal(barrier, inc=1, device_id=(c, peer), device_id_type=pl.DeviceIdType.MESH)
    pl.semaphore_wait(barrier, ctx - 1 + zs - 1)

    load_feats = cp.local(feats_in, s.feats)
    for row, ref in enumerate(smalls):
        s.small_own[row : row + 1, 0 : ref.shape[0]] = ref[...].reshape(1, -1).astype(FULL)
    small_pair = cp.group()
    for peer in zed:
        cp.send(small_pair, s.small_own, s.small.at[z], c, peer)
    cp.sent(small_pair, s.small.at[0 : zs - 1])

    class Weight:
        def __init__(self, ref, source, cuts, line):
            self.ref, self.source, self.cuts, self.line = ref, source, cuts, line
            if line:
                self.up = [cp.group() for _ in range(zs - 1)]
                self.down = [cp.group() for _ in range(zs - 1)]
            self.rows, cols = source.shape
            self.part, self.cols = self.rows // cuts, cols // 2
            self.slot = q if cuts == 4 else lax.rem(x + y, 2)
            self.mine = at(h * self.cols, self.cols)
            self.pairs = [cp.group() for _ in range(4)]

        def view(self, rows):
            return self.ref.at[pl.ds(0, rows), pl.ds(0, self.cols)]

        def block(self, zz, qq):
            return self.ref.at[at(zz * self.rows + qq * self.part, self.part, 16), self.mine]

        def hop(self, i):
            one = self.view(self.part)

            def forward(pair, source, dest, when):
                @pl.when(when)
                def _():
                    cp.send(pair, source, self.block(dest[0], self.slot), c, dest[1])

                cp.sent(pair, one, when)

            if i == 0:
                mine = self.source.at[at(self.slot * self.part, self.part, 16), self.mine]
                forward(self.up[0], mine, (z, z + 1), z < zs - 1)
                forward(self.down[0], mine, (z, z - 1), z > 0)
                self.load = cp.local(self.source, self.ref.at[at(z * self.rows, self.rows, 16), :])
                return

            @pl.when(z >= i)
            def _():
                cp.got(self.up[i - 1], one)

            if i < zs - 1:
                block = self.block(lax.rem(z + zs - i, zs), self.slot)
                forward(self.up[i], block, (lax.rem(z + zs - i, zs), z + 1), (z >= i) & (z < zs - 1))

            @pl.when(z + i < zs)
            def _():
                cp.got(self.down[i - 1], one)

            if i < zs - 1:
                block = self.block(lax.rem(z + i, zs), self.slot)
                forward(self.down[i], block, (lax.rem(z + i, zs), z - 1), (z + i < zs) & (z > 0))

        def start(self):
            for peer in zed:
                cp.send(
                    self.pairs[0],
                    self.source.at[at(self.slot * self.part, self.part, 16), self.mine],
                    self.block(z, self.slot),
                    c,
                    peer,
                )
            cp.sent(self.pairs[0], self.view(3 * self.part))
            self.load = cp.local(self.source, self.ref.at[at(z * self.rows, self.rows, 16), :])

        def first(self):
            if self.line:
                self.hop(zs - 1)
            else:
                cp.got(self.pairs[0], self.view(3 * self.part))
            for zz in zed:
                block = self.block(zz, self.slot)
                cp.send(self.pairs[1], block, block, near[0], z)
            cp.sent(self.pairs[1], self.view(3 * self.part))

        def second(self):
            cp.got(self.pairs[1], self.view(3 * self.part))
            for zz in zed:
                for qq in (q, lax.div(near[0], 2)):
                    block = self.block(zz, qq)
                    cp.send(self.pairs[2], block, block, near[1], z)
            cp.sent(self.pairs[2], self.view(6 * self.part))

        def third(self):
            if self.cuts == 4:
                cp.got(self.pairs[2], self.view(6 * self.part))
            else:
                cp.got(self.pairs[1], self.view(3 * self.part))
            for zz in zed:
                block = self.ref.at[at(zz * self.rows, self.rows, 16), self.mine]
                cp.send(self.pairs[3], block, block, core, z)
            cp.sent(self.pairs[3], self.view(3 * self.rows))

        def ready(self):
            cp.got(self.pairs[3], self.view(3 * self.rows))
            self.load.wait()

    wk, wq, lat = Weight(s.wk, wk_in, 4, False), Weight(s.wq, wq_in, 4, False), Weight(s.lat, lat_in, 4, False)
    wv, wo = Weight(s.wv, wv_in, 4, False), Weight(s.wo, wo_in, 4, True)
    wu, wd = Weight(s.wu, wu_in, 4, True), Weight(s.wd, wd_in, 2, True)
    for weight in (wk, wq, lat, wv):
        weight.start()
    wo.hop(0)
    load_cot = cp.local(cot_in, s.cot)

    cp.got(small_pair, s.small.at[0 : zs - 1])
    s.small[z] = s.small_own[...]
    for row, ref in enumerate(smalls):
        size = ref.shape[0]
        for zz in range(zs):
            s.vec[row : row + 1, zz * size : (zz + 1) * size] = s.small[zz, row : row + 1, 0:size]
    vec = s.vec
    gain_lat, bias_lat = vec[0:1, :], vec[1:2, :]

    half_cols = at(h * (p.dl // 2), p.dl // 2)
    own = at(h * p.lat, p.lat)
    tiles = p.dl // 256
    quarter = p.lat // 4
    own_rows = at(h * p.lat + q * quarter, quarter)
    score_scale = 1.0 / math.sqrt(p.head)
    start_slot = c * p.slots
    lane_stat = lanes(p.lat, 128)
    gain_mlp, bias_mlp = vec[4:5, :], vec[5:6, :]
    qhalf, vhalf = p.qk // 2, p.vd // 2
    zrows = p.din // zs
    vpart = zrows // 4
    order = [*zed, z]

    def window(head):
        low_lane = pl.multiple_of(lax.div(head * p.vhead, 128) * 128, 128)
        return pl.ds(low_lane, 256), head * p.vhead - low_lane

    def mask_of(rows, low_lane):
        lane = lanes(rows, 256)
        return ((lane >= low_lane) & (lane < low_lane + p.vhead)).astype(FULL)

    def normed_bytes():
        load_feats.wait()

        @pl.loop(0, p.rows_in // 64)
        def _(i):
            rows = at(i * 64, 64)
            normed, _ = ln_parts(s.feats[rows, :].astype(FULL))
            s.nin[rows, :] = (normed * vec[2:3, 0 : p.din] + vec[3:4, 0 : p.din]).astype(LOW)

    def turned_bytes():
        @pl.loop(0, p.din // 128)
        def _(i):
            tile = at(i * 128, 128)
            s.nin_t[tile, :] = s.nin[:, tile].T

    def make_keys():
        @pl.loop(0, p.seqs)
        def _(i):
            rows = at(i * p.slots, p.slots)
            low = matmul(s.nin[rows, :], s.wk[...]).astype(LOW)
            s.keys[rows, :] = low
            s.keys_t[:, rows] = low.T

    def normed_latents():
        @pl.loop(0, p.lat // 64, unroll=2)
        def _(i):
            rows = at(i * 64, 64)
            normed, _ = ln_parts(s.lat[rows, :].astype(FULL))
            s.nlat[rows, :] = (normed * gain_lat + bias_lat).astype(LOW)

    def make_queries():
        queries = matmul(s.nlat[...], s.wq[...])
        lane_q = lanes(p.lat, p.qk)
        for head in range(H):
            inside = (lane_q >= head * p.head) & (lane_q < (head + 1) * p.head)
            s.qmask[head * p.lat : (head + 1) * p.lat, :] = jnp.where(inside, queries, 0.0).astype(LOW)

    max_pair = cp.group()

    def make_scores():
        s.stat[...] = jnp.zeros_like(s.stat)
        for seq in range(p.seqs):

            @pl.loop(0, H, unroll=4)
            def _(head):
                raw = matmul_nt(
                    s.qmask[at(head * p.lat, p.lat), :], s.keys[seq * p.slots : (seq + 1) * p.slots, :]
                )
                valid = lanes(p.lat, p.slots) < lengths[seq] - start_slot
                scores = jnp.where(valid, raw * score_scale, -1e30)
                s.scores[at((seq * H + head) * p.lat, p.lat), :] = scores
                top = jnp.max(scores, axis=-1, keepdims=True)
                s.stat[...] = jnp.where(lanes(p.lat, 128) == seq * H + head, top, s.stat[...])

        s.stat_t[...] = s.stat[...].T
        s.max_own[...] = s.stat_t[0 : 2 * H, :]
        for peer in plane:
            cp.send(max_pair, s.max_own, s.max_in.at[c], peer, z)
        cp.sent(max_pair, s.max_in.at[0 : ctx - 1])

    def make_values():
        @pl.loop(0, p.vd // 256, unroll=True)
        def _(i):
            tile = at(i * 256, 256)
            s.values[:, tile] = matmul(s.nin[...], s.wv[:, tile]).astype(LOW)

    def get_max():
        cp.got(max_pair, s.max_in.at[0 : ctx - 1])
        s.max_in[c] = s.max_own[...]
        top = s.max_in[0]
        for i in range(1, ctx):
            top = jnp.maximum(top, s.max_in[i])
        s.max_all[...] = top
        s.stat_t[0 : 2 * H, :] = top
        s.max_t[...] = s.stat_t[...].T
        s.stat[...] = jnp.zeros_like(s.stat)

    def partial(seq):
        s.numer[...] = jnp.zeros_like(s.numer)

        @pl.loop(0, H, unroll=4)
        def _(head):
            i = seq * H + head
            lane = lanes(p.lat, 128)
            top = jnp.sum(jnp.where(lane == i, s.max_t[...], 0.0), axis=-1, keepdims=True)
            weights = jnp.exp(s.scores[at(i * p.lat, p.lat), :] - top)
            total = jnp.sum(weights, axis=-1, keepdims=True)
            s.stat[...] = jnp.where(lane == i, total, s.stat[...])
            cols, low_lane = window(head)
            part = s.values[at(seq * p.slots, p.slots), cols] * mask_of(p.slots, low_lane).astype(LOW)
            s.numer[:, cols] += matmul(weights.astype(LOW), part)

        s.stat_t[...] = s.stat[...].T
        s.sums[seq] = s.stat_t[at(seq * H, H), :]

    pair_pair, sums_pair = cp.group(), cp.group()
    chip_sums_pair = cp.group()
    chip_pairs, att_pairs = [cp.group() for _ in range(2)], [cp.group() for _ in range(2)]
    near_chip = [lax.div(near[0], 2), lax.div(near[1], 2)]

    def partial_other():
        partial(other)
        s.numer_low[...] = s.numer[...].astype(LOW)
        cp.send(sums_pair, s.sums.at[other], s.sums_in, core, z)
        cp.send(pair_pair, s.numer_low, s.numer_in, core, z)
        cp.sent(pair_pair, s.numer_low)
        cp.sent(sums_pair, s.sums_in)

    def partial_own():
        partial(h)

    def chip_numer():
        cp.got(sums_pair, s.sums_in)
        s.chip_sums[...] = s.sums[h] + s.sums_in[...]
        for peer in chips:
            cp.send(chip_sums_pair, s.chip_sums, s.chip_sums_in.at[q], peer, z)
        cp.sent(chip_sums_pair, s.chip_sums_in.at[0:3])
        cp.got(pair_pair, s.numer_in)
        s.chip[...] = (s.numer[...] + s.numer_in[...].astype(FULL)).astype(LOW)
        for slot, qq in enumerate((3 - q, near_chip[0])):
            rows = at(qq * quarter, quarter)
            cp.send(chip_pairs[0], s.chip.at[rows, :], s.chip_in.at[slot], near[0], z)
        cp.sent(chip_pairs[0], s.chip_in.at[0:2])

    def chip_pass():
        cp.got(chip_pairs[0], s.chip_in.at[0:2])
        rows = at(near_chip[1] * quarter, quarter)
        s.chip_in[3] = (s.chip[rows, :].astype(FULL) + s.chip_in[0].astype(FULL)).astype(LOW)
        cp.send(chip_pairs[1], s.chip_in.at[3], s.chip_in.at[2], near[1], z)
        cp.sent(chip_pairs[1], s.chip_in.at[3])

    def turned_weights():
        for seq in range(p.seqs):

            @pl.loop(0, H, unroll=4)
            def _(head):
                i = seq * H + head
                raw = matmul_nt(
                    s.keys[seq * p.slots : (seq + 1) * p.slots, :], s.qmask[at(head * p.lat, p.lat), :]
                )
                slot = lax.broadcasted_iota(jnp.int32, (p.slots, p.lat), 0)
                masked = jnp.where(slot < lengths[seq] - start_slot, raw * score_scale, -1e30)
                s.scores[at(i * p.slots, p.slots), :] = jnp.exp(masked - s.max_all[pl.ds(i, 1), :])

    def make_scale():
        cp.got(chip_sums_pair, s.chip_sums_in.at[0:3])
        s.chip_sums_in[q] = s.chip_sums[...]
        sums = s.chip_sums_in
        inverse = 1.0 / ((sums[0] + sums[1]) + (sums[2] + sums[3]))
        s.stats[h, 0:H, :] = inverse
        s.stat_t[0:H, :] = inverse
        s.stat[...] = s.stat_t[...].T
        s.scale[...] = jnp.zeros_like(s.scale)
        own_quarter = s.stat[at(q * quarter, quarter), :]
        for head in range(H):
            low_lane = head * p.vhead // 128 * 128
            lane = lanes(quarter, 256) + low_lane
            inside = (lane >= head * p.vhead) & (lane < (head + 1) * p.vhead)
            cols = slice(low_lane, low_lane + 256)
            s.scale[:, cols] = jnp.where(inside, own_quarter[:, head : head + 1], s.scale[:, cols])

    def make_att():
        cp.got(chip_pairs[1], s.chip_in.at[2])
        own_numer = s.chip[at(q * quarter, quarter), :].astype(FULL)
        added = own_numer + (s.chip_in[1].astype(FULL) + s.chip_in[2].astype(FULL))
        s.att[own_rows, :] = (added * s.scale[...]).astype(LOW)
        cp.send(att_pairs[0], s.att.at[own_rows, :], s.att.at[own_rows, :], near[0], z)
        cp.sent(att_pairs[0], s.att.at[0:quarter, :])

    def att_pass():
        cp.got(att_pairs[0], s.att.at[0:quarter, :])
        for qq in (q, near_chip[0]):
            rows = at(h * p.lat + qq * quarter, quarter)
            cp.send(att_pairs[1], s.att.at[rows, :], s.att.at[rows, :], near[1], z)
        cp.sent(att_pairs[1], s.att.at[0 : 2 * quarter, :])

    shares = {}

    def share(ref):
        pair = cp.group()
        cp.send(pair, ref.at[own, :], ref.at[own, :], core, z)
        cp.sent(pair, ref.at[0 : p.lat, :])
        shares[id(ref)] = pair

    def shared(ref):
        cp.got(shares.pop(id(ref)), ref.at[0 : p.lat, :])

    def get_att():
        cp.got(att_pairs[1], s.att.at[0 : 2 * quarter, :])
        share(s.att)

    def make_hidden():
        @pl.loop(0, tiles, unroll=True)
        def _(i):
            tile = at(i * 256, 256)
            s.hid[:, tile] = s.lat[:, tile].astype(FULL) + matmul(s.att[own, :], s.wo[:, tile])

    def make_mid():
        @pl.loop(0, p.lat // 64, unroll=2)
        def _(i):
            normed, _ = ln_parts(s.hid[at(i * 64, 64), :])
            s.mid[at(h * p.lat + i * 64, 64), :] = (normed * gain_mlp + bias_mlp).astype(LOW)

        share(s.mid)

    def make_act():
        load_cot.wait()

        @pl.loop(0, tiles, unroll=True)
        def _(i):
            tile = at(i * 256, 256)
            up = matmul(s.mid[own, :], s.wu[:, tile])
            cdf = 0.5 * (1.0 + lax.erf(up * (1.0 / math.sqrt(2.0))))
            density = jnp.exp(-0.5 * up * up) * (1.0 / math.sqrt(2.0 * math.pi))
            s.act[own, tile] = (up * cdf).astype(LOW)
            s.slope[:, tile] = cdf + up * density

        share(s.act)

    class Reduce:
        def __init__(self, left, right, grads, arrive, final, out):
            self.left, self.right, self.out = left, right, out
            self.grads, self.arrive, self.final = grads, arrive, final
            self.part = self.final.shape[0]
            self.rows = self.part * 4
            self.pairs = [cp.group() for _ in range(4)]

        def product(self):
            @pl.loop(0, self.grads.shape[0] // 256, unroll=True)
            def _(i):
                rows = at(i * 256, 256)
                self.grads[rows, :] = matmul_tn(self.left[:, rows], self.right[:, half_cols]).astype(LOW)

        def block(self, zz):
            return self.grads.at[at(zz * self.rows + q * self.part, self.part, 16), :]

        def scatter(self):
            for peer in zed:
                cp.send(self.pairs[0], self.block(peer), self.arrive.at[z], c, peer)
            cp.sent(self.pairs[0], self.arrive.at[0 : zs - 1])

        def add(self):
            cp.got(self.pairs[0], self.arrive.at[0 : zs - 1])
            self.arrive[z] = self.grads[at(z * self.rows + q * self.part, self.part, 16), :]
            total = self.arrive[0].astype(FULL)
            for zz in range(1, zs):
                total = total + self.arrive[zz].astype(FULL)
            self.final[...] = total.astype(LOW)
            here = self.out.at[at(q * self.part, self.part, 16), half_cols]
            cp.send(self.pairs[1], self.final, here, near[0], z)
            cp.sent(self.pairs[1], self.final)
            self.store = cp.local(self.final, here)

        def spread(self):
            cp.got(self.pairs[1], self.final)
            here = self.out.at[at(q * self.part, self.part, 16), half_cols]
            there = self.out.at[at(near_chip[0] * self.part, self.part, 16), half_cols]
            cp.send(self.pairs[2], self.final, here, near[1], z)
            cp.send(self.pairs[2], there, there, near[1], z)
            cp.sent(self.pairs[2], self.arrive.at[0:2])

        def halve(self):
            cp.got(self.pairs[2], self.arrive.at[0:2])
            self.store.wait()
            block = self.out.at[:, half_cols]
            cp.send(self.pairs[3], block, block, core, z)
            cp.sent(self.pairs[3], block)

        def done(self):
            cp.got(self.pairs[3], self.out.at[:, half_cols])

    down = Reduce(s.act, s.cot, s.dwd, s.zd, s.fd, gd)
    upper = Reduce(s.mid, s.dup, s.dwu, s.zu, s.fu, gu)
    outer = Reduce(s.att, s.dhid, s.dwo, s.zo, s.fo, go)
    latents = Reduce(s.att, s.dhid, s.dlat, s.zl, s.fl, gl)
    reduces = (down, upper, outer, latents)

    def down_grads():
        shared(s.act)
        down.product()
        down.scatter()

    def upper_grads():
        shared(s.mid)
        shared(s.dup)
        upper.product()
        upper.scatter()

    def outer_grads():
        shared(s.att)
        shared(s.dhid)
        outer.product()
        outer.scatter()
        s.dlat[...] = (
            s.dhid[0 : p.lat, half_cols].astype(FULL) + s.dhid[p.lat : 2 * p.lat, half_cols].astype(FULL)
        ).astype(LOW)
        latents.scatter()

    def make_dup():
        @pl.loop(0, tiles, unroll=True)
        def _(i):
            tile = at(i * 256, 256)
            dact = matmul_nt(s.cot[own, :], s.wd[tile, :])
            s.dup[own, tile] = (dact * s.slope[:, tile]).astype(LOW)

        share(s.dup)

    def make_dmid():
        @pl.loop(0, tiles, unroll=True)
        def _(i):
            tile = at(i * 256, 256)
            s.dmid[:, tile] = matmul_nt(s.dup[own, :], s.wu[tile, :])

    def make_dhid():
        s.vs[...] = jnp.zeros_like(s.vs)

        @pl.loop(0, p.lat // 64, unroll=2)
        def _(i):
            rows = at(i * 64, 64)
            full_rows = at(h * p.lat + i * 64, 64)
            normed, scale = ln_parts(s.hid[rows, :])
            grad = s.dmid[rows, :]
            s.vs[0:1, :] += columns_sum(grad * normed)
            s.vs[1:2, :] += columns_sum(grad)
            total = s.cot[full_rows, :].astype(FULL) + ln_grad(grad, gain_mlp, normed, scale)
            s.dhid[full_rows, :] = total.astype(LOW)

        share(s.dhid)

    stats_pairs = [cp.group() for _ in range(2)]

    def share_inverse():
        cp.send(stats_pairs[0], s.stats.at[h, 0:H], s.stats.at[h, 0:H], core, z)
        cp.sent(stats_pairs[0], s.stats.at[0, 0:H])

    def make_datt():
        @pl.loop(0, tiles, unroll=True)
        def _(i):
            tile = at(i * 256, 256)
            s.datt[own, tile] = matmul_nt(s.dhid[own, :], s.wo[tile, :]).astype(LOW)

        share(s.datt)

    def make_delta():
        s.stat[...] = jnp.zeros_like(s.stat)

        @pl.loop(0, H, unroll=4)
        def _(head):
            cols, low_lane = window(head)
            product = s.datt[own, cols].astype(FULL) * s.att[own, cols].astype(FULL)
            delta = jnp.sum(product * mask_of(p.lat, low_lane), axis=-1, keepdims=True)
            s.stat[...] = jnp.where(lanes(p.lat, 128) == head, delta, s.stat[...])

        s.stat_t[...] = s.stat[...].T
        s.stats[h, H : 2 * H, :] = s.stat_t[0:H, :]
        cp.send(stats_pairs[1], s.stats.at[h, H : 2 * H], s.stats.at[h, H : 2 * H], core, z)
        cp.sent(stats_pairs[1], s.stats.at[0, 0:H])

    def values_grad(seq):
        latent_rows = at(seq * p.lat, p.lat)
        s.numer[...] = jnp.zeros_like(s.numer)

        @pl.loop(0, H, unroll=4)
        def _(head):
            cols, low_lane = window(head)
            inverse = s.stats[seq, pl.ds(head, 1), :]
            probs = s.scores[at((seq * H + head) * p.slots, p.slots), :] * inverse
            grad = s.datt[latent_rows, cols] * mask_of(p.lat, low_lane).astype(LOW)
            s.numer[:, cols] += matmul(probs.astype(LOW), grad)

        s.dvalues[at(seq * p.slots, p.slots), :] = s.numer[...].astype(LOW)

    def scores_grad(seq):
        slots = at(seq * p.slots, p.slots)
        latent_rows = at(seq * p.lat, p.lat)
        s.dk_sum[...] = jnp.zeros_like(s.dk_sum)

        @pl.loop(0, H, unroll=4)
        def _(head):
            heads = at(head * p.lat, p.lat)
            cols, low_lane = window(head)
            inverse = s.stats[seq, pl.ds(head, 1), :]
            delta = s.stats[seq, pl.ds(H + head, 1), :]
            probs = s.scores[at((seq * H + head) * p.slots, p.slots), :] * inverse
            grad = s.datt[latent_rows, cols] * mask_of(p.lat, low_lane).astype(LOW)
            dprobs = matmul_nt(s.values[slots, cols], grad)
            dscores = (probs * (dprobs - delta)).astype(LOW)
            s.dk_sum[...] += matmul(dscores, s.qmask[heads, :])
            block = at(head * p.head, p.head)
            s.dq_t[block, :] += matmul(s.keys_t[block, slots], dscores)

        s.dkeys[slots, :] = (s.dk_sum[...] * score_scale).astype(LOW)

    def weight_grads(ref, grad, width, side):
        cols = at(side * width, width)

        @pl.loop(0, p.din // 256, unroll=True)
        def _(i):
            rows = at(i * 256, 256)
            ref[side, rows, :] = matmul(s.nin_t[rows, :], grad[:, cols]).astype(LOW)

    class Local:
        def __init__(self, grads, arrive, chip, plane_in, plane, z_in, final, out):
            self.grads, self.arrive, self.chip, self.plane_in = grads, arrive, chip, plane_in
            self.plane, self.z_in, self.final, self.out = plane, z_in, final, out
            self.width = final.shape[1]
            self.pairs = [cp.group() for _ in range(5)]
            self.firsts = [cp.group() for _ in range(zs // 2)]
            self.seconds = [cp.group() for _ in range(zs // 2)]
            self.mine = at(h * self.width, self.width)

        def pair(self):
            cp.send(self.pairs[0], self.grads.at[other], self.arrive, core, z)
            cp.sent(self.pairs[0], self.arrive)

        def rows(self, qq):
            return at(qq * vpart, vpart, 16)

        def chunk(self, i):
            for zz in order[2 * i : 2 * i + 2]:
                rows = at(zz * zrows, zrows)
                total = self.grads[h, rows, :].astype(FULL) + self.arrive[rows, :].astype(FULL)
                self.chip[zz] = total.astype(LOW)
                for slot, qq in enumerate((3 - q, near_chip[0])):
                    cp.send(
                        self.firsts[i],
                        self.chip.at[zz, self.rows(qq), :],
                        self.plane_in.at[slot, zz],
                        near[0],
                        z,
                    )
            cp.sent(self.firsts[i], self.plane_in.at[0])

        def middle(self, i):
            cp.got(self.firsts[i], self.plane_in.at[0])
            for zz in order[2 * i : 2 * i + 2]:
                mine = self.chip[zz, self.rows(near_chip[1]), :].astype(FULL)
                self.plane_in[3, zz] = (mine + self.plane_in[0, zz].astype(FULL)).astype(LOW)
                cp.send(self.seconds[i], self.plane_in.at[3, zz], self.plane_in.at[2, zz], near[1], z)
            cp.sent(self.seconds[i], self.plane_in.at[0, 0:2])

        def add(self, i):
            cp.got(self.seconds[i], self.plane_in.at[0, 0:2])
            for zz in order[2 * i : 2 * i + 2]:
                mine = self.chip[zz, self.rows(q), :].astype(FULL)
                parts = self.plane_in[1, zz].astype(FULL) + self.plane_in[2, zz].astype(FULL)
                self.plane[zz] = (mine + parts).astype(LOW)
                if zz is not order[-1]:
                    cp.send(self.pairs[1], self.plane.at[zz], self.z_in.at[z], c, zz)
            if i == zs // 2 - 1:
                cp.sent(self.pairs[1], self.z_in.at[0 : zs - 1])

        def finish(self):
            cp.got(self.pairs[1], self.z_in.at[0 : zs - 1])
            self.z_in[z] = self.plane[z]
            total = self.z_in[0].astype(FULL)
            for zz in range(1, zs):
                total = total + self.z_in[zz].astype(FULL)
            self.final[...] = total.astype(LOW)
            here = self.out.at[self.rows(q), self.mine]
            cp.send(self.pairs[2], self.final, here, near[0], z)
            cp.sent(self.pairs[2], self.final)
            self.store = cp.local(self.final, here)

        def spread(self):
            cp.got(self.pairs[2], self.final)
            here = self.out.at[self.rows(q), self.mine]
            there = self.out.at[self.rows(near_chip[0]), self.mine]
            cp.send(self.pairs[3], self.final, here, near[1], z)
            cp.send(self.pairs[3], there, there, near[1], z)
            cp.sent(self.pairs[3], self.z_in.at[0:2])

        def halve(self):
            cp.got(self.pairs[3], self.z_in.at[0:2])
            self.store.wait()
            block = self.out.at[:, self.mine]
            cp.send(self.pairs[4], block, block, core, z)
            cp.sent(self.pairs[4], block)

        def done(self):
            cp.got(self.pairs[4], self.out.at[:, self.mine])

    key_grads = Local(s.swk, s.rwk, s.cwk, s.pwk_in, s.pwk, s.zwk_in, s.fwk, gk)
    value_grads = Local(s.swv, s.rwv, s.cwv, s.pwv_in, s.pwv, s.zwv_in, s.fwv, gv)
    def byte_matmul(seq):
        rows = at(seq * p.slots, p.slots)
        for tile in range(p.din // 256):
            cols = slice(tile * 256, (tile + 1) * 256)
            grad = matmul_nt(s.dkeys[rows, :], s.wk[cols, :]) + matmul_nt(s.dvalues[rows, :], s.wv[cols, :])
            s.scores[at(tile * p.rows_in + seq * p.slots, p.slots), :] = grad

    def byte_part(part):
        byte_matmul(part)

        @pl.loop(part * p.slots // 64, (part + 1) * p.slots // 64, unroll=2)
        def _(i):
            rows = at(i * 64, 64)
            tiles_in = [s.scores[at(k * p.rows_in + i * 64, 64), :] for k in range(p.din // 256)]
            grad = jnp.concatenate(tiles_in, axis=1)
            normed, scale = ln_parts(s.feats[rows, :].astype(FULL))
            s.vs[2:3, 0 : p.din] += columns_sum(grad * normed)
            s.vs[3:4, 0 : p.din] += columns_sum(grad)
            s.bgrad[rows, :] = ln_grad(grad, vec[2:3, 0 : p.din], normed, scale).astype(LOW)

    kv = (value_grads, key_grads)
    dq_pairs = [cp.group() for _ in range(5)]
    vs_pairs = [cp.group() for _ in range(3)]
    res_pair = cp.group()
    stores = []
    own_half = at(h * qhalf, qhalf)

    def values_own():
        values_grad(h)

    def values_other():
        cp.got(stats_pairs[0], s.stats.at[0, 0:H])
        shared(s.datt)
        values_grad(other)

    def value_weights():
        weight_grads(s.swv, s.dvalues, vhalf, other)
        value_grads.pair()

    def value_weights_own():
        weight_grads(s.swv, s.dvalues, vhalf, h)

    def value_chunks():
        cp.got(value_grads.pairs[0], value_grads.arrive)
        for i in range(zs // 2):
            value_grads.chunk(i)

    def scores_own():
        s.dq_t[...] = jnp.zeros_like(s.dq_t)
        scores_grad(h)

    def scores_other():
        cp.got(stats_pairs[1], s.stats.at[0, 0:H])
        scores_grad(other)
        s.dq[...] = (s.dq_t[...] * score_scale).T.astype(LOW)
        cp.send(dq_pairs[0], s.dq.at[:, at(other * qhalf, qhalf)], s.dq_in1, core, z)
        cp.sent(dq_pairs[0], s.dq_in1)

    def key_weights():
        weight_grads(s.swk, s.dkeys, qhalf, other)
        key_grads.pair()
        weight_grads(s.swk, s.dkeys, qhalf, h)

    def dq_chip():
        cp.got(dq_pairs[0], s.dq_in1)
        s.dq_chip[...] = (s.dq[:, own_half].astype(FULL) + s.dq_in1[...].astype(FULL)).astype(LOW)
        cp.send(dq_pairs[1], s.dq_chip, s.dq_in2.at[0], near[0], z)
        cp.sent(dq_pairs[1], s.dq_chip)

    def dq_pass():
        cp.got(dq_pairs[1], s.dq_chip)
        s.dq_in2[2] = (s.dq_chip[...].astype(FULL) + s.dq_in2[0].astype(FULL)).astype(LOW)
        cp.send(dq_pairs[4], s.dq_in2.at[2], s.dq_in2.at[1], near[1], z)
        cp.sent(dq_pairs[4], s.dq_chip)

    def key_chunks():
        cp.got(key_grads.pairs[0], key_grads.arrive)
        for i in range(zs // 2):
            key_grads.chunk(i)

    def byte_store():
        stores.append(cp.local(s.bgrad, byte_out))
        cp.send(vs_pairs[0], s.vs, s.vs_in1, core, z)
        cp.sent(vs_pairs[0], s.vs)

    def dq_plane():
        cp.got(dq_pairs[4], s.dq_chip)
        s.dq_plane[...] = (s.dq_in2[1].astype(FULL) + s.dq_in2[2].astype(FULL)).astype(LOW)
        for peer in zed:
            cp.send(dq_pairs[2], s.dq_plane, s.dq_in3.at[z], c, peer)
        cp.sent(dq_pairs[2], s.dq_in3.at[0 : zs - 1])

    def vs_chip():
        cp.got(vs_pairs[0], s.vs_in1)
        s.vs_chip[...] = s.vs[...] + s.vs_in1[...]
        for peer in chips:
            cp.send(vs_pairs[1], s.vs_chip, s.vs_in2.at[q], peer, z)
        cp.sent(vs_pairs[1], s.vs_in2.at[0:3])

    def make_result():
        @pl.loop(0, tiles, unroll=True)
        def _(i):
            tile = at(i * 256, 256)
            s.res[:, tile] = (s.hid[:, tile] + matmul(s.act[own, :], s.wd[:, tile])).astype(LOW)

        cp.send(res_pair, s.res, res_out.at[own, :], core, z)
        cp.sent(res_pair, s.res)
        stores.append(cp.local(s.res, res_out.at[own, :]))

    def vs_plane():
        cp.got(vs_pairs[1], s.vs_in2.at[0:3])
        s.vs_in2[q] = s.vs_chip[...]
        parts = s.vs_in2
        total = (parts[0] + parts[1]) + (parts[2] + parts[3])
        row_ids = lax.broadcasted_iota(jnp.int32, (8, p.dl), 0)
        s.vs_plane[...] = jnp.where(row_ids < 2, s.vs_chip[...], total)
        for peer in zed:
            cp.send(vs_pairs[2], s.vs_plane, s.vs_in3.at[z], c, peer)
        cp.sent(vs_pairs[2], s.vs_in3.at[0 : zs - 1])

    def dq_total():
        cp.got(dq_pairs[2], s.dq_in3.at[0 : zs - 1])
        s.dq_in3[z] = s.dq_plane[...]
        parts = s.dq_in3
        total = parts[0].astype(FULL)
        for zz in range(1, zs):
            total = total + parts[zz].astype(FULL)
        s.dq_all[:, own_half] = total.astype(LOW)
        cp.send(dq_pairs[3], s.dq_all.at[:, own_half], s.dq_all.at[:, own_half], core, z)
        cp.sent(dq_pairs[3], s.dq_in1)

    def query_grads():
        cp.got(dq_pairs[3], s.dq_in1)

        @pl.loop(0, tiles, unroll=True)
        def _(i):
            tile = at(i * 256, 256)
            s.gq[tile, :] = matmul_tn(s.nlat[:, tile], s.dq_all[...])
            s.dmid[:, tile] = matmul_nt(s.dq_all[...], s.wq[tile, :])

        stores.append(cp.local(s.gq.at[at(z * (p.dl // zs), p.dl // zs, 16), :], gq_out))

    def latent_grads():
        cp.got(vs_pairs[2], s.vs_in3.at[0 : zs - 1])
        s.vs_in3[z] = s.vs_plane[...]
        total = s.vs_in3[0]
        for zz in range(1, zs):
            total = total + s.vs_in3[zz]
        s.vs_all[...] = total
        s.vs_all[4:6, :] = jnp.zeros((2, p.dl), FULL)

        @pl.loop(0, p.lat // 64, unroll=2)
        def _(i):
            rows = at(i * 64, 64)
            normed, scale = ln_parts(s.lat[rows, :].astype(FULL))
            grad = s.dmid[rows, :]
            s.vs_all[4:5, :] += columns_sum(grad * normed)
            s.vs_all[5:6, :] += columns_sum(grad)
            s.slope[rows, :] = ln_grad(grad, gain_lat, normed, scale)

        stores.append(cp.local(s.slope.at[at(z * (p.lat // zs), p.lat // zs, 16), :], glat_out))
        stores.append(cp.local(s.vs_all, vec_out))

    wq.first()
    wk.first()
    normed_bytes()
    lat.first()
    lat.second()
    turned_bytes()
    wk.second()
    wq.second()
    wk.third()
    wq.third()
    wk.ready()
    wv.first()
    wo.hop(1)
    make_keys()
    wq.ready()
    lat.third()
    wu.hop(0)
    lat.ready()
    normed_latents()
    make_queries()
    wo.hop(2)
    wv.second()
    make_scores()
    wd.hop(0)
    wo.first()
    wv.third()
    get_max()
    wu.hop(1)
    wv.ready()
    make_values()
    wo.second()
    wu.hop(2)
    partial_other()
    partial_own()
    chip_numer()
    wd.hop(1)
    wu.first()
    wo.third()
    turned_weights()
    chip_pass()
    wu.second()
    wd.hop(2)
    make_scale()
    make_att()
    att_pass()
    wu.third()
    share_inverse()
    wo.ready()
    wd.first()
    get_att()
    make_hidden()
    make_mid()
    wu.ready()
    make_act()
    wd.third()
    down_grads()
    wd.ready()
    make_dup()
    make_dmid()
    make_dhid()
    make_datt()
    make_delta()
    values_own()
    values_other()
    value_weights()
    down.add()
    upper_grads()
    value_weights_own()
    value_chunks()
    scores_own()
    scores_other()
    value_grads.middle(0)
    value_grads.middle(1)
    dq_chip()
    key_weights()
    value_grads.add(0)
    down.spread()
    value_grads.add(1)
    key_chunks()
    outer_grads()
    down.halve()
    key_grads.middle(0)
    dq_pass()
    upper.add()
    key_grads.middle(1)
    byte_part(0)
    byte_part(1)
    byte_store()
    key_grads.add(0)
    key_grads.add(1)
    dq_plane()
    upper.spread()
    value_grads.finish()
    value_grads.spread()
    make_result()
    vs_chip()
    outer.add()
    upper.halve()
    key_grads.finish()
    value_grads.halve()
    latents.add()
    vs_plane()
    outer.spread()
    key_grads.spread()
    dq_total()
    latents.spread()
    query_grads()
    key_grads.halve()
    outer.halve()
    latents.halve()
    latent_grads()
    for part in (*reduces, *kv):
        part.done()
    cp.got(res_pair, s.res)
    for store in stores:
        store.wait()
    cp.drain()


def finish_kernel(p, res, byte, go, gu, gd, gv, gk, gl, gq, glat, vec, *outs):
    z = lax.axis_index("wshard")
    outs[0][...] = res[...]
    outs[1][...] = byte[...]
    outs[2][...] = glat[...] + gl[...].astype(FULL)
    for out, row in ((3, 4), (4, 5), (5, 2), (6, 3), (11, 0), (12, 1)):
        size = outs[out].shape[0]
        picked = vec[row : row + 1, 0:size]
        for zz in range(1, p.zs):
            picked = jnp.where(z == zz, vec[row : row + 1, zz * size : (zz + 1) * size], picked)
        outs[out][...] = picked.reshape(size)
    outs[7][...] = gq[...]
    for out, source in ((8, gk), (9, gv), (10, go), (13, gu), (14, gd)):
        outs[out][...] = source[...].astype(FULL)


def fused(*args):
    (byte_feats, lengths, latent, *smalls, cot) = (args[0], args[1], args[2], *args[3:7], args[11], args[12], args[15])
    w_query, w_key, w_value, w_output = args[7:11]
    w_up, w_down = args[13:15]
    seqs, slots, din = byte_feats.shape
    ctx, zs = lax.axis_size("ctx"), lax.axis_size("wshard")
    feats = byte_feats.reshape(seqs * slots, din)
    cot_flat = cot.reshape(-1, cot.shape[-1])
    p = Plan(ctx, zs, feats, latent, w_query, w_key, w_value, w_output, cot_flat)
    table = scratch_table(p)
    anywhere = pl.BlockSpec(memory_space=pl.ANY)
    in_vmem = pl.BlockSpec(memory_space=pltpu.VMEM)
    struct = jax.ShapeDtypeStruct
    made = pl.pallas_call(
        functools.partial(fused_kernel, p, tuple(table)),
        out_shape=(
            struct(cot_flat.shape, LOW),
            struct(feats.shape, LOW),
            struct(w_output.shape, LOW),
            struct(w_up.shape, LOW),
            struct(w_down.shape, LOW),
            struct(w_value.shape, LOW),
            struct(w_key.shape, LOW),
            struct(latent.shape, LOW),
            struct(w_query.shape, FULL),
            struct(latent.shape, FULL),
            struct((8, p.dl), FULL),
        ),
        in_specs=[pl.BlockSpec(memory_space=pltpu.SMEM)] + [anywhere] * 8 + [in_vmem] * 6 + [anywhere],
        out_specs=(anywhere,) * 11,
        scratch_shapes=[pltpu.VMEM(shape, kind) for shape, kind in table.values()]
        + [pltpu.SemaphoreType.DMA((SEMS,))],
        compiler_params=pltpu.CompilerParams(
            collective_id=0, has_side_effects=True, vmem_limit_bytes=67043328
        ),
        name="block",
    )(lengths, feats, latent, w_query, w_key, w_value, w_output, w_up, w_down, *smalls, cot_flat)
    shapes = (
        (cot_flat.shape, LOW),
        (feats.shape, LOW),
        (latent.shape, FULL),
        *((smalls[i].shape, FULL) for i in range(4)),
        *((w.shape, FULL) for w in (w_query, w_key, w_value, w_output)),
        *((smalls[i].shape, FULL) for i in (4, 5)),
        *((w.shape, FULL) for w in (w_up, w_down)),
    )
    outs = pl.pallas_call(
        functools.partial(finish_kernel, p),
        out_shape=tuple(struct(shape, kind) for shape, kind in shapes),
        in_specs=[in_vmem] * 11,
        out_specs=(in_vmem,) * 15,
        compiler_params=pltpu.CompilerParams(vmem_limit_bytes=60 * 2**20),
        name="finish",
    )(*made)
    return (outs[0].reshape(cot.shape), outs[1].reshape(byte_feats.shape), *outs[2:])


def shards(*args):
    if lax.axis_size("ctx") == 8 and lax.axis_size("wshard") == 4 and args[0].shape[0] == 2:
        return fused(*args)
    return plain(*args)


def solution(mesh):
    sharded, plain = P("wshard", None), P("wshard")
    return jax.shard_map(
        shards,
        mesh=mesh,
        in_specs=(
            P("wshard", "ctx", None),
            plain,
            sharded,
            plain,
            plain,
            plain,
            plain,
            sharded,
            sharded,
            sharded,
            sharded,
            plain,
            plain,
            sharded,
            sharded,
            P("wshard", None, None),
        ),
        out_specs=(
            P("wshard", None, None),
            P("wshard", "ctx", None),
            sharded,
            plain,
            plain,
            plain,
            plain,
            sharded,
            sharded,
            sharded,
            sharded,
            plain,
            plain,
            sharded,
            sharded,
        ),
        check_vma=False,
    )
```

```python
import functools
import math
import types

import jax
import jax.numpy as jnp
from jax import lax
from jax.experimental import pallas as pl
from jax.experimental.pallas import tpu as pltpu
from jax.sharding import PartitionSpec as P

H = 8
LOW = jnp.bfloat16
FULL = jnp.float32


def layer_norm(values, gain, offset):
    center = jnp.mean(values, axis=-1, keepdims=True)
    centred = values - center
    variance = jnp.mean(centred * centred, axis=-1, keepdims=True)
    return centred * lax.rsqrt(variance + 1e-05) * gain + offset


def exact_gelu(values):
    return jax.nn.gelu(values, approximate=False)


def matmul(left, right):
    return jnp.dot(left, right, preferred_element_type=FULL)


def matmul_tn(left, right):
    return lax.dot_general(left, right, (((0,), (0,)), ((), ())), preferred_element_type=FULL)


def matmul_nt(left, right):
    return lax.dot_general(left, right, (((1,), (1,)), ((), ())), preferred_element_type=FULL)


def gather(shard):
    return lax.all_gather(shard, "wshard", axis=0, tiled=True)


def scatter(total):
    return lax.psum_scatter(
        total.astype(LOW), "wshard", scatter_dimension=0, tiled=True
    ).astype(FULL)


SEMS = 256


def own_part(total, shard):
    size = shard.shape[0]
    return lax.dynamic_slice_in_dim(total, lax.axis_index("wshard") * size, size, 0)


def plain(
    byte_feats,
    lengths,
    latent_array,
    lat_gain,
    lat_bias,
    in_gain,
    in_bias,
    w_query,
    w_key,
    w_value,
    w_output,
    mlp_gain,
    mlp_bias,
    w_up,
    w_down,
    cotangent,
):
    seqs, slots, width = byte_feats.shape
    gain_in, bias_in = gather(in_gain).astype(FULL), gather(in_bias).astype(FULL)
    key_w, value_w = gather(w_key), gather(w_value)
    latent = gather(latent_array).astype(FULL)
    gain_lat, bias_lat = gather(lat_gain).astype(FULL), gather(lat_bias).astype(FULL)
    query_w = gather(w_query)
    gain_mlp, bias_mlp = gather(mlp_gain).astype(FULL), gather(mlp_bias).astype(FULL)
    output_w, up_w, down_w = gather(w_output), gather(w_up), gather(w_down)

    features = byte_feats.reshape(seqs * slots, width).astype(FULL)
    normed_in, in_back = jax.vjp(layer_norm, features, gain_in, bias_in)
    input_low = normed_in.astype(LOW)
    keys = matmul(input_low, key_w).astype(LOW)
    values = matmul(input_low, value_w).astype(LOW)
    normed_lat, lat_back = jax.vjp(layer_norm, latent, gain_lat, bias_lat)
    lat_low = normed_lat.astype(LOW)
    rows = lat_low.shape[0]
    queries = matmul(lat_low, query_w).astype(LOW)
    score_scale = 1.0 / math.sqrt(queries.shape[1] // H)
    qheads = queries.reshape(rows, H, -1)
    kheads = keys.reshape(seqs, slots, H, -1)
    vheads = values.reshape(seqs, slots, H, -1)

    scores = jnp.einsum("lhd,mkhd->mhlk", qheads, kheads, preferred_element_type=FULL) * score_scale
    slot_ids = lax.axis_index("ctx") * slots + lax.iota(jnp.int32, slots)
    valid = (slot_ids[None, :] < lengths[:, None])[:, None, None, :]
    scores = jnp.where(valid, scores, -1e30)
    highest = lax.pmax(jnp.max(scores, axis=-1), "ctx")
    weights = jnp.where(valid, jnp.exp(scores - highest[..., None]), 0.0)
    total = lax.psum(jnp.sum(weights, axis=-1), "ctx")
    numer = jnp.einsum("mhlk,mkhe->mlhe", weights.astype(LOW), vheads, preferred_element_type=FULL)
    numer = lax.psum(numer.astype(LOW), "ctx").astype(FULL)
    attended = numer / jnp.transpose(total, (0, 2, 1))[..., None]
    attended = attended.reshape(seqs * rows, -1)

    att_low = attended.astype(LOW)
    hidden = jnp.tile(latent, (seqs, 1)) + matmul(att_low, output_w)
    normed_mid, mid_back = jax.vjp(layer_norm, hidden, gain_mlp, bias_mlp)
    mid_low = normed_mid.astype(LOW)
    upward = matmul(mid_low, up_w)
    activated, gelu_back = jax.vjp(exact_gelu, upward)
    act_low = activated.astype(LOW)
    result = hidden + matmul(act_low, down_w)
    dout_low = cotangent.reshape(seqs * rows, -1)
    grad_down = scatter(matmul_tn(act_low, dout_low))
    (grad_upward,) = gelu_back(matmul_nt(dout_low, down_w))
    up_low = grad_upward.astype(LOW)
    grad_up = scatter(matmul_tn(mid_low, up_low))
    dhid_norm, grad_gmlp, grad_bmlp = mid_back(matmul_nt(up_low, up_w))
    dhidden = dout_low.astype(FULL) + dhid_norm
    dhid_low = dhidden.astype(LOW)
    grad_output = scatter(matmul_tn(att_low, dhid_low))
    grad_hidden = scatter(jnp.sum(dhidden.reshape(seqs, rows, -1), axis=0))
    grad_att = matmul_nt(dhid_low, output_w).astype(LOW)

    grad_heads = grad_att.reshape(seqs, rows, H, -1)
    delta = jnp.sum(
        grad_heads.astype(FULL) * attended.reshape(seqs, rows, H, -1), axis=-1
    ).transpose(0, 2, 1)
    probs = weights / total[..., None]
    dprobs = jnp.einsum("mlhe,mkhe->mhlk", grad_heads, vheads, preferred_element_type=FULL)
    dscores = (probs * (dprobs - delta[..., None])).astype(LOW)
    dquery = jnp.einsum("mhlk,mkhd->lhd", dscores, kheads, preferred_element_type=FULL) * score_scale
    dkeys = jnp.einsum("mhlk,lhd->mkhd", dscores, qheads, preferred_element_type=FULL) * score_scale
    dvalues = jnp.einsum("mhlk,mlhe->mkhe", probs.astype(LOW), grad_heads, preferred_element_type=FULL)
    dkeys = dkeys.astype(LOW).reshape(seqs * slots, -1)
    dvalues = dvalues.astype(LOW).reshape(seqs * slots, -1)

    dquery = lax.psum(dquery.reshape(rows, -1).astype(LOW), ("ctx", "wshard"))
    grad_query = matmul_tn(
        lax.dynamic_slice_in_dim(
            lat_low, lax.axis_index("wshard") * w_query.shape[0], w_query.shape[0], 1
        ),
        dquery,
    )
    dlat_norm, grad_glat, grad_blat = lat_back(matmul_nt(dquery, query_w))
    grad_latent = grad_hidden + own_part(dlat_norm, latent_array)

    dnorm_in = matmul_nt(dkeys, key_w) + matmul_nt(dvalues, value_w)
    dfeatures, grad_gin, grad_bin = in_back(dnorm_in)
    grad_key = lax.psum(scatter(matmul_tn(input_low, dkeys)).astype(LOW), "ctx").astype(FULL)
    grad_value = lax.psum(scatter(matmul_tn(input_low, dvalues)).astype(LOW), "ctx").astype(FULL)
    in_sums = lax.psum(jnp.concatenate([grad_gin, grad_bin]), ("ctx", "wshard"))
    grad_gin, grad_bin = jnp.split(in_sums, 2)
    mlp_sums = lax.psum(jnp.concatenate([grad_gmlp, grad_bmlp]), "wshard")
    grad_gmlp, grad_bmlp = jnp.split(mlp_sums, 2)
    return (
        result.astype(LOW).reshape(seqs, rows, -1),
        dfeatures.astype(LOW).reshape(seqs, slots, width),
        grad_latent,
        own_part(grad_glat, lat_gain),
        own_part(grad_blat, lat_bias),
        own_part(grad_gin, in_gain),
        own_part(grad_bin, in_bias),
        grad_query,
        grad_key,
        grad_value,
        grad_output,
        own_part(grad_gmlp, mlp_gain),
        own_part(grad_bmlp, mlp_bias),
        grad_up,
        grad_down,
    )


def ln_parts(values):
    centred = values - jnp.mean(values, axis=-1, keepdims=True)
    scale = lax.rsqrt(jnp.mean(centred * centred, axis=-1, keepdims=True) + 1e-05)
    return centred * scale, scale


def ln_grad(cotangent, gain, normed, scale):
    scaled = cotangent * gain
    first = jnp.mean(scaled, axis=-1, keepdims=True)
    second = jnp.mean(scaled * normed, axis=-1, keepdims=True)
    return scale * (scaled - first - normed * second)


def lanes(rows, columns):
    return lax.broadcasted_iota(jnp.int32, (rows, columns), 1)


def columns_sum(values):
    return jnp.sum(values, axis=0, keepdims=True)


class Plan:
    def __init__(self, ctx, zs, feats, latent, w_query, w_key, w_value, w_output, cot):
        self.ctx, self.zs = ctx, zs
        self.rows_in, self.din = feats.shape
        self.lat = latent.shape[0] * zs
        self.dl = latent.shape[1]
        self.qk, self.vd = w_key.shape[1], w_value.shape[1]
        self.seqs = cot.shape[0] // self.lat
        self.slots = self.rows_in // self.seqs
        self.head, self.vhead = self.qk // H, self.vd // H


def scratch_table(p):
    both = p.seqs * p.lat
    half = p.dl // 2
    part = p.dl // p.zs // 4
    vpart = p.din // p.zs // 4
    return dict(
        wk=((p.din, p.qk), LOW),
        wq=((p.dl, p.qk), LOW),
        lat=((p.lat, p.dl), LOW),
        wv=((p.din, p.vd), LOW),
        wo=((p.vd, p.dl), LOW),
        wu=((p.dl, p.dl), LOW),
        wd=((p.dl, p.dl), LOW),
        small_own=((8, 384), FULL),
        small=((p.zs, 8, 384), FULL),
        vec=((8, p.dl), FULL),
        feats=((p.rows_in, p.din), LOW),
        nin=((p.rows_in, p.din), LOW),
        nin_t=((p.din, p.rows_in), LOW),
        keys=((p.rows_in, p.qk), LOW),
        keys_t=((p.qk, p.rows_in), LOW),
        values=((p.rows_in, p.vd), LOW),
        nlat=((p.lat, p.dl), LOW),
        qmask=((H * p.lat, p.qk), LOW),
        scores=((p.seqs * H * max(p.lat, p.slots), max(p.lat, p.slots)), FULL),
        stat=((p.lat, 128), FULL),
        stat_t=((128, p.lat), FULL),
        max_t=((p.lat, 128), FULL),
        max_own=((2 * H, p.lat), FULL),
        max_in=((p.ctx, 2 * H, p.lat), FULL),
        max_all=((2 * H, p.lat), FULL),
        numer=((p.lat, p.vd), FULL),
        numer_low=((p.lat, p.vd), LOW),
        numer_in=((p.lat, p.vd), LOW),
        sums=((2, H, p.lat), FULL),
        sums_in=((H, p.lat), FULL),
        chip=((p.lat, p.vd), LOW),
        chip_in=((4, p.lat // 4, p.vd), LOW),
        chip_sums=((H, p.lat), FULL),
        chip_sums_in=((4, H, p.lat), FULL),
        scale=((p.lat // 4, p.vd), FULL),
        att=((both, p.vd), LOW),
        mid=((both, p.dl), LOW),
        act=((both, p.dl), LOW),
        dup=((both, p.dl), LOW),
        dhid=((both, p.dl), LOW),
        datt=((both, p.vd), LOW),
        cot=((both, p.dl), LOW),
        hid=((p.lat, p.dl), FULL),
        slope=((p.lat, p.dl), FULL),
        dmid=((p.lat, p.dl), FULL),
        res=((p.lat, p.dl), LOW),
        stats=((2, 2 * H, p.lat), FULL),
        dwo=((p.vd, half), LOW),
        dwu=((p.dl, half), LOW),
        dwd=((p.dl, half), LOW),
        dlat=((p.lat, half), LOW),
        zo=((p.zs, part, half), LOW),
        zu=((p.zs, part, half), LOW),
        zd=((p.zs, part, half), LOW),
        zl=((p.zs, p.lat // p.zs // 4, half), LOW),
        fo=((part, half), LOW),
        fu=((part, half), LOW),
        fd=((part, half), LOW),
        fl=((p.lat // p.zs // 4, half), LOW),
        dkeys=((p.rows_in, p.qk), LOW),
        dvalues=((p.rows_in, p.vd), LOW),
        dk_sum=((p.slots, p.qk), FULL),
        dq_t=((p.qk, p.lat), FULL),
        dq=((p.lat, p.qk), LOW),
        dq_in1=((p.lat, p.qk // 2), LOW),
        dq_chip=((p.lat, p.qk // 2), LOW),
        dq_in2=((4, p.lat, p.qk // 2), LOW),
        dq_plane=((p.lat, p.qk // 2), LOW),
        dq_in3=((p.zs, p.lat, p.qk // 2), LOW),
        dq_all=((p.lat, p.qk), LOW),
        bgrad=((p.rows_in, p.din), LOW),
        swk=((2, p.din, p.qk // 2), LOW),
        swv=((2, p.din, p.vd // 2), LOW),
        rwk=((p.din, p.qk // 2), LOW),
        rwv=((p.din, p.vd // 2), LOW),
        cwk=((p.zs, p.din // p.zs, p.qk // 2), LOW),
        cwv=((p.zs, p.din // p.zs, p.vd // 2), LOW),
        pwk_in=((4, p.zs, vpart, p.qk // 2), LOW),
        pwv_in=((4, p.zs, vpart, p.vd // 2), LOW),
        pwk=((p.zs, vpart, p.qk // 2), LOW),
        pwv=((p.zs, vpart, p.vd // 2), LOW),
        zwk_in=((p.zs, vpart, p.qk // 2), LOW),
        zwv_in=((p.zs, vpart, p.vd // 2), LOW),
        fwk=((vpart, p.qk // 2), LOW),
        fwv=((vpart, p.vd // 2), LOW),
        vs=((8, p.dl), FULL),
        vs_in1=((8, p.dl), FULL),
        vs_chip=((8, p.dl), FULL),
        vs_in2=((4, 8, p.dl), FULL),
        vs_plane=((8, p.dl), FULL),
        vs_in3=((p.zs, 8, p.dl), FULL),
        vs_all=((8, p.dl), FULL),
        gq=((p.dl, p.qk), FULL),
    )


class Copies:
    def __init__(self, sems):
        self.sems, self.used, self.open = sems, 0, []

    def new(self):
        self.used += 1
        return self.sems.at[self.used - 1]

    def group(self):
        return (self.new(), self.new())

    def send(self, pair, src, dst, ctx, z):
        pltpu.make_async_remote_copy(
            src_ref=src,
            dst_ref=dst,
            send_sem=pair[0],
            recv_sem=pair[1],
            device_id=(ctx, z),
            device_id_type=pl.DeviceIdType.MESH,
        ).start()

    def local(self, src, dst):
        copy = pltpu.make_async_copy(src, dst, self.new())
        copy.start()
        return copy

    def got(self, pair, view):
        pltpu.make_async_copy(view, view, pair[1]).wait()

    def sent(self, pair, view, when=None):
        self.open.append((pair[0], view, when))

    def drain(self):
        for sem, view, when in self.open:
            wait = pltpu.make_async_copy(view, view, sem).wait
            if when is None:
                wait()
            else:
                pl.when(when)(wait)


def at(start, size, step=None):
    return pl.ds(pl.multiple_of(start, step or size), size)


def fused_kernel(p, names, *refs):
    ins, refs = refs[:16], refs[16:]
    lengths, feats_in, lat_in, wq_in, wk_in, wv_in, wo_in, wu_in, wd_in = ins[:9]
    smalls, cot_in = ins[9:15], ins[15]
    outs, refs = refs[:11], refs[11:]
    res_out, byte_out, go, gu, gd, gv, gk, gl, gq_out, glat_out, vec_out = outs
    sems = refs[-1]
    s = types.SimpleNamespace(**dict(zip(names, refs[:-1])))
    cp = Copies(sems)
    ctx, zs = p.ctx, p.zs
    c, z = lax.axis_index("ctx"), lax.axis_index("wshard")
    h, q = lax.rem(c, 2), lax.div(c, 2)
    x, y = lax.rem(q, 2), lax.div(q, 2)
    other = 1 - h
    core = c + 1 - 2 * h
    chips = (c + 2 - 4 * x, c + 4 - 8 * y, c + 6 - 4 * x - 8 * y)
    near = (chips[0] * (1 - h) + chips[1] * h, chips[1] * (1 - h) + chips[0] * h)
    zed = [lax.rem(z + j, zs) for j in range(1, zs)]
    plane = [lax.rem(c + j, ctx) for j in range(1, ctx)]

    barrier = pltpu.get_barrier_semaphore()
    for peer in plane:
        pl.semaphore_signal(barrier, inc=1, device_id=(peer, z), device_id_type=pl.DeviceIdType.MESH)
    for peer in zed:
        pl.semaphore_signal(barrier, inc=1, device_id=(c, peer), device_id_type=pl.DeviceIdType.MESH)
    pl.semaphore_wait(barrier, ctx - 1 + zs - 1)

    load_feats = cp.local(feats_in, s.feats)
    for row, ref in enumerate(smalls):
        s.small_own[row : row + 1, 0 : ref.shape[0]] = ref[...].reshape(1, -1).astype(FULL)
    small_pair = cp.group()
    for peer in zed:
        cp.send(small_pair, s.small_own, s.small.at[z], c, peer)
    cp.sent(small_pair, s.small.at[0 : zs - 1])

    class Weight:
        def __init__(self, ref, source, cuts, line):
            self.ref, self.source, self.cuts, self.line = ref, source, cuts, line
            if line:
                self.up = [cp.group() for _ in range(zs - 1)]
                self.down = [cp.group() for _ in range(zs - 1)]
            self.rows, cols = source.shape
            self.part, self.cols = self.rows // cuts, cols // 2
            self.slot = q if cuts == 4 else lax.rem(x + y, 2)
            self.mine = at(h * self.cols, self.cols)
            self.pairs = [cp.group() for _ in range(4)]

        def view(self, rows):
            return self.ref.at[pl.ds(0, rows), pl.ds(0, self.cols)]

        def block(self, zz, qq):
            return self.ref.at[at(zz * self.rows + qq * self.part, self.part, 16), self.mine]

        def hop(self, i):
            one = self.view(self.part)

            def forward(pair, source, dest, when):
                @pl.when(when)
                def _():
                    cp.send(pair, source, self.block(dest[0], self.slot), c, dest[1])

                cp.sent(pair, one, when)

            if i == 0:
                mine = self.source.at[at(self.slot * self.part, self.part, 16), self.mine]
                forward(self.up[0], mine, (z, z + 1), z < zs - 1)
                forward(self.down[0], mine, (z, z - 1), z > 0)
                self.load = cp.local(self.source, self.ref.at[at(z * self.rows, self.rows, 16), :])
                return

            @pl.when(z >= i)
            def _():
                cp.got(self.up[i - 1], one)

            if i < zs - 1:
                block = self.block(lax.rem(z + zs - i, zs), self.slot)
                forward(self.up[i], block, (lax.rem(z + zs - i, zs), z + 1), (z >= i) & (z < zs - 1))

            @pl.when(z + i < zs)
            def _():
                cp.got(self.down[i - 1], one)

            if i < zs - 1:
                block = self.block(lax.rem(z + i, zs), self.slot)
                forward(self.down[i], block, (lax.rem(z + i, zs), z - 1), (z + i < zs) & (z > 0))

        def start(self):
            for peer in zed:
                cp.send(
                    self.pairs[0],
                    self.source.at[at(self.slot * self.part, self.part, 16), self.mine],
                    self.block(z, self.slot),
                    c,
                    peer,
                )
            cp.sent(self.pairs[0], self.view(3 * self.part))
            self.load = cp.local(self.source, self.ref.at[at(z * self.rows, self.rows, 16), :])

        def first(self):
            if self.line:
                self.hop(zs - 1)
            else:
                cp.got(self.pairs[0], self.view(3 * self.part))
            for zz in zed:
                block = self.block(zz, self.slot)
                cp.send(self.pairs[1], block, block, near[0], z)
            cp.sent(self.pairs[1], self.view(3 * self.part))

        def second(self):
            cp.got(self.pairs[1], self.view(3 * self.part))
            for zz in zed:
                for qq in (q, lax.div(near[0], 2)):
                    block = self.block(zz, qq)
                    cp.send(self.pairs[2], block, block, near[1], z)
            cp.sent(self.pairs[2], self.view(6 * self.part))

        def third(self):
            if self.cuts == 4:
                cp.got(self.pairs[2], self.view(6 * self.part))
            else:
                cp.got(self.pairs[1], self.view(3 * self.part))
            for zz in zed:
                block = self.ref.at[at(zz * self.rows, self.rows, 16), self.mine]
                cp.send(self.pairs[3], block, block, core, z)
            cp.sent(self.pairs[3], self.view(3 * self.rows))

        def ready(self):
            cp.got(self.pairs[3], self.view(3 * self.rows))
            self.load.wait()

    wk, wq, lat = Weight(s.wk, wk_in, 4, False), Weight(s.wq, wq_in, 4, False), Weight(s.lat, lat_in, 4, False)
    wv, wo = Weight(s.wv, wv_in, 4, False), Weight(s.wo, wo_in, 4, True)
    wu, wd = Weight(s.wu, wu_in, 4, True), Weight(s.wd, wd_in, 2, True)
    for weight in (wk, wq, lat, wv):
        weight.start()
    wo.hop(0)
    load_cot = cp.local(cot_in, s.cot)

    cp.got(small_pair, s.small.at[0 : zs - 1])
    s.small[z] = s.small_own[...]
    for row, ref in enumerate(smalls):
        size = ref.shape[0]
        for zz in range(zs):
            s.vec[row : row + 1, zz * size : (zz + 1) * size] = s.small[zz, row : row + 1, 0:size]
    vec = s.vec
    gain_lat, bias_lat = vec[0:1, :], vec[1:2, :]

    half_cols = at(h * (p.dl // 2), p.dl // 2)
    own = at(h * p.lat, p.lat)
    tiles = p.dl // 256
    quarter = p.lat // 4
    own_rows = at(h * p.lat + q * quarter, quarter)
    score_scale = 1.0 / math.sqrt(p.head)
    start_slot = c * p.slots
    lane_stat = lanes(p.lat, 128)
    gain_mlp, bias_mlp = vec[4:5, :], vec[5:6, :]
    qhalf, vhalf = p.qk // 2, p.vd // 2
    zrows = p.din // zs
    vpart = zrows // 4
    order = [*zed, z]

    def window(head):
        low_lane = pl.multiple_of(lax.div(head * p.vhead, 128) * 128, 128)
        return pl.ds(low_lane, 256), head * p.vhead - low_lane

    def mask_of(rows, low_lane):
        lane = lanes(rows, 256)
        return ((lane >= low_lane) & (lane < low_lane + p.vhead)).astype(FULL)

    def normed_bytes():
        load_feats.wait()

        @pl.loop(0, p.rows_in // 64)
        def _(i):
            rows = at(i * 64, 64)
            normed, _ = ln_parts(s.feats[rows, :].astype(FULL))
            s.nin[rows, :] = (normed * vec[2:3, 0 : p.din] + vec[3:4, 0 : p.din]).astype(LOW)

    def turned_bytes():
        @pl.loop(0, p.din // 128)
        def _(i):
            tile = at(i * 128, 128)
            s.nin_t[tile, :] = s.nin[:, tile].T

    def make_keys():
        @pl.loop(0, p.seqs)
        def _(i):
            rows = at(i * p.slots, p.slots)
            low = matmul(s.nin[rows, :], s.wk[...]).astype(LOW)
            s.keys[rows, :] = low
            s.keys_t[:, rows] = low.T

    def normed_latents():
        @pl.loop(0, p.lat // 64, unroll=2)
        def _(i):
            rows = at(i * 64, 64)
            normed, _ = ln_parts(s.lat[rows, :].astype(FULL))
            s.nlat[rows, :] = (normed * gain_lat + bias_lat).astype(LOW)

    def make_queries():
        queries = matmul(s.nlat[...], s.wq[...])
        lane_q = lanes(p.lat, p.qk)
        for head in range(H):
            inside = (lane_q >= head * p.head) & (lane_q < (head + 1) * p.head)
            s.qmask[head * p.lat : (head + 1) * p.lat, :] = jnp.where(inside, queries, 0.0).astype(LOW)

    max_pair = cp.group()

    def make_scores():
        s.stat[...] = jnp.zeros_like(s.stat)
        for seq in range(p.seqs):

            @pl.loop(0, H, unroll=4)
            def _(head):
                raw = matmul_nt(
                    s.qmask[at(head * p.lat, p.lat), :], s.keys[seq * p.slots : (seq + 1) * p.slots, :]
                )
                valid = lanes(p.lat, p.slots) < lengths[seq] - start_slot
                scores = jnp.where(valid, raw * score_scale, -1e30)
                s.scores[at((seq * H + head) * p.lat, p.lat), :] = scores
                top = jnp.max(scores, axis=-1, keepdims=True)
                s.stat[...] = jnp.where(lanes(p.lat, 128) == seq * H + head, top, s.stat[...])

        s.stat_t[...] = s.stat[...].T
        s.max_own[...] = s.stat_t[0 : 2 * H, :]
        for peer in plane:
            cp.send(max_pair, s.max_own, s.max_in.at[c], peer, z)
        cp.sent(max_pair, s.max_in.at[0 : ctx - 1])

    def make_values():
        @pl.loop(0, p.vd // 256, unroll=True)
        def _(i):
            tile = at(i * 256, 256)
            s.values[:, tile] = matmul(s.nin[...], s.wv[:, tile]).astype(LOW)

    def get_max():
        cp.got(max_pair, s.max_in.at[0 : ctx - 1])
        s.max_in[c] = s.max_own[...]
        top = s.max_in[0]
        for i in range(1, ctx):
            top = jnp.maximum(top, s.max_in[i])
        s.max_all[...] = top
        s.stat_t[0 : 2 * H, :] = top
        s.max_t[...] = s.stat_t[...].T
        s.stat[...] = jnp.zeros_like(s.stat)

    def partial(seq):
        s.numer[...] = jnp.zeros_like(s.numer)

        @pl.loop(0, H, unroll=4)
        def _(head):
            i = seq * H + head
            lane = lanes(p.lat, 128)
            top = jnp.sum(jnp.where(lane == i, s.max_t[...], 0.0), axis=-1, keepdims=True)
            weights = jnp.exp(s.scores[at(i * p.lat, p.lat), :] - top)
            total = jnp.sum(weights, axis=-1, keepdims=True)
            s.stat[...] = jnp.where(lane == i, total, s.stat[...])
            cols, low_lane = window(head)
            part = s.values[at(seq * p.slots, p.slots), cols] * mask_of(p.slots, low_lane).astype(LOW)
            s.numer[:, cols] += matmul(weights.astype(LOW), part)

        s.stat_t[...] = s.stat[...].T
        s.sums[seq] = s.stat_t[at(seq * H, H), :]

    pair_pair, sums_pair = cp.group(), cp.group()
    chip_sums_pair = cp.group()
    chip_pairs, att_pairs = [cp.group() for _ in range(2)], [cp.group() for _ in range(2)]
    near_chip = [lax.div(near[0], 2), lax.div(near[1], 2)]

    def partial_other():
        partial(other)
        s.numer_low[...] = s.numer[...].astype(LOW)
        cp.send(sums_pair, s.sums.at[other], s.sums_in, core, z)
        cp.send(pair_pair, s.numer_low, s.numer_in, core, z)
        cp.sent(pair_pair, s.numer_low)
        cp.sent(sums_pair, s.sums_in)

    def partial_own():
        partial(h)

    def chip_numer():
        cp.got(sums_pair, s.sums_in)
        s.chip_sums[...] = s.sums[h] + s.sums_in[...]
        for peer in chips:
            cp.send(chip_sums_pair, s.chip_sums, s.chip_sums_in.at[q], peer, z)
        cp.sent(chip_sums_pair, s.chip_sums_in.at[0:3])
        cp.got(pair_pair, s.numer_in)
        s.chip[...] = (s.numer[...] + s.numer_in[...].astype(FULL)).astype(LOW)
        for slot, qq in enumerate((3 - q, near_chip[0])):
            rows = at(qq * quarter, quarter)
            cp.send(chip_pairs[0], s.chip.at[rows, :], s.chip_in.at[slot], near[0], z)
        cp.sent(chip_pairs[0], s.chip_in.at[0:2])

    def chip_pass():
        cp.got(chip_pairs[0], s.chip_in.at[0:2])
        rows = at(near_chip[1] * quarter, quarter)
        s.chip_in[3] = (s.chip[rows, :].astype(FULL) + s.chip_in[0].astype(FULL)).astype(LOW)
        cp.send(chip_pairs[1], s.chip_in.at[3], s.chip_in.at[2], near[1], z)
        cp.sent(chip_pairs[1], s.chip_in.at[3])

    def turned_weights():
        for seq in range(p.seqs):

            @pl.loop(0, H, unroll=4)
            def _(head):
                i = seq * H + head
                raw = matmul_nt(
                    s.keys[seq * p.slots : (seq + 1) * p.slots, :], s.qmask[at(head * p.lat, p.lat), :]
                )
                slot = lax.broadcasted_iota(jnp.int32, (p.slots, p.lat), 0)
                masked = jnp.where(slot < lengths[seq] - start_slot, raw * score_scale, -1e30)
                s.scores[at(i * p.slots, p.slots), :] = jnp.exp(masked - s.max_all[pl.ds(i, 1), :])

    def make_scale():
        cp.got(chip_sums_pair, s.chip_sums_in.at[0:3])
        s.chip_sums_in[q] = s.chip_sums[...]
        sums = s.chip_sums_in
        inverse = 1.0 / ((sums[0] + sums[1]) + (sums[2] + sums[3]))
        s.stats[h, 0:H, :] = inverse
        s.stat_t[0:H, :] = inverse
        s.stat[...] = s.stat_t[...].T
        s.scale[...] = jnp.zeros_like(s.scale)
        own_quarter = s.stat[at(q * quarter, quarter), :]
        for head in range(H):
            low_lane = head * p.vhead // 128 * 128
            lane = lanes(quarter, 256) + low_lane
            inside = (lane >= head * p.vhead) & (lane < (head + 1) * p.vhead)
            cols = slice(low_lane, low_lane + 256)
            s.scale[:, cols] = jnp.where(inside, own_quarter[:, head : head + 1], s.scale[:, cols])

    def make_att():
        cp.got(chip_pairs[1], s.chip_in.at[2])
        own_numer = s.chip[at(q * quarter, quarter), :].astype(FULL)
        added = own_numer + (s.chip_in[1].astype(FULL) + s.chip_in[2].astype(FULL))
        s.att[own_rows, :] = (added * s.scale[...]).astype(LOW)
        cp.send(att_pairs[0], s.att.at[own_rows, :], s.att.at[own_rows, :], near[0], z)
        cp.sent(att_pairs[0], s.att.at[0:quarter, :])

    def att_pass():
        cp.got(att_pairs[0], s.att.at[0:quarter, :])
        for qq in (q, near_chip[0]):
            rows = at(h * p.lat + qq * quarter, quarter)
            cp.send(att_pairs[1], s.att.at[rows, :], s.att.at[rows, :], near[1], z)
        cp.sent(att_pairs[1], s.att.at[0 : 2 * quarter, :])

    shares = {}

    def share(ref):
        pair = cp.group()
        cp.send(pair, ref.at[own, :], ref.at[own, :], core, z)
        cp.sent(pair, ref.at[0 : p.lat, :])
        shares[id(ref)] = pair

    def shared(ref):
        cp.got(shares.pop(id(ref)), ref.at[0 : p.lat, :])

    def get_att():
        cp.got(att_pairs[1], s.att.at[0 : 2 * quarter, :])
        share(s.att)

    def make_hidden():
        @pl.loop(0, tiles, unroll=True)
        def _(i):
            tile = at(i * 256, 256)
            s.hid[:, tile] = s.lat[:, tile].astype(FULL) + matmul(s.att[own, :], s.wo[:, tile])

    def make_mid():
        @pl.loop(0, p.lat // 64, unroll=2)
        def _(i):
            normed, _ = ln_parts(s.hid[at(i * 64, 64), :])
            s.mid[at(h * p.lat + i * 64, 64), :] = (normed * gain_mlp + bias_mlp).astype(LOW)

        share(s.mid)

    def make_act():
        load_cot.wait()

        @pl.loop(0, tiles, unroll=True)
        def _(i):
            tile = at(i * 256, 256)
            up = matmul(s.mid[own, :], s.wu[:, tile])
            cdf = 0.5 * (1.0 + lax.erf(up * (1.0 / math.sqrt(2.0))))
            density = jnp.exp(-0.5 * up * up) * (1.0 / math.sqrt(2.0 * math.pi))
            s.act[own, tile] = (up * cdf).astype(LOW)
            s.slope[:, tile] = cdf + up * density

        share(s.act)

    class Reduce:
        def __init__(self, left, right, grads, arrive, final, out):
            self.left, self.right, self.out = left, right, out
            self.grads, self.arrive, self.final = grads, arrive, final
            self.part = self.final.shape[0]
            self.rows = self.part * 4
            self.pairs = [cp.group() for _ in range(4)]

        def product(self):
            @pl.loop(0, self.grads.shape[0] // 256, unroll=True)
            def _(i):
                rows = at(i * 256, 256)
                self.grads[rows, :] = matmul_tn(self.left[:, rows], self.right[:, half_cols]).astype(LOW)

        def block(self, zz):
            return self.grads.at[at(zz * self.rows + q * self.part, self.part, 16), :]

        def scatter(self):
            for peer in zed:
                cp.send(self.pairs[0], self.block(peer), self.arrive.at[z], c, peer)
            cp.sent(self.pairs[0], self.arrive.at[0 : zs - 1])

        def add(self):
            cp.got(self.pairs[0], self.arrive.at[0 : zs - 1])
            self.arrive[z] = self.grads[at(z * self.rows + q * self.part, self.part, 16), :]
            total = self.arrive[0].astype(FULL)
            for zz in range(1, zs):
                total = total + self.arrive[zz].astype(FULL)
            self.final[...] = total.astype(LOW)
            here = self.out.at[at(q * self.part, self.part, 16), half_cols]
            cp.send(self.pairs[1], self.final, here, near[0], z)
            cp.sent(self.pairs[1], self.final)
            self.store = cp.local(self.final, here)

        def spread(self):
            cp.got(self.pairs[1], self.final)
            here = self.out.at[at(q * self.part, self.part, 16), half_cols]
            there = self.out.at[at(near_chip[0] * self.part, self.part, 16), half_cols]
            cp.send(self.pairs[2], self.final, here, near[1], z)
            cp.send(self.pairs[2], there, there, near[1], z)
            cp.sent(self.pairs[2], self.arrive.at[0:2])

        def halve(self):
            cp.got(self.pairs[2], self.arrive.at[0:2])
            self.store.wait()
            block = self.out.at[:, half_cols]
            cp.send(self.pairs[3], block, block, core, z)
            cp.sent(self.pairs[3], block)

        def done(self):
            cp.got(self.pairs[3], self.out.at[:, half_cols])

    down = Reduce(s.act, s.cot, s.dwd, s.zd, s.fd, gd)
    upper = Reduce(s.mid, s.dup, s.dwu, s.zu, s.fu, gu)
    outer = Reduce(s.att, s.dhid, s.dwo, s.zo, s.fo, go)
    latents = Reduce(s.att, s.dhid, s.dlat, s.zl, s.fl, gl)
    reduces = (down, upper, outer, latents)

    def down_grads():
        shared(s.act)
        down.product()
        down.scatter()

    def upper_grads():
        shared(s.mid)
        shared(s.dup)
        upper.product()
        upper.scatter()

    def outer_grads():
        shared(s.att)
        shared(s.dhid)
        outer.product()
        outer.scatter()
        s.dlat[...] = (
            s.dhid[0 : p.lat, half_cols].astype(FULL) + s.dhid[p.lat : 2 * p.lat, half_cols].astype(FULL)
        ).astype(LOW)
        latents.scatter()

    def make_dup():
        @pl.loop(0, tiles, unroll=True)
        def _(i):
            tile = at(i * 256, 256)
            dact = matmul_nt(s.cot[own, :], s.wd[tile, :])
            s.dup[own, tile] = (dact * s.slope[:, tile]).astype(LOW)

        share(s.dup)

    def make_dmid():
        @pl.loop(0, tiles, unroll=True)
        def _(i):
            tile = at(i * 256, 256)
            s.dmid[:, tile] = matmul_nt(s.dup[own, :], s.wu[tile, :])

    def make_dhid():
        s.vs[...] = jnp.zeros_like(s.vs)

        @pl.loop(0, p.lat // 64, unroll=2)
        def _(i):
            rows = at(i * 64, 64)
            full_rows = at(h * p.lat + i * 64, 64)
            normed, scale = ln_parts(s.hid[rows, :])
            grad = s.dmid[rows, :]
            s.vs[0:1, :] += columns_sum(grad * normed)
            s.vs[1:2, :] += columns_sum(grad)
            total = s.cot[full_rows, :].astype(FULL) + ln_grad(grad, gain_mlp, normed, scale)
            s.dhid[full_rows, :] = total.astype(LOW)

        share(s.dhid)

    stats_pairs = [cp.group() for _ in range(2)]

    def share_inverse():
        cp.send(stats_pairs[0], s.stats.at[h, 0:H], s.stats.at[h, 0:H], core, z)
        cp.sent(stats_pairs[0], s.stats.at[0, 0:H])

    def make_datt():
        @pl.loop(0, tiles, unroll=True)
        def _(i):
            tile = at(i * 256, 256)
            s.datt[own, tile] = matmul_nt(s.dhid[own, :], s.wo[tile, :]).astype(LOW)

        share(s.datt)

    def make_delta():
        s.stat[...] = jnp.zeros_like(s.stat)

        @pl.loop(0, H, unroll=4)
        def _(head):
            cols, low_lane = window(head)
            product = s.datt[own, cols].astype(FULL) * s.att[own, cols].astype(FULL)
            delta = jnp.sum(product * mask_of(p.lat, low_lane), axis=-1, keepdims=True)
            s.stat[...] = jnp.where(lanes(p.lat, 128) == head, delta, s.stat[...])

        s.stat_t[...] = s.stat[...].T
        s.stats[h, H : 2 * H, :] = s.stat_t[0:H, :]
        cp.send(stats_pairs[1], s.stats.at[h, H : 2 * H], s.stats.at[h, H : 2 * H], core, z)
        cp.sent(stats_pairs[1], s.stats.at[0, 0:H])

    def values_grad(seq):
        latent_rows = at(seq * p.lat, p.lat)
        s.numer[...] = jnp.zeros_like(s.numer)

        @pl.loop(0, H, unroll=4)
        def _(head):
            cols, low_lane = window(head)
            inverse = s.stats[seq, pl.ds(head, 1), :]
            probs = s.scores[at((seq * H + head) * p.slots, p.slots), :] * inverse
            grad = s.datt[latent_rows, cols] * mask_of(p.lat, low_lane).astype(LOW)
            s.numer[:, cols] += matmul(probs.astype(LOW), grad)

        s.dvalues[at(seq * p.slots, p.slots), :] = s.numer[...].astype(LOW)

    def scores_grad(seq):
        slots = at(seq * p.slots, p.slots)
        latent_rows = at(seq * p.lat, p.lat)
        s.dk_sum[...] = jnp.zeros_like(s.dk_sum)

        @pl.loop(0, H, unroll=4)
        def _(head):
            heads = at(head * p.lat, p.lat)
            cols, low_lane = window(head)
            inverse = s.stats[seq, pl.ds(head, 1), :]
            delta = s.stats[seq, pl.ds(H + head, 1), :]
            probs = s.scores[at((seq * H + head) * p.slots, p.slots), :] * inverse
            grad = s.datt[latent_rows, cols] * mask_of(p.lat, low_lane).astype(LOW)
            dprobs = matmul_nt(s.values[slots, cols], grad)
            dscores = (probs * (dprobs - delta)).astype(LOW)
            s.dk_sum[...] += matmul(dscores, s.qmask[heads, :])
            block = at(head * p.head, p.head)
            s.dq_t[block, :] += matmul(s.keys_t[block, slots], dscores)

        s.dkeys[slots, :] = (s.dk_sum[...] * score_scale).astype(LOW)

    def weight_grads(ref, grad, width, side):
        cols = at(side * width, width)

        @pl.loop(0, p.din // 256, unroll=True)
        def _(i):
            rows = at(i * 256, 256)
            ref[side, rows, :] = matmul(s.nin_t[rows, :], grad[:, cols]).astype(LOW)

    class Local:
        def __init__(self, grads, arrive, chip, plane_in, plane, z_in, final, out):
            self.grads, self.arrive, self.chip, self.plane_in = grads, arrive, chip, plane_in
            self.plane, self.z_in, self.final, self.out = plane, z_in, final, out
            self.width = final.shape[1]
            self.pairs = [cp.group() for _ in range(5)]
            self.firsts = [cp.group() for _ in range(zs // 2)]
            self.seconds = [cp.group() for _ in range(zs // 2)]
            self.mine = at(h * self.width, self.width)

        def pair(self):
            cp.send(self.pairs[0], self.grads.at[other], self.arrive, core, z)
            cp.sent(self.pairs[0], self.arrive)

        def rows(self, qq):
            return at(qq * vpart, vpart, 16)

        def chunk(self, i):
            for zz in order[2 * i : 2 * i + 2]:
                rows = at(zz * zrows, zrows)
                total = self.grads[h, rows, :].astype(FULL) + self.arrive[rows, :].astype(FULL)
                self.chip[zz] = total.astype(LOW)
                for slot, qq in enumerate((3 - q, near_chip[0])):
                    cp.send(
                        self.firsts[i],
                        self.chip.at[zz, self.rows(qq), :],
                        self.plane_in.at[slot, zz],
                        near[0],
                        z,
                    )
            cp.sent(self.firsts[i], self.plane_in.at[0])

        def middle(self, i):
            cp.got(self.firsts[i], self.plane_in.at[0])
            for zz in order[2 * i : 2 * i + 2]:
                mine = self.chip[zz, self.rows(near_chip[1]), :].astype(FULL)
                self.plane_in[3, zz] = (mine + self.plane_in[0, zz].astype(FULL)).astype(LOW)
                cp.send(self.seconds[i], self.plane_in.at[3, zz], self.plane_in.at[2, zz], near[1], z)
            cp.sent(self.seconds[i], self.plane_in.at[0, 0:2])

        def add(self, i):
            cp.got(self.seconds[i], self.plane_in.at[0, 0:2])
            for zz in order[2 * i : 2 * i + 2]:
                mine = self.chip[zz, self.rows(q), :].astype(FULL)
                parts = self.plane_in[1, zz].astype(FULL) + self.plane_in[2, zz].astype(FULL)
                self.plane[zz] = (mine + parts).astype(LOW)
                if zz is not order[-1]:
                    cp.send(self.pairs[1], self.plane.at[zz], self.z_in.at[z], c, zz)
            if i == zs // 2 - 1:
                cp.sent(self.pairs[1], self.z_in.at[0 : zs - 1])

        def finish(self):
            cp.got(self.pairs[1], self.z_in.at[0 : zs - 1])
            self.z_in[z] = self.plane[z]
            total = self.z_in[0].astype(FULL)
            for zz in range(1, zs):
                total = total + self.z_in[zz].astype(FULL)
            self.final[...] = total.astype(LOW)
            here = self.out.at[self.rows(q), self.mine]
            cp.send(self.pairs[2], self.final, here, near[0], z)
            cp.sent(self.pairs[2], self.final)
            self.store = cp.local(self.final, here)

        def spread(self):
            cp.got(self.pairs[2], self.final)
            here = self.out.at[self.rows(q), self.mine]
            there = self.out.at[self.rows(near_chip[0]), self.mine]
            cp.send(self.pairs[3], self.final, here, near[1], z)
            cp.send(self.pairs[3], there, there, near[1], z)
            cp.sent(self.pairs[3], self.z_in.at[0:2])

        def halve(self):
            cp.got(self.pairs[3], self.z_in.at[0:2])
            self.store.wait()
            block = self.out.at[:, self.mine]
            cp.send(self.pairs[4], block, block, core, z)
            cp.sent(self.pairs[4], block)

        def done(self):
            cp.got(self.pairs[4], self.out.at[:, self.mine])

    key_grads = Local(s.swk, s.rwk, s.cwk, s.pwk_in, s.pwk, s.zwk_in, s.fwk, gk)
    value_grads = Local(s.swv, s.rwv, s.cwv, s.pwv_in, s.pwv, s.zwv_in, s.fwv, gv)
    def byte_matmul(seq):
        rows = at(seq * p.slots, p.slots)
        for tile in range(p.din // 256):
            cols = slice(tile * 256, (tile + 1) * 256)
            grad = matmul_nt(s.dkeys[rows, :], s.wk[cols, :]) + matmul_nt(s.dvalues[rows, :], s.wv[cols, :])
            s.scores[at(tile * p.rows_in + seq * p.slots, p.slots), :] = grad

    def byte_part(part):
        byte_matmul(part)

        @pl.loop(part * p.slots // 64, (part + 1) * p.slots // 64, unroll=2)
        def _(i):
            rows = at(i * 64, 64)
            tiles_in = [s.scores[at(k * p.rows_in + i * 64, 64), :] for k in range(p.din // 256)]
            grad = jnp.concatenate(tiles_in, axis=1)
            normed, scale = ln_parts(s.feats[rows, :].astype(FULL))
            s.vs[2:3, 0 : p.din] += columns_sum(grad * normed)
            s.vs[3:4, 0 : p.din] += columns_sum(grad)
            s.bgrad[rows, :] = ln_grad(grad, vec[2:3, 0 : p.din], normed, scale).astype(LOW)

    kv = (value_grads, key_grads)
    dq_pairs = [cp.group() for _ in range(5)]
    vs_pairs = [cp.group() for _ in range(3)]
    res_pair = cp.group()
    stores = []
    own_half = at(h * qhalf, qhalf)

    def values_own():
        values_grad(h)

    def values_other():
        cp.got(stats_pairs[0], s.stats.at[0, 0:H])
        shared(s.datt)
        values_grad(other)

    def value_weights():
        weight_grads(s.swv, s.dvalues, vhalf, other)
        value_grads.pair()

    def value_weights_own():
        weight_grads(s.swv, s.dvalues, vhalf, h)

    def value_chunks():
        cp.got(value_grads.pairs[0], value_grads.arrive)
        for i in range(zs // 2):
            value_grads.chunk(i)

    def scores_own():
        s.dq_t[...] = jnp.zeros_like(s.dq_t)
        scores_grad(h)

    def scores_other():
        cp.got(stats_pairs[1], s.stats.at[0, 0:H])
        scores_grad(other)
        s.dq[...] = (s.dq_t[...] * score_scale).T.astype(LOW)
        cp.send(dq_pairs[0], s.dq.at[:, at(other * qhalf, qhalf)], s.dq_in1, core, z)
        cp.sent(dq_pairs[0], s.dq_in1)

    def key_weights():
        weight_grads(s.swk, s.dkeys, qhalf, other)
        key_grads.pair()
        weight_grads(s.swk, s.dkeys, qhalf, h)

    def dq_chip():
        cp.got(dq_pairs[0], s.dq_in1)
        s.dq_chip[...] = (s.dq[:, own_half].astype(FULL) + s.dq_in1[...].astype(FULL)).astype(LOW)
        cp.send(dq_pairs[1], s.dq_chip, s.dq_in2.at[0], near[0], z)
        cp.sent(dq_pairs[1], s.dq_chip)

    def dq_pass():
        cp.got(dq_pairs[1], s.dq_chip)
        s.dq_in2[2] = (s.dq_chip[...].astype(FULL) + s.dq_in2[0].astype(FULL)).astype(LOW)
        cp.send(dq_pairs[4], s.dq_in2.at[2], s.dq_in2.at[1], near[1], z)
        cp.sent(dq_pairs[4], s.dq_chip)

    def key_chunks():
        cp.got(key_grads.pairs[0], key_grads.arrive)
        for i in range(zs // 2):
            key_grads.chunk(i)

    def byte_store():
        stores.append(cp.local(s.bgrad, byte_out))
        cp.send(vs_pairs[0], s.vs, s.vs_in1, core, z)
        cp.sent(vs_pairs[0], s.vs)

    def dq_plane():
        cp.got(dq_pairs[4], s.dq_chip)
        s.dq_plane[...] = (s.dq_in2[1].astype(FULL) + s.dq_in2[2].astype(FULL)).astype(LOW)
        for peer in zed:
            cp.send(dq_pairs[2], s.dq_plane, s.dq_in3.at[z], c, peer)
        cp.sent(dq_pairs[2], s.dq_in3.at[0 : zs - 1])

    def vs_chip():
        cp.got(vs_pairs[0], s.vs_in1)
        s.vs_chip[...] = s.vs[...] + s.vs_in1[...]
        for peer in chips:
            cp.send(vs_pairs[1], s.vs_chip, s.vs_in2.at[q], peer, z)
        cp.sent(vs_pairs[1], s.vs_in2.at[0:3])

    def make_result():
        @pl.loop(0, tiles, unroll=True)
        def _(i):
            tile = at(i * 256, 256)
            s.res[:, tile] = (s.hid[:, tile] + matmul(s.act[own, :], s.wd[:, tile])).astype(LOW)

        cp.send(res_pair, s.res, res_out.at[own, :], core, z)
        cp.sent(res_pair, s.res)
        stores.append(cp.local(s.res, res_out.at[own, :]))

    def vs_plane():
        cp.got(vs_pairs[1], s.vs_in2.at[0:3])
        s.vs_in2[q] = s.vs_chip[...]
        parts = s.vs_in2
        total = (parts[0] + parts[1]) + (parts[2] + parts[3])
        row_ids = lax.broadcasted_iota(jnp.int32, (8, p.dl), 0)
        s.vs_plane[...] = jnp.where(row_ids < 2, s.vs_chip[...], total)
        for peer in zed:
            cp.send(vs_pairs[2], s.vs_plane, s.vs_in3.at[z], c, peer)
        cp.sent(vs_pairs[2], s.vs_in3.at[0 : zs - 1])

    def dq_total():
        cp.got(dq_pairs[2], s.dq_in3.at[0 : zs - 1])
        s.dq_in3[z] = s.dq_plane[...]
        parts = s.dq_in3
        total = parts[0].astype(FULL)
        for zz in range(1, zs):
            total = total + parts[zz].astype(FULL)
        s.dq_all[:, own_half] = total.astype(LOW)
        cp.send(dq_pairs[3], s.dq_all.at[:, own_half], s.dq_all.at[:, own_half], core, z)
        cp.sent(dq_pairs[3], s.dq_in1)

    def query_grads():
        cp.got(dq_pairs[3], s.dq_in1)

        @pl.loop(0, tiles, unroll=True)
        def _(i):
            tile = at(i * 256, 256)
            s.gq[tile, :] = matmul_tn(s.nlat[:, tile], s.dq_all[...])
            s.dmid[:, tile] = matmul_nt(s.dq_all[...], s.wq[tile, :])

        stores.append(cp.local(s.gq.at[at(z * (p.dl // zs), p.dl // zs, 16), :], gq_out))

    def latent_grads():
        cp.got(vs_pairs[2], s.vs_in3.at[0 : zs - 1])
        s.vs_in3[z] = s.vs_plane[...]
        total = s.vs_in3[0]
        for zz in range(1, zs):
            total = total + s.vs_in3[zz]
        s.vs_all[...] = total
        s.vs_all[4:6, :] = jnp.zeros((2, p.dl), FULL)

        @pl.loop(0, p.lat // 64, unroll=2)
        def _(i):
            rows = at(i * 64, 64)
            normed, scale = ln_parts(s.lat[rows, :].astype(FULL))
            grad = s.dmid[rows, :]
            s.vs_all[4:5, :] += columns_sum(grad * normed)
            s.vs_all[5:6, :] += columns_sum(grad)
            s.slope[rows, :] = ln_grad(grad, gain_lat, normed, scale)

        stores.append(cp.local(s.slope.at[at(z * (p.lat // zs), p.lat // zs, 16), :], glat_out))
        stores.append(cp.local(s.vs_all, vec_out))

    normed_bytes()
    wk.first()
    turned_bytes()
    wk.second()
    wq.first()
    wk.third()
    wu.hop(0)
    wq.second()
    lat.first()
    lat.second()
    wo.hop(1)
    wv.first()
    wq.third()
    wk.ready()
    wq.ready()
    lat.third()
    lat.ready()
    normed_latents()
    make_keys()
    wv.second()
    make_queries()
    wo.hop(2)
    make_scores()
    wd.hop(0)
    wo.first()
    wv.third()
    wu.hop(1)
    wv.ready()
    wo.second()
    get_max()
    make_values()
    partial_other()
    wu.hop(2)
    partial_own()
    chip_numer()
    wd.hop(1)
    wu.first()
    wo.third()
    wd.hop(2)
    turned_weights()
    chip_pass()
    make_scale()
    wo.ready()
    wu.second()
    make_att()
    att_pass()
    wu.third()
    wd.first()
    get_att()
    make_hidden()
    wu.ready()
    make_mid()
    make_act()
    wd.third()
    share_inverse()
    down_grads()
    wd.ready()
    make_dup()
    make_dmid()
    make_dhid()
    make_datt()
    make_delta()
    values_own()
    values_other()
    value_weights()
    upper_grads()
    down.add()
    value_weights_own()
    value_chunks()
    scores_own()
    scores_other()
    value_grads.middle(0)
    byte_part(0)
    dq_chip()
    value_grads.middle(1)
    value_grads.add(0)
    key_weights()
    down.spread()
    key_chunks()
    value_grads.add(1)
    outer_grads()
    down.halve()
    key_grads.middle(0)
    upper.add()
    key_grads.middle(1)
    byte_part(1)
    dq_pass()
    key_grads.add(0)
    upper.spread()
    key_grads.add(1)
    dq_plane()
    value_grads.finish()
    value_grads.spread()
    byte_store()
    value_grads.halve()
    vs_chip()
    outer.add()
    key_grads.finish()
    make_result()
    latents.add()
    upper.halve()
    outer.spread()
    key_grads.spread()
    vs_plane()
    latents.spread()
    dq_total()
    query_grads()
    outer.halve()
    key_grads.halve()
    latents.halve()
    latent_grads()
    for part in (*reduces, *kv):
        part.done()
    cp.got(res_pair, s.res)
    for store in stores:
        store.wait()
    cp.drain()


def finish_kernel(p, *refs):
    ins, outs, scratch = refs[:11], refs[11:26], refs[26:]
    held, wide, sems = scratch[:11], scratch[11:17], scratch[17]
    z = lax.axis_index("wshard")
    order = (10, 2, 3, 4, 5, 0, 1, 7, 9, 8, 6)
    loads = {n: pltpu.make_async_copy(ins[n], held[n], sems.at[n]) for n in order}
    for load in loads.values():
        load.start()
    stores = []

    def store(ref, out):
        copy = pltpu.make_async_copy(ref, outs[out], sems.at[11 + out])
        copy.start()
        stores.append(copy)

    loads[10].wait()
    vec = held[10]
    for out, row in ((3, 4), (4, 5), (5, 2), (6, 3), (11, 0), (12, 1)):
        size = outs[out].shape[0]
        picked = vec[row : row + 1, 0:size]
        for zz in range(1, p.zs):
            picked = jnp.where(z == zz, vec[row : row + 1, zz * size : (zz + 1) * size], picked)
        outs[out][...] = picked.reshape(size)
    for n, out, slot in ((2, 10, 0), (3, 13, 1), (4, 14, 2), (5, 9, 3)):
        loads[n].wait()
        wide[slot][...] = held[n][...].astype(FULL)
        store(wide[slot], out)
    for n, out in ((0, 0), (1, 1)):
        loads[n].wait()
        store(held[n], out)
    loads[7].wait()
    loads[9].wait()
    wide[5][...] = held[9][...] + held[7][...].astype(FULL)
    store(wide[5], 2)
    loads[8].wait()
    store(held[8], 7)
    loads[6].wait()
    wide[4][...] = held[6][...].astype(FULL)
    store(wide[4], 8)
    for copy in stores:
        copy.wait()


def fused(*args):
    (byte_feats, lengths, latent, *smalls, cot) = (args[0], args[1], args[2], *args[3:7], args[11], args[12], args[15])
    w_query, w_key, w_value, w_output = args[7:11]
    w_up, w_down = args[13:15]
    seqs, slots, din = byte_feats.shape
    ctx, zs = lax.axis_size("ctx"), lax.axis_size("wshard")
    feats = byte_feats.reshape(seqs * slots, din)
    cot_flat = cot.reshape(-1, cot.shape[-1])
    p = Plan(ctx, zs, feats, latent, w_query, w_key, w_value, w_output, cot_flat)
    table = scratch_table(p)
    anywhere = pl.BlockSpec(memory_space=pl.ANY)
    in_vmem = pl.BlockSpec(memory_space=pltpu.VMEM)
    struct = jax.ShapeDtypeStruct
    made = pl.pallas_call(
        functools.partial(fused_kernel, p, tuple(table)),
        out_shape=(
            struct(cot_flat.shape, LOW),
            struct(feats.shape, LOW),
            struct(w_output.shape, LOW),
            struct(w_up.shape, LOW),
            struct(w_down.shape, LOW),
            struct(w_value.shape, LOW),
            struct(w_key.shape, LOW),
            struct(latent.shape, LOW),
            struct(w_query.shape, FULL),
            struct(latent.shape, FULL),
            struct((8, p.dl), FULL),
        ),
        in_specs=[pl.BlockSpec(memory_space=pltpu.SMEM)] + [anywhere] * 8 + [in_vmem] * 6 + [anywhere],
        out_specs=(anywhere,) * 11,
        scratch_shapes=[pltpu.VMEM(shape, kind) for shape, kind in table.values()]
        + [pltpu.SemaphoreType.DMA((SEMS,))],
        compiler_params=pltpu.CompilerParams(
            collective_id=0, has_side_effects=True, vmem_limit_bytes=67043328
        ),
        name="block",
    )(lengths, feats, latent, w_query, w_key, w_value, w_output, w_up, w_down, *smalls, cot_flat)
    shapes = (
        (cot_flat.shape, LOW),
        (feats.shape, LOW),
        (latent.shape, FULL),
        *((smalls[i].shape, FULL) for i in range(4)),
        *((w.shape, FULL) for w in (w_query, w_key, w_value, w_output)),
        *((smalls[i].shape, FULL) for i in (4, 5)),
        *((w.shape, FULL) for w in (w_up, w_down)),
    )
    outs = pl.pallas_call(
        functools.partial(finish_kernel, p),
        out_shape=tuple(struct(shape, kind) for shape, kind in shapes),
        in_specs=[anywhere] * 11,
        out_specs=tuple(in_vmem if len(shape) == 1 else anywhere for shape, _ in shapes),
        scratch_shapes=[pltpu.VMEM(one.shape, one.dtype) for one in made]
        + [pltpu.VMEM(shapes[n][0], FULL) for n in (10, 13, 14, 9, 8, 2)]
        + [pltpu.SemaphoreType.DMA((26,))],
        compiler_params=pltpu.CompilerParams(vmem_limit_bytes=60 * 2**20),
        name="finish",
    )(*made)
    return (outs[0].reshape(cot.shape), outs[1].reshape(byte_feats.shape), *outs[2:])


def shards(*args):
    if lax.axis_size("ctx") == 8 and lax.axis_size("wshard") == 4 and args[0].shape[0] == 2:
        return fused(*args)
    return plain(*args)


def solution(mesh):
    sharded, plain = P("wshard", None), P("wshard")
    return jax.shard_map(
        shards,
        mesh=mesh,
        in_specs=(
            P("wshard", "ctx", None),
            plain,
            sharded,
            plain,
            plain,
            plain,
            plain,
            sharded,
            sharded,
            sharded,
            sharded,
            plain,
            plain,
            sharded,
            sharded,
            P("wshard", None, None),
        ),
        out_specs=(
            P("wshard", None, None),
            P("wshard", "ctx", None),
            sharded,
            plain,
            plain,
            plain,
            plain,
            sharded,
            sharded,
            sharded,
            sharded,
            plain,
            plain,
            sharded,
            sharded,
        ),
        check_vma=False,
    )
```

```python
import functools
import math
import types

import jax
import jax.numpy as jnp
from jax import lax
from jax.experimental import pallas as pl
from jax.experimental.pallas import tpu as pltpu
from jax.sharding import PartitionSpec as P

H = 8
LOW = jnp.bfloat16
FULL = jnp.float32


def layer_norm(values, gain, offset):
    center = jnp.mean(values, axis=-1, keepdims=True)
    centred = values - center
    variance = jnp.mean(centred * centred, axis=-1, keepdims=True)
    return centred * lax.rsqrt(variance + 1e-05) * gain + offset


def exact_gelu(values):
    return jax.nn.gelu(values, approximate=False)


def matmul(left, right):
    return jnp.dot(left, right, preferred_element_type=FULL)


def matmul_tn(left, right):
    return lax.dot_general(left, right, (((0,), (0,)), ((), ())), preferred_element_type=FULL)


def matmul_nt(left, right):
    return lax.dot_general(left, right, (((1,), (1,)), ((), ())), preferred_element_type=FULL)


def gather(shard):
    return lax.all_gather(shard, "wshard", axis=0, tiled=True)


def scatter(total):
    return lax.psum_scatter(
        total.astype(LOW), "wshard", scatter_dimension=0, tiled=True
    ).astype(FULL)


SEMS = 256


def own_part(total, shard):
    size = shard.shape[0]
    return lax.dynamic_slice_in_dim(total, lax.axis_index("wshard") * size, size, 0)


def plain(
    byte_feats,
    lengths,
    latent_array,
    lat_gain,
    lat_bias,
    in_gain,
    in_bias,
    w_query,
    w_key,
    w_value,
    w_output,
    mlp_gain,
    mlp_bias,
    w_up,
    w_down,
    cotangent,
):
    seqs, slots, width = byte_feats.shape
    gain_in, bias_in = gather(in_gain).astype(FULL), gather(in_bias).astype(FULL)
    key_w, value_w = gather(w_key), gather(w_value)
    latent = gather(latent_array).astype(FULL)
    gain_lat, bias_lat = gather(lat_gain).astype(FULL), gather(lat_bias).astype(FULL)
    query_w = gather(w_query)
    gain_mlp, bias_mlp = gather(mlp_gain).astype(FULL), gather(mlp_bias).astype(FULL)
    output_w, up_w, down_w = gather(w_output), gather(w_up), gather(w_down)

    features = byte_feats.reshape(seqs * slots, width).astype(FULL)
    normed_in, in_back = jax.vjp(layer_norm, features, gain_in, bias_in)
    input_low = normed_in.astype(LOW)
    keys = matmul(input_low, key_w).astype(LOW)
    values = matmul(input_low, value_w).astype(LOW)
    normed_lat, lat_back = jax.vjp(layer_norm, latent, gain_lat, bias_lat)
    lat_low = normed_lat.astype(LOW)
    rows = lat_low.shape[0]
    queries = matmul(lat_low, query_w).astype(LOW)
    score_scale = 1.0 / math.sqrt(queries.shape[1] // H)
    qheads = queries.reshape(rows, H, -1)
    kheads = keys.reshape(seqs, slots, H, -1)
    vheads = values.reshape(seqs, slots, H, -1)

    scores = jnp.einsum("lhd,mkhd->mhlk", qheads, kheads, preferred_element_type=FULL) * score_scale
    slot_ids = lax.axis_index("ctx") * slots + lax.iota(jnp.int32, slots)
    valid = (slot_ids[None, :] < lengths[:, None])[:, None, None, :]
    scores = jnp.where(valid, scores, -1e30)
    highest = lax.pmax(jnp.max(scores, axis=-1), "ctx")
    weights = jnp.where(valid, jnp.exp(scores - highest[..., None]), 0.0)
    total = lax.psum(jnp.sum(weights, axis=-1), "ctx")
    numer = jnp.einsum("mhlk,mkhe->mlhe", weights.astype(LOW), vheads, preferred_element_type=FULL)
    numer = lax.psum(numer.astype(LOW), "ctx").astype(FULL)
    attended = numer / jnp.transpose(total, (0, 2, 1))[..., None]
    attended = attended.reshape(seqs * rows, -1)

    att_low = attended.astype(LOW)
    hidden = jnp.tile(latent, (seqs, 1)) + matmul(att_low, output_w)
    normed_mid, mid_back = jax.vjp(layer_norm, hidden, gain_mlp, bias_mlp)
    mid_low = normed_mid.astype(LOW)
    upward = matmul(mid_low, up_w)
    activated, gelu_back = jax.vjp(exact_gelu, upward)
    act_low = activated.astype(LOW)
    result = hidden + matmul(act_low, down_w)
    dout_low = cotangent.reshape(seqs * rows, -1)
    grad_down = scatter(matmul_tn(act_low, dout_low))
    (grad_upward,) = gelu_back(matmul_nt(dout_low, down_w))
    up_low = grad_upward.astype(LOW)
    grad_up = scatter(matmul_tn(mid_low, up_low))
    dhid_norm, grad_gmlp, grad_bmlp = mid_back(matmul_nt(up_low, up_w))
    dhidden = dout_low.astype(FULL) + dhid_norm
    dhid_low = dhidden.astype(LOW)
    grad_output = scatter(matmul_tn(att_low, dhid_low))
    grad_hidden = scatter(jnp.sum(dhidden.reshape(seqs, rows, -1), axis=0))
    grad_att = matmul_nt(dhid_low, output_w).astype(LOW)

    grad_heads = grad_att.reshape(seqs, rows, H, -1)
    delta = jnp.sum(
        grad_heads.astype(FULL) * attended.reshape(seqs, rows, H, -1), axis=-1
    ).transpose(0, 2, 1)
    probs = weights / total[..., None]
    dprobs = jnp.einsum("mlhe,mkhe->mhlk", grad_heads, vheads, preferred_element_type=FULL)
    dscores = (probs * (dprobs - delta[..., None])).astype(LOW)
    dquery = jnp.einsum("mhlk,mkhd->lhd", dscores, kheads, preferred_element_type=FULL) * score_scale
    dkeys = jnp.einsum("mhlk,lhd->mkhd", dscores, qheads, preferred_element_type=FULL) * score_scale
    dvalues = jnp.einsum("mhlk,mlhe->mkhe", probs.astype(LOW), grad_heads, preferred_element_type=FULL)
    dkeys = dkeys.astype(LOW).reshape(seqs * slots, -1)
    dvalues = dvalues.astype(LOW).reshape(seqs * slots, -1)

    dquery = lax.psum(dquery.reshape(rows, -1).astype(LOW), ("ctx", "wshard"))
    grad_query = matmul_tn(
        lax.dynamic_slice_in_dim(
            lat_low, lax.axis_index("wshard") * w_query.shape[0], w_query.shape[0], 1
        ),
        dquery,
    )
    dlat_norm, grad_glat, grad_blat = lat_back(matmul_nt(dquery, query_w))
    grad_latent = grad_hidden + own_part(dlat_norm, latent_array)

    dnorm_in = matmul_nt(dkeys, key_w) + matmul_nt(dvalues, value_w)
    dfeatures, grad_gin, grad_bin = in_back(dnorm_in)
    grad_key = lax.psum(scatter(matmul_tn(input_low, dkeys)).astype(LOW), "ctx").astype(FULL)
    grad_value = lax.psum(scatter(matmul_tn(input_low, dvalues)).astype(LOW), "ctx").astype(FULL)
    in_sums = lax.psum(jnp.concatenate([grad_gin, grad_bin]), ("ctx", "wshard"))
    grad_gin, grad_bin = jnp.split(in_sums, 2)
    mlp_sums = lax.psum(jnp.concatenate([grad_gmlp, grad_bmlp]), "wshard")
    grad_gmlp, grad_bmlp = jnp.split(mlp_sums, 2)
    return (
        result.astype(LOW).reshape(seqs, rows, -1),
        dfeatures.astype(LOW).reshape(seqs, slots, width),
        grad_latent,
        own_part(grad_glat, lat_gain),
        own_part(grad_blat, lat_bias),
        own_part(grad_gin, in_gain),
        own_part(grad_bin, in_bias),
        grad_query,
        grad_key,
        grad_value,
        grad_output,
        own_part(grad_gmlp, mlp_gain),
        own_part(grad_bmlp, mlp_bias),
        grad_up,
        grad_down,
    )


def ln_parts(values):
    centred = values - jnp.mean(values, axis=-1, keepdims=True)
    scale = lax.rsqrt(jnp.mean(centred * centred, axis=-1, keepdims=True) + 1e-05)
    return centred * scale, scale


def ln_grad(cotangent, gain, normed, scale):
    scaled = cotangent * gain
    first = jnp.mean(scaled, axis=-1, keepdims=True)
    second = jnp.mean(scaled * normed, axis=-1, keepdims=True)
    return scale * (scaled - first - normed * second)


def lanes(rows, columns):
    return lax.broadcasted_iota(jnp.int32, (rows, columns), 1)


def columns_sum(values):
    return jnp.sum(values, axis=0, keepdims=True)


class Plan:
    def __init__(self, ctx, zs, feats, latent, w_query, w_key, w_value, w_output, cot):
        self.ctx, self.zs = ctx, zs
        self.rows_in, self.din = feats.shape
        self.lat = latent.shape[0] * zs
        self.dl = latent.shape[1]
        self.qk, self.vd = w_key.shape[1], w_value.shape[1]
        self.seqs = cot.shape[0] // self.lat
        self.slots = self.rows_in // self.seqs
        self.head, self.vhead = self.qk // H, self.vd // H


def scratch_table(p):
    both = p.seqs * p.lat
    half = p.dl // 2
    part = p.dl // p.zs // 4
    vpart = p.din // p.zs // 4
    return dict(
        wk=((p.din, p.qk), LOW),
        wq=((p.dl, p.qk), LOW),
        lat=((p.lat, p.dl), LOW),
        wv=((p.din, p.vd), LOW),
        wo=((p.vd, p.dl), LOW),
        wu=((p.dl, p.dl), LOW),
        wd=((p.dl, p.dl), LOW),
        small_own=((8, 384), FULL),
        small=((p.zs, 8, 384), FULL),
        vec=((8, p.dl), FULL),
        feats=((p.rows_in, p.din), LOW),
        nin=((p.rows_in, p.din), LOW),
        nin_t=((p.din, p.rows_in), LOW),
        keys=((p.rows_in, p.qk), LOW),
        keys_t=((p.qk, p.rows_in), LOW),
        values=((p.rows_in, p.vd), LOW),
        nlat=((p.lat, p.dl), LOW),
        qmask=((H * p.lat, p.qk), LOW),
        scores=((p.seqs * H * max(p.lat, p.slots), max(p.lat, p.slots)), FULL),
        stat=((p.lat, 128), FULL),
        stat_t=((128, p.lat), FULL),
        max_t=((p.lat, 128), FULL),
        max_own=((2 * H, p.lat), FULL),
        max_in=((p.ctx, 2 * H, p.lat), FULL),
        max_all=((2 * H, p.lat), FULL),
        numer=((p.lat, p.vd), FULL),
        numer_low=((p.lat, p.vd), LOW),
        numer_in=((p.lat, p.vd), LOW),
        sums=((2, H, p.lat), FULL),
        sums_in=((H, p.lat), FULL),
        chip=((p.lat, p.vd), LOW),
        chip_in=((4, p.lat // 4, p.vd), LOW),
        chip_sums=((H, p.lat), FULL),
        chip_sums_in=((4, H, p.lat), FULL),
        scale=((p.lat // 4, p.vd), FULL),
        att=((both, p.vd), LOW),
        mid=((both, p.dl), LOW),
        act=((both, p.dl), LOW),
        dup=((both, p.dl), LOW),
        dhid=((both, p.dl), LOW),
        datt=((both, p.vd), LOW),
        cot=((both, p.dl), LOW),
        hid=((p.lat, p.dl), FULL),
        slope=((p.lat, p.dl), FULL),
        dmid=((p.lat, p.dl), FULL),
        res=((p.lat, p.dl), LOW),
        stats=((2, 2 * H, p.lat), FULL),
        dwo=((p.vd, half), LOW),
        dwu=((p.dl, half), LOW),
        dwd=((p.dl, half), LOW),
        dlat=((p.lat, half), LOW),
        zo=((p.zs, part, half), LOW),
        zu=((p.zs, part, half), LOW),
        zd=((p.zs, part, half), LOW),
        zl=((p.zs, p.lat // p.zs // 4, half), LOW),
        fo=((part, half), LOW),
        fu=((part, half), LOW),
        fd=((part, half), LOW),
        fl=((p.lat // p.zs // 4, half), LOW),
        dkeys=((p.rows_in, p.qk), LOW),
        dvalues=((p.rows_in, p.vd), LOW),
        dk_sum=((p.slots, p.qk), FULL),
        dq_t=((p.qk, p.lat), FULL),
        dq=((p.lat, p.qk), LOW),
        dq_in1=((p.lat, p.qk // 2), LOW),
        dq_chip=((p.lat, p.qk // 2), LOW),
        dq_in2=((4, p.lat, p.qk // 2), LOW),
        dq_plane=((p.lat, p.qk // 2), LOW),
        dq_in3=((p.zs, p.lat, p.qk // 2), LOW),
        dq_all=((p.lat, p.qk), LOW),
        bgrad=((p.rows_in, p.din), LOW),
        swk=((2, p.din, p.qk // 2), LOW),
        swv=((2, p.din, p.vd // 2), LOW),
        rwk=((p.din, p.qk // 2), LOW),
        rwv=((p.din, p.vd // 2), LOW),
        cwk=((p.zs, p.din // p.zs, p.qk // 2), LOW),
        cwv=((p.zs, p.din // p.zs, p.vd // 2), LOW),
        pwk_in=((4, p.zs, vpart, p.qk // 2), LOW),
        pwv_in=((4, p.zs, vpart, p.vd // 2), LOW),
        pwk=((p.zs, vpart, p.qk // 2), LOW),
        pwv=((p.zs, vpart, p.vd // 2), LOW),
        zwk_in=((p.zs, vpart, p.qk // 2), LOW),
        zwv_in=((p.zs, vpart, p.vd // 2), LOW),
        fwk=((vpart, p.qk // 2), LOW),
        fwv=((vpart, p.vd // 2), LOW),
        vs=((8, p.dl), FULL),
        vs_in1=((8, p.dl), FULL),
        vs_chip=((8, p.dl), FULL),
        vs_in2=((4, 8, p.dl), FULL),
        vs_plane=((8, p.dl), FULL),
        vs_in3=((p.zs, 8, p.dl), FULL),
        vs_all=((8, p.dl), FULL),
        gq=((p.dl, p.qk), FULL),
    )


class Copies:
    def __init__(self, sems):
        self.sems, self.used, self.open = sems, 0, []

    def new(self):
        self.used += 1
        return self.sems.at[self.used - 1]

    def group(self):
        return (self.new(), self.new())

    def send(self, pair, src, dst, ctx, z):
        pltpu.make_async_remote_copy(
            src_ref=src,
            dst_ref=dst,
            send_sem=pair[0],
            recv_sem=pair[1],
            device_id=(ctx, z),
            device_id_type=pl.DeviceIdType.MESH,
        ).start()

    def local(self, src, dst):
        copy = pltpu.make_async_copy(src, dst, self.new())
        copy.start()
        return copy

    def got(self, pair, view):
        pltpu.make_async_copy(view, view, pair[1]).wait()

    def sent(self, pair, view, when=None):
        self.open.append((pair[0], view, when))

    def drain(self):
        for sem, view, when in self.open:
            wait = pltpu.make_async_copy(view, view, sem).wait
            if when is None:
                wait()
            else:
                pl.when(when)(wait)


def at(start, size, step=None):
    return pl.ds(pl.multiple_of(start, step or size), size)


def fused_kernel(p, names, *refs):
    ins, refs = refs[:16], refs[16:]
    lengths, feats_in, lat_in, wq_in, wk_in, wv_in, wo_in, wu_in, wd_in = ins[:9]
    smalls, cot_in = ins[9:15], ins[15]
    outs, refs = refs[:11], refs[11:]
    res_out, byte_out, go, gu, gd, gv, gk, gl, gq_out, glat_out, vec_out = outs
    sems = refs[-1]
    s = types.SimpleNamespace(**dict(zip(names, refs[:-1])))
    cp = Copies(sems)
    ctx, zs = p.ctx, p.zs
    c, z = lax.axis_index("ctx"), lax.axis_index("wshard")
    h, q = lax.rem(c, 2), lax.div(c, 2)
    x, y = lax.rem(q, 2), lax.div(q, 2)
    other = 1 - h
    core = c + 1 - 2 * h
    chips = (c + 2 - 4 * x, c + 4 - 8 * y, c + 6 - 4 * x - 8 * y)
    near = (chips[0] * (1 - h) + chips[1] * h, chips[1] * (1 - h) + chips[0] * h)
    zed = [lax.rem(z + j, zs) for j in range(1, zs)]
    plane = [lax.rem(c + j, ctx) for j in range(1, ctx)]

    barrier = pltpu.get_barrier_semaphore()
    for peer in plane:
        pl.semaphore_signal(barrier, inc=1, device_id=(peer, z), device_id_type=pl.DeviceIdType.MESH)
    for peer in zed:
        pl.semaphore_signal(barrier, inc=1, device_id=(c, peer), device_id_type=pl.DeviceIdType.MESH)

    load_feats = cp.local(feats_in, s.feats)
    for row, ref in enumerate(smalls):
        s.small_own[row : row + 1, 0 : ref.shape[0]] = ref[...].reshape(1, -1).astype(FULL)
    pl.semaphore_wait(barrier, ctx - 1 + zs - 1)
    small_pair = cp.group()
    for peer in zed:
        cp.send(small_pair, s.small_own, s.small.at[z], c, peer)
    cp.sent(small_pair, s.small.at[0 : zs - 1])

    class Weight:
        def __init__(self, ref, source, cuts, line):
            self.ref, self.source, self.cuts, self.line = ref, source, cuts, line
            if line:
                self.up = [cp.group() for _ in range(zs - 1)]
                self.down = [cp.group() for _ in range(zs - 1)]
            self.rows, cols = source.shape
            self.part, self.cols = self.rows // cuts, cols // 2
            self.slot = q if cuts == 4 else lax.rem(x + y, 2)
            self.mine = at(h * self.cols, self.cols)
            self.pairs = [cp.group() for _ in range(4)]

        def view(self, rows):
            return self.ref.at[pl.ds(0, rows), pl.ds(0, self.cols)]

        def block(self, zz, qq):
            return self.ref.at[at(zz * self.rows + qq * self.part, self.part, 16), self.mine]

        def hop(self, i):
            one = self.view(self.part)

            def forward(pair, source, dest, when):
                @pl.when(when)
                def _():
                    cp.send(pair, source, self.block(dest[0], self.slot), c, dest[1])

                cp.sent(pair, one, when)

            if i == 0:
                mine = self.source.at[at(self.slot * self.part, self.part, 16), self.mine]
                forward(self.up[0], mine, (z, z + 1), z < zs - 1)
                forward(self.down[0], mine, (z, z - 1), z > 0)
                self.load = cp.local(self.source, self.ref.at[at(z * self.rows, self.rows, 16), :])
                return

            @pl.when(z >= i)
            def _():
                cp.got(self.up[i - 1], one)

            if i < zs - 1:
                block = self.block(lax.rem(z + zs - i, zs), self.slot)
                forward(self.up[i], block, (lax.rem(z + zs - i, zs), z + 1), (z >= i) & (z < zs - 1))

            @pl.when(z + i < zs)
            def _():
                cp.got(self.down[i - 1], one)

            if i < zs - 1:
                block = self.block(lax.rem(z + i, zs), self.slot)
                forward(self.down[i], block, (lax.rem(z + i, zs), z - 1), (z + i < zs) & (z > 0))

        def start(self):
            for peer in zed:
                cp.send(
                    self.pairs[0],
                    self.source.at[at(self.slot * self.part, self.part, 16), self.mine],
                    self.block(z, self.slot),
                    c,
                    peer,
                )
            cp.sent(self.pairs[0], self.view(3 * self.part))
            self.load = cp.local(self.source, self.ref.at[at(z * self.rows, self.rows, 16), :])

        def first(self):
            if self.line:
                self.hop(zs - 1)
            else:
                cp.got(self.pairs[0], self.view(3 * self.part))
            for zz in zed:
                block = self.block(zz, self.slot)
                cp.send(self.pairs[1], block, block, near[0], z)
            cp.sent(self.pairs[1], self.view(3 * self.part))

        def second(self):
            cp.got(self.pairs[1], self.view(3 * self.part))
            for zz in zed:
                for qq in (q, lax.div(near[0], 2)):
                    block = self.block(zz, qq)
                    cp.send(self.pairs[2], block, block, near[1], z)
            cp.sent(self.pairs[2], self.view(6 * self.part))

        def third(self):
            if self.cuts == 4:
                cp.got(self.pairs[2], self.view(6 * self.part))
            else:
                cp.got(self.pairs[1], self.view(3 * self.part))
            for zz in zed:
                block = self.ref.at[at(zz * self.rows, self.rows, 16), self.mine]
                cp.send(self.pairs[3], block, block, core, z)
            cp.sent(self.pairs[3], self.view(3 * self.rows))

        def ready(self):
            cp.got(self.pairs[3], self.view(3 * self.rows))
            self.load.wait()

    wk, wq, lat = Weight(s.wk, wk_in, 4, False), Weight(s.wq, wq_in, 4, False), Weight(s.lat, lat_in, 4, False)
    wv, wo = Weight(s.wv, wv_in, 4, False), Weight(s.wo, wo_in, 4, True)
    wu, wd = Weight(s.wu, wu_in, 4, True), Weight(s.wd, wd_in, 2, True)
    for weight in (wk, wq, lat, wv):
        weight.start()
    wo.hop(0)
    load_cot = cp.local(cot_in, s.cot)

    cp.got(small_pair, s.small.at[0 : zs - 1])
    s.small[z] = s.small_own[...]
    for row, ref in enumerate(smalls):
        size = ref.shape[0]
        for zz in range(zs):
            s.vec[row : row + 1, zz * size : (zz + 1) * size] = s.small[zz, row : row + 1, 0:size]
    vec = s.vec
    gain_lat, bias_lat = vec[0:1, :], vec[1:2, :]

    half_cols = at(h * (p.dl // 2), p.dl // 2)
    own = at(h * p.lat, p.lat)
    tiles = p.dl // 256
    quarter = p.lat // 4
    own_rows = at(h * p.lat + q * quarter, quarter)
    score_scale = 1.0 / math.sqrt(p.head)
    start_slot = c * p.slots
    lane_stat = lanes(p.lat, 128)
    gain_mlp, bias_mlp = vec[4:5, :], vec[5:6, :]
    qhalf, vhalf = p.qk // 2, p.vd // 2
    zrows = p.din // zs
    vpart = zrows // 4
    order = [*zed, z]

    def window(head):
        low_lane = pl.multiple_of(lax.div(head * p.vhead, 128) * 128, 128)
        return pl.ds(low_lane, 256), head * p.vhead - low_lane

    def mask_of(rows, low_lane):
        lane = lanes(rows, 256)
        return ((lane >= low_lane) & (lane < low_lane + p.vhead)).astype(FULL)

    def normed_bytes():
        load_feats.wait()

        @pl.loop(0, p.rows_in // 64)
        def _(i):
            rows = at(i * 64, 64)
            normed, _ = ln_parts(s.feats[rows, :].astype(FULL))
            s.nin[rows, :] = (normed * vec[2:3, 0 : p.din] + vec[3:4, 0 : p.din]).astype(LOW)

    def turned_bytes():
        @pl.loop(0, p.din // 128)
        def _(i):
            tile = at(i * 128, 128)
            s.nin_t[tile, :] = s.nin[:, tile].T

    def make_keys():
        @pl.loop(0, p.seqs)
        def _(i):
            rows = at(i * p.slots, p.slots)
            low = matmul(s.nin[rows, :], s.wk[...]).astype(LOW)
            s.keys[rows, :] = low
            s.keys_t[:, rows] = low.T

    def normed_latents():
        @pl.loop(0, p.lat // 64, unroll=True)
        def _(i):
            rows = at(i * 64, 64)
            normed, _ = ln_parts(s.lat[rows, :].astype(FULL))
            s.nlat[rows, :] = (normed * gain_lat + bias_lat).astype(LOW)

    def make_queries():
        queries = matmul(s.nlat[...], s.wq[...])
        lane_q = lanes(p.lat, p.qk)
        for head in range(H):
            inside = (lane_q >= head * p.head) & (lane_q < (head + 1) * p.head)
            s.qmask[head * p.lat : (head + 1) * p.lat, :] = jnp.where(inside, queries, 0.0).astype(LOW)

    max_pair = cp.group()

    def make_scores():
        s.stat[...] = jnp.zeros_like(s.stat)
        for seq in range(p.seqs):

            @pl.loop(0, H, unroll=4)
            def _(head):
                raw = matmul_nt(
                    s.qmask[at(head * p.lat, p.lat), :], s.keys[seq * p.slots : (seq + 1) * p.slots, :]
                )
                valid = lanes(p.lat, p.slots) < lengths[seq] - start_slot
                scores = jnp.where(valid, raw * score_scale, -1e30)
                s.scores[at((seq * H + head) * p.lat, p.lat), :] = scores
                top = jnp.max(scores, axis=-1, keepdims=True)
                s.stat[...] = jnp.where(lanes(p.lat, 128) == seq * H + head, top, s.stat[...])

        s.stat_t[...] = s.stat[...].T
        s.max_own[...] = s.stat_t[0 : 2 * H, :]
        for peer in plane:
            cp.send(max_pair, s.max_own, s.max_in.at[c], peer, z)
        cp.sent(max_pair, s.max_in.at[0 : ctx - 1])

    def make_values():
        @pl.loop(0, p.vd // 256, unroll=True)
        def _(i):
            tile = at(i * 256, 256)
            s.values[:, tile] = matmul(s.nin[...], s.wv[:, tile]).astype(LOW)

    def get_max():
        cp.got(max_pair, s.max_in.at[0 : ctx - 1])
        s.max_in[c] = s.max_own[...]
        top = s.max_in[0]
        for i in range(1, ctx):
            top = jnp.maximum(top, s.max_in[i])
        s.max_all[...] = top
        s.stat_t[0 : 2 * H, :] = top
        s.max_t[...] = s.stat_t[...].T
        s.stat[...] = jnp.zeros_like(s.stat)

    def partial(seq):
        s.numer[...] = jnp.zeros_like(s.numer)

        @pl.loop(0, H, unroll=4)
        def _(head):
            i = seq * H + head
            lane = lanes(p.lat, 128)
            top = jnp.sum(jnp.where(lane == i, s.max_t[...], 0.0), axis=-1, keepdims=True)
            weights = jnp.exp(s.scores[at(i * p.lat, p.lat), :] - top)
            total = jnp.sum(weights, axis=-1, keepdims=True)
            s.stat[...] = jnp.where(lane == i, total, s.stat[...])
            cols, low_lane = window(head)
            part = s.values[at(seq * p.slots, p.slots), cols] * mask_of(p.slots, low_lane).astype(LOW)
            s.numer[:, cols] += matmul(weights.astype(LOW), part)

        s.stat_t[...] = s.stat[...].T
        s.sums[seq] = s.stat_t[at(seq * H, H), :]

    pair_pair, sums_pair = cp.group(), cp.group()
    chip_sums_pair = cp.group()
    chip_pairs, att_pairs = [cp.group() for _ in range(2)], [cp.group() for _ in range(2)]
    near_chip = [lax.div(near[0], 2), lax.div(near[1], 2)]

    def partial_other():
        partial(other)
        s.numer_low[...] = s.numer[...].astype(LOW)
        cp.send(sums_pair, s.sums.at[other], s.sums_in, core, z)
        cp.send(pair_pair, s.numer_low, s.numer_in, core, z)
        cp.sent(pair_pair, s.numer_low)
        cp.sent(sums_pair, s.sums_in)

    def partial_own():
        partial(h)

    def chip_numer():
        cp.got(sums_pair, s.sums_in)
        s.chip_sums[...] = s.sums[h] + s.sums_in[...]
        for peer in chips:
            cp.send(chip_sums_pair, s.chip_sums, s.chip_sums_in.at[q], peer, z)
        cp.sent(chip_sums_pair, s.chip_sums_in.at[0:3])
        cp.got(pair_pair, s.numer_in)
        s.chip[...] = (s.numer[...] + s.numer_in[...].astype(FULL)).astype(LOW)
        for slot, qq in enumerate((3 - q, near_chip[0])):
            rows = at(qq * quarter, quarter)
            cp.send(chip_pairs[0], s.chip.at[rows, :], s.chip_in.at[slot], near[0], z)
        cp.sent(chip_pairs[0], s.chip_in.at[0:2])

    def chip_pass():
        cp.got(chip_pairs[0], s.chip_in.at[0:2])
        rows = at(near_chip[1] * quarter, quarter)
        s.chip_in[3] = (s.chip[rows, :].astype(FULL) + s.chip_in[0].astype(FULL)).astype(LOW)
        cp.send(chip_pairs[1], s.chip_in.at[3], s.chip_in.at[2], near[1], z)
        cp.sent(chip_pairs[1], s.chip_in.at[3])

    def turned_weights():
        for seq in range(p.seqs):

            @pl.loop(0, H, unroll=4)
            def _(head):
                i = seq * H + head
                raw = matmul_nt(
                    s.keys[seq * p.slots : (seq + 1) * p.slots, :], s.qmask[at(head * p.lat, p.lat), :]
                )
                slot = lax.broadcasted_iota(jnp.int32, (p.slots, p.lat), 0)
                masked = jnp.where(slot < lengths[seq] - start_slot, raw * score_scale, -1e30)
                s.scores[at(i * p.slots, p.slots), :] = jnp.exp(masked - s.max_all[pl.ds(i, 1), :])

    def make_scale():
        cp.got(chip_sums_pair, s.chip_sums_in.at[0:3])
        s.chip_sums_in[q] = s.chip_sums[...]
        sums = s.chip_sums_in
        inverse = 1.0 / ((sums[0] + sums[1]) + (sums[2] + sums[3]))
        s.stats[h, 0:H, :] = inverse
        s.stat_t[0:H, :] = inverse
        s.stat[...] = s.stat_t[...].T
        s.scale[...] = jnp.zeros_like(s.scale)
        own_quarter = s.stat[at(q * quarter, quarter), :]
        for head in range(H):
            low_lane = head * p.vhead // 128 * 128
            lane = lanes(quarter, 256) + low_lane
            inside = (lane >= head * p.vhead) & (lane < (head + 1) * p.vhead)
            cols = slice(low_lane, low_lane + 256)
            s.scale[:, cols] = jnp.where(inside, own_quarter[:, head : head + 1], s.scale[:, cols])

    def make_att():
        cp.got(chip_pairs[1], s.chip_in.at[2])
        own_numer = s.chip[at(q * quarter, quarter), :].astype(FULL)
        added = own_numer + (s.chip_in[1].astype(FULL) + s.chip_in[2].astype(FULL))
        s.att[own_rows, :] = (added * s.scale[...]).astype(LOW)
        cp.send(att_pairs[0], s.att.at[own_rows, :], s.att.at[own_rows, :], near[0], z)
        cp.sent(att_pairs[0], s.att.at[0:quarter, :])

    def att_pass():
        cp.got(att_pairs[0], s.att.at[0:quarter, :])
        for qq in (q, near_chip[0]):
            rows = at(h * p.lat + qq * quarter, quarter)
            cp.send(att_pairs[1], s.att.at[rows, :], s.att.at[rows, :], near[1], z)
        cp.sent(att_pairs[1], s.att.at[0 : 2 * quarter, :])

    shares = {}

    def share(ref):
        pair = cp.group()
        cp.send(pair, ref.at[own, :], ref.at[own, :], core, z)
        cp.sent(pair, ref.at[0 : p.lat, :])
        shares[id(ref)] = pair

    def shared(ref):
        cp.got(shares.pop(id(ref)), ref.at[0 : p.lat, :])

    def get_att():
        cp.got(att_pairs[1], s.att.at[0 : 2 * quarter, :])
        share(s.att)

    def make_hidden():
        @pl.loop(0, tiles, unroll=True)
        def _(i):
            tile = at(i * 256, 256)
            s.hid[:, tile] = s.lat[:, tile].astype(FULL) + matmul(s.att[own, :], s.wo[:, tile])

    def make_mid():
        @pl.loop(0, p.lat // 64, unroll=True)
        def _(i):
            normed, _ = ln_parts(s.hid[at(i * 64, 64), :])
            s.mid[at(h * p.lat + i * 64, 64), :] = (normed * gain_mlp + bias_mlp).astype(LOW)

        share(s.mid)

    def make_act():
        load_cot.wait()

        @pl.loop(0, tiles, unroll=True)
        def _(i):
            tile = at(i * 256, 256)
            up = matmul(s.mid[own, :], s.wu[:, tile])
            cdf = 0.5 * (1.0 + lax.erf(up * (1.0 / math.sqrt(2.0))))
            density = jnp.exp(-0.5 * up * up) * (1.0 / math.sqrt(2.0 * math.pi))
            s.act[own, tile] = (up * cdf).astype(LOW)
            s.slope[:, tile] = cdf + up * density

        share(s.act)

    class Reduce:
        def __init__(self, left, right, grads, arrive, final, out):
            self.left, self.right, self.out = left, right, out
            self.grads, self.arrive, self.final = grads, arrive, final
            self.part = self.final.shape[0]
            self.rows = self.part * 4
            self.pairs = [cp.group() for _ in range(4)]

        def product(self):
            @pl.loop(0, self.grads.shape[0] // 256, unroll=True)
            def _(i):
                rows = at(i * 256, 256)
                self.grads[rows, :] = matmul_tn(self.left[:, rows], self.right[:, half_cols]).astype(LOW)

        def block(self, zz):
            return self.grads.at[at(zz * self.rows + q * self.part, self.part, 16), :]

        def scatter(self):
            for peer in zed:
                cp.send(self.pairs[0], self.block(peer), self.arrive.at[z], c, peer)
            cp.sent(self.pairs[0], self.arrive.at[0 : zs - 1])

        def add(self):
            cp.got(self.pairs[0], self.arrive.at[0 : zs - 1])
            self.arrive[z] = self.grads[at(z * self.rows + q * self.part, self.part, 16), :]
            total = self.arrive[0].astype(FULL)
            for zz in range(1, zs):
                total = total + self.arrive[zz].astype(FULL)
            self.final[...] = total.astype(LOW)
            here = self.out.at[at(q * self.part, self.part, 16), half_cols]
            cp.send(self.pairs[1], self.final, here, near[0], z)
            cp.sent(self.pairs[1], self.final)
            self.store = cp.local(self.final, here)

        def spread(self):
            cp.got(self.pairs[1], self.final)
            here = self.out.at[at(q * self.part, self.part, 16), half_cols]
            there = self.out.at[at(near_chip[0] * self.part, self.part, 16), half_cols]
            cp.send(self.pairs[2], self.final, here, near[1], z)
            cp.send(self.pairs[2], there, there, near[1], z)
            cp.sent(self.pairs[2], self.arrive.at[0:2])

        def halve(self):
            cp.got(self.pairs[2], self.arrive.at[0:2])
            self.store.wait()
            block = self.out.at[:, half_cols]
            cp.send(self.pairs[3], block, block, core, z)
            cp.sent(self.pairs[3], block)

        def done(self):
            cp.got(self.pairs[3], self.out.at[:, half_cols])

    down = Reduce(s.act, s.cot, s.dwd, s.zd, s.fd, gd)
    upper = Reduce(s.mid, s.dup, s.dwu, s.zu, s.fu, gu)
    outer = Reduce(s.att, s.dhid, s.dwo, s.zo, s.fo, go)
    latents = Reduce(s.att, s.dhid, s.dlat, s.zl, s.fl, gl)
    reduces = (down, upper, outer, latents)

    def down_grads():
        shared(s.act)
        down.product()
        down.scatter()

    def upper_grads():
        shared(s.mid)
        shared(s.dup)
        upper.product()
        upper.scatter()

    def outer_grads():
        shared(s.att)
        shared(s.dhid)
        outer.product()
        outer.scatter()
        s.dlat[...] = (
            s.dhid[0 : p.lat, half_cols].astype(FULL) + s.dhid[p.lat : 2 * p.lat, half_cols].astype(FULL)
        ).astype(LOW)
        latents.scatter()

    def make_dup():
        @pl.loop(0, tiles, unroll=True)
        def _(i):
            tile = at(i * 256, 256)
            dact = matmul_nt(s.cot[own, :], s.wd[tile, :])
            s.dup[own, tile] = (dact * s.slope[:, tile]).astype(LOW)

        share(s.dup)

    def make_dmid():
        @pl.loop(0, tiles, unroll=True)
        def _(i):
            tile = at(i * 256, 256)
            s.dmid[:, tile] = matmul_nt(s.dup[own, :], s.wu[tile, :])

    def make_dhid():
        s.vs[...] = jnp.zeros_like(s.vs)

        @pl.loop(0, p.lat // 64, unroll=True)
        def _(i):
            rows = at(i * 64, 64)
            full_rows = at(h * p.lat + i * 64, 64)
            normed, scale = ln_parts(s.hid[rows, :])
            grad = s.dmid[rows, :]
            s.vs[0:1, :] += columns_sum(grad * normed)
            s.vs[1:2, :] += columns_sum(grad)
            total = s.cot[full_rows, :].astype(FULL) + ln_grad(grad, gain_mlp, normed, scale)
            s.dhid[full_rows, :] = total.astype(LOW)

        share(s.dhid)

    stats_pairs = [cp.group() for _ in range(2)]

    def share_inverse():
        cp.send(stats_pairs[0], s.stats.at[h, 0:H], s.stats.at[h, 0:H], core, z)
        cp.sent(stats_pairs[0], s.stats.at[0, 0:H])

    def make_datt():
        @pl.loop(0, tiles, unroll=True)
        def _(i):
            tile = at(i * 256, 256)
            s.datt[own, tile] = matmul_nt(s.dhid[own, :], s.wo[tile, :]).astype(LOW)

        share(s.datt)

    def make_delta():
        s.stat[...] = jnp.zeros_like(s.stat)

        @pl.loop(0, H, unroll=True)
        def _(head):
            cols, low_lane = window(head)
            product = s.datt[own, cols].astype(FULL) * s.att[own, cols].astype(FULL)
            delta = jnp.sum(product * mask_of(p.lat, low_lane), axis=-1, keepdims=True)
            s.stat[...] = jnp.where(lanes(p.lat, 128) == head, delta, s.stat[...])

        s.stat_t[...] = s.stat[...].T
        s.stats[h, H : 2 * H, :] = s.stat_t[0:H, :]
        cp.send(stats_pairs[1], s.stats.at[h, H : 2 * H], s.stats.at[h, H : 2 * H], core, z)
        cp.sent(stats_pairs[1], s.stats.at[0, 0:H])

    def values_grad(seq):
        latent_rows = at(seq * p.lat, p.lat)
        s.numer[...] = jnp.zeros_like(s.numer)

        @pl.loop(0, H, unroll=True)
        def _(head):
            cols, low_lane = window(head)
            inverse = s.stats[seq, pl.ds(head, 1), :]
            probs = s.scores[at((seq * H + head) * p.slots, p.slots), :] * inverse
            grad = s.datt[latent_rows, cols] * mask_of(p.lat, low_lane).astype(LOW)
            s.numer[:, cols] += matmul(probs.astype(LOW), grad)

        s.dvalues[at(seq * p.slots, p.slots), :] = s.numer[...].astype(LOW)

    def scores_grad(seq):
        slots = at(seq * p.slots, p.slots)
        latent_rows = at(seq * p.lat, p.lat)
        s.dk_sum[...] = jnp.zeros_like(s.dk_sum)

        @pl.loop(0, H, unroll=True)
        def _(head):
            heads = at(head * p.lat, p.lat)
            cols, low_lane = window(head)
            inverse = s.stats[seq, pl.ds(head, 1), :]
            delta = s.stats[seq, pl.ds(H + head, 1), :]
            probs = s.scores[at((seq * H + head) * p.slots, p.slots), :] * inverse
            grad = s.datt[latent_rows, cols] * mask_of(p.lat, low_lane).astype(LOW)
            dprobs = matmul_nt(s.values[slots, cols], grad)
            dscores = (probs * (dprobs - delta)).astype(LOW)
            s.dk_sum[...] += matmul(dscores, s.qmask[heads, :])
            block = at(head * p.head, p.head)
            s.dq_t[block, :] += matmul(s.keys_t[block, slots], dscores)

        s.dkeys[slots, :] = (s.dk_sum[...] * score_scale).astype(LOW)

    def weight_grads(ref, grad, width, side):
        cols = at(side * width, width)

        @pl.loop(0, p.din // 256, unroll=True)
        def _(i):
            rows = at(i * 256, 256)
            ref[side, rows, :] = matmul(s.nin_t[rows, :], grad[:, cols]).astype(LOW)

    class Local:
        def __init__(self, grads, arrive, chip, plane_in, plane, z_in, final, out):
            self.grads, self.arrive, self.chip, self.plane_in = grads, arrive, chip, plane_in
            self.plane, self.z_in, self.final, self.out = plane, z_in, final, out
            self.width = final.shape[1]
            self.pairs = [cp.group() for _ in range(5)]
            self.firsts = [cp.group() for _ in range(zs // 2)]
            self.seconds = [cp.group() for _ in range(zs // 2)]
            self.mine = at(h * self.width, self.width)

        def pair(self):
            cp.send(self.pairs[0], self.grads.at[other], self.arrive, core, z)
            cp.sent(self.pairs[0], self.arrive)

        def rows(self, qq):
            return at(qq * vpart, vpart, 16)

        def chunk(self, i):
            for zz in order[2 * i : 2 * i + 2]:
                rows = at(zz * zrows, zrows)
                total = self.grads[h, rows, :].astype(FULL) + self.arrive[rows, :].astype(FULL)
                self.chip[zz] = total.astype(LOW)
                for slot, qq in enumerate((3 - q, near_chip[0])):
                    cp.send(
                        self.firsts[i],
                        self.chip.at[zz, self.rows(qq), :],
                        self.plane_in.at[slot, zz],
                        near[0],
                        z,
                    )
            cp.sent(self.firsts[i], self.plane_in.at[0])

        def middle(self, i):
            cp.got(self.firsts[i], self.plane_in.at[0])
            for zz in order[2 * i : 2 * i + 2]:
                mine = self.chip[zz, self.rows(near_chip[1]), :].astype(FULL)
                self.plane_in[3, zz] = (mine + self.plane_in[0, zz].astype(FULL)).astype(LOW)
                cp.send(self.seconds[i], self.plane_in.at[3, zz], self.plane_in.at[2, zz], near[1], z)
            cp.sent(self.seconds[i], self.plane_in.at[0, 0:2])

        def add(self, i):
            cp.got(self.seconds[i], self.plane_in.at[0, 0:2])
            for zz in order[2 * i : 2 * i + 2]:
                mine = self.chip[zz, self.rows(q), :].astype(FULL)
                parts = self.plane_in[1, zz].astype(FULL) + self.plane_in[2, zz].astype(FULL)
                self.plane[zz] = (mine + parts).astype(LOW)
                if zz is not order[-1]:
                    cp.send(self.pairs[1], self.plane.at[zz], self.z_in.at[z], c, zz)
            if i == zs // 2 - 1:
                cp.sent(self.pairs[1], self.z_in.at[0 : zs - 1])

        def finish(self):
            cp.got(self.pairs[1], self.z_in.at[0 : zs - 1])
            self.z_in[z] = self.plane[z]
            total = self.z_in[0].astype(FULL)
            for zz in range(1, zs):
                total = total + self.z_in[zz].astype(FULL)
            self.final[...] = total.astype(LOW)
            here = self.out.at[self.rows(q), self.mine]
            cp.send(self.pairs[2], self.final, here, near[0], z)
            cp.sent(self.pairs[2], self.final)
            self.store = cp.local(self.final, here)

        def spread(self):
            cp.got(self.pairs[2], self.final)
            here = self.out.at[self.rows(q), self.mine]
            there = self.out.at[self.rows(near_chip[0]), self.mine]
            cp.send(self.pairs[3], self.final, here, near[1], z)
            cp.send(self.pairs[3], there, there, near[1], z)
            cp.sent(self.pairs[3], self.z_in.at[0:2])

        def halve(self):
            cp.got(self.pairs[3], self.z_in.at[0:2])
            self.store.wait()
            block = self.out.at[:, self.mine]
            cp.send(self.pairs[4], block, block, core, z)
            cp.sent(self.pairs[4], block)

        def done(self):
            cp.got(self.pairs[4], self.out.at[:, self.mine])

    key_grads = Local(s.swk, s.rwk, s.cwk, s.pwk_in, s.pwk, s.zwk_in, s.fwk, gk)
    value_grads = Local(s.swv, s.rwv, s.cwv, s.pwv_in, s.pwv, s.zwv_in, s.fwv, gv)
    def byte_matmul(seq):
        rows = at(seq * p.slots, p.slots)
        for tile in range(p.din // 256):
            cols = slice(tile * 256, (tile + 1) * 256)
            grad = matmul_nt(s.dkeys[rows, :], s.wk[cols, :]) + matmul_nt(s.dvalues[rows, :], s.wv[cols, :])
            s.scores[at(tile * p.rows_in + seq * p.slots, p.slots), :] = grad

    def byte_part(part):
        byte_matmul(part)

        @pl.loop(part * p.slots // 64, (part + 1) * p.slots // 64, unroll=2)
        def _(i):
            rows = at(i * 64, 64)
            tiles_in = [s.scores[at(k * p.rows_in + i * 64, 64), :] for k in range(p.din // 256)]
            grad = jnp.concatenate(tiles_in, axis=1)
            normed, scale = ln_parts(s.feats[rows, :].astype(FULL))
            s.vs[2:3, 0 : p.din] += columns_sum(grad * normed)
            s.vs[3:4, 0 : p.din] += columns_sum(grad)
            s.bgrad[rows, :] = ln_grad(grad, vec[2:3, 0 : p.din], normed, scale).astype(LOW)

    kv = (value_grads, key_grads)
    dq_pairs = [cp.group() for _ in range(5)]
    vs_pairs = [cp.group() for _ in range(3)]
    res_pair = cp.group()
    stores = []
    own_half = at(h * qhalf, qhalf)

    def values_own():
        values_grad(h)

    def values_other():
        cp.got(stats_pairs[0], s.stats.at[0, 0:H])
        shared(s.datt)
        values_grad(other)

    def value_weights():
        weight_grads(s.swv, s.dvalues, vhalf, other)
        value_grads.pair()

    def value_weights_own():
        weight_grads(s.swv, s.dvalues, vhalf, h)

    def value_chunks():
        cp.got(value_grads.pairs[0], value_grads.arrive)
        for i in range(zs // 2):
            value_grads.chunk(i)

    def scores_own():
        s.dq_t[...] = jnp.zeros_like(s.dq_t)
        scores_grad(h)

    def scores_other():
        cp.got(stats_pairs[1], s.stats.at[0, 0:H])
        scores_grad(other)
        s.dq[...] = (s.dq_t[...] * score_scale).T.astype(LOW)
        cp.send(dq_pairs[0], s.dq.at[:, at(other * qhalf, qhalf)], s.dq_in1, core, z)
        cp.sent(dq_pairs[0], s.dq_in1)

    def key_weights():
        weight_grads(s.swk, s.dkeys, qhalf, other)
        key_grads.pair()
        weight_grads(s.swk, s.dkeys, qhalf, h)

    def dq_chip():
        cp.got(dq_pairs[0], s.dq_in1)
        s.dq_chip[...] = (s.dq[:, own_half].astype(FULL) + s.dq_in1[...].astype(FULL)).astype(LOW)
        cp.send(dq_pairs[1], s.dq_chip, s.dq_in2.at[0], near[0], z)
        cp.sent(dq_pairs[1], s.dq_chip)

    def dq_pass():
        cp.got(dq_pairs[1], s.dq_chip)
        s.dq_in2[2] = (s.dq_chip[...].astype(FULL) + s.dq_in2[0].astype(FULL)).astype(LOW)
        cp.send(dq_pairs[4], s.dq_in2.at[2], s.dq_in2.at[1], near[1], z)
        cp.sent(dq_pairs[4], s.dq_chip)

    def key_chunks():
        cp.got(key_grads.pairs[0], key_grads.arrive)
        for i in range(zs // 2):
            key_grads.chunk(i)

    def byte_store():
        stores.append(cp.local(s.bgrad, byte_out))
        cp.send(vs_pairs[0], s.vs, s.vs_in1, core, z)
        cp.sent(vs_pairs[0], s.vs)

    def dq_plane():
        cp.got(dq_pairs[4], s.dq_chip)
        s.dq_plane[...] = (s.dq_in2[1].astype(FULL) + s.dq_in2[2].astype(FULL)).astype(LOW)
        for peer in zed:
            cp.send(dq_pairs[2], s.dq_plane, s.dq_in3.at[z], c, peer)
        cp.sent(dq_pairs[2], s.dq_in3.at[0 : zs - 1])

    def vs_chip():
        cp.got(vs_pairs[0], s.vs_in1)
        s.vs_chip[...] = s.vs[...] + s.vs_in1[...]
        for peer in chips:
            cp.send(vs_pairs[1], s.vs_chip, s.vs_in2.at[q], peer, z)
        cp.sent(vs_pairs[1], s.vs_in2.at[0:3])

    def make_result():
        @pl.loop(0, tiles, unroll=True)
        def _(i):
            tile = at(i * 256, 256)
            s.res[:, tile] = (s.hid[:, tile] + matmul(s.act[own, :], s.wd[:, tile])).astype(LOW)

        cp.send(res_pair, s.res, res_out.at[own, :], core, z)
        cp.sent(res_pair, s.res)
        stores.append(cp.local(s.res, res_out.at[own, :]))

    def vs_plane():
        cp.got(vs_pairs[1], s.vs_in2.at[0:3])
        s.vs_in2[q] = s.vs_chip[...]
        parts = s.vs_in2
        total = (parts[0] + parts[1]) + (parts[2] + parts[3])
        row_ids = lax.broadcasted_iota(jnp.int32, (8, p.dl), 0)
        s.vs_plane[...] = jnp.where(row_ids < 2, s.vs_chip[...], total)
        for peer in zed:
            cp.send(vs_pairs[2], s.vs_plane, s.vs_in3.at[z], c, peer)
        cp.sent(vs_pairs[2], s.vs_in3.at[0 : zs - 1])

    def dq_total():
        cp.got(dq_pairs[2], s.dq_in3.at[0 : zs - 1])
        s.dq_in3[z] = s.dq_plane[...]
        parts = s.dq_in3
        total = parts[0].astype(FULL)
        for zz in range(1, zs):
            total = total + parts[zz].astype(FULL)
        s.dq_all[:, own_half] = total.astype(LOW)
        cp.send(dq_pairs[3], s.dq_all.at[:, own_half], s.dq_all.at[:, own_half], core, z)
        cp.sent(dq_pairs[3], s.dq_in1)

    def query_grads():
        cp.got(dq_pairs[3], s.dq_in1)

        @pl.loop(0, tiles, unroll=True)
        def _(i):
            tile = at(i * 256, 256)
            s.gq[tile, :] = matmul_tn(s.nlat[:, tile], s.dq_all[...])
            s.dmid[:, tile] = matmul_nt(s.dq_all[...], s.wq[tile, :])

        stores.append(cp.local(s.gq.at[at(z * (p.dl // zs), p.dl // zs, 16), :], gq_out))

    def latent_grads():
        cp.got(vs_pairs[2], s.vs_in3.at[0 : zs - 1])
        s.vs_in3[z] = s.vs_plane[...]
        total = s.vs_in3[0]
        for zz in range(1, zs):
            total = total + s.vs_in3[zz]
        s.vs_all[...] = total
        s.vs_all[4:6, :] = jnp.zeros((2, p.dl), FULL)

        @pl.loop(0, p.lat // 64, unroll=True)
        def _(i):
            rows = at(i * 64, 64)
            normed, scale = ln_parts(s.lat[rows, :].astype(FULL))
            grad = s.dmid[rows, :]
            s.vs_all[4:5, :] += columns_sum(grad * normed)
            s.vs_all[5:6, :] += columns_sum(grad)
            s.slope[rows, :] = ln_grad(grad, gain_lat, normed, scale)

        stores.append(cp.local(s.slope.at[at(z * (p.lat // zs), p.lat // zs, 16), :], glat_out))
        stores.append(cp.local(s.vs_all, vec_out))

    normed_bytes()
    wk.first()
    turned_bytes()
    wk.second()
    wq.first()
    wk.third()
    wu.hop(0)
    wq.second()
    lat.first()
    lat.second()
    wo.hop(1)
    wv.first()
    wq.third()
    wq.ready()
    lat.third()
    wk.ready()
    lat.ready()
    make_keys()
    normed_latents()
    wv.second()
    make_queries()
    wo.hop(2)
    make_scores()
    wu.hop(1)
    wd.hop(0)
    wo.first()
    wv.third()
    wv.ready()
    wo.second()
    make_values()
    get_max()
    partial_other()
    wu.hop(2)
    partial_own()
    chip_numer()
    wd.hop(1)
    wu.first()
    wo.third()
    wd.hop(2)
    turned_weights()
    chip_pass()
    make_scale()
    wu.second()
    make_att()
    wo.ready()
    att_pass()
    wu.third()
    wd.first()
    get_att()
    wu.ready()
    share_inverse()
    make_hidden()
    make_mid()
    make_act()
    wd.third()
    down_grads()
    wd.ready()
    make_dup()
    make_dmid()
    make_dhid()
    make_datt()
    make_delta()
    values_own()
    values_other()
    value_weights()
    upper_grads()
    down.add()
    value_weights_own()
    value_chunks()
    scores_own()
    scores_other()
    value_grads.middle(0)
    byte_part(0)
    dq_chip()
    value_grads.middle(1)
    value_grads.add(0)
    key_weights()
    down.spread()
    value_grads.add(1)
    key_chunks()
    outer_grads()
    down.halve()
    upper.add()
    key_grads.middle(0)
    dq_pass()
    key_grads.middle(1)
    byte_part(1)
    key_grads.add(0)
    key_grads.add(1)
    value_grads.finish()
    upper.spread()
    value_grads.spread()
    dq_plane()
    byte_store()
    value_grads.halve()
    outer.add()
    vs_chip()
    key_grads.finish()
    upper.halve()
    make_result()
    latents.add()
    outer.spread()
    key_grads.spread()
    vs_plane()
    dq_total()
    latents.spread()
    outer.halve()
    key_grads.halve()
    query_grads()
    latents.halve()
    latent_grads()
    for part in (*reduces, *kv):
        part.done()
    cp.got(res_pair, s.res)
    for store in stores:
        store.wait()
    cp.drain()


def finish_kernel(p, *refs):
    ins, outs, scratch = refs[:11], refs[11:26], refs[26:]
    held, wide, sems = scratch[:11], scratch[11:17], scratch[17]
    z = lax.axis_index("wshard")
    order = (10, 2, 3, 4, 5, 0, 1, 7, 9, 8, 6)
    loads = {n: pltpu.make_async_copy(ins[n], held[n], sems.at[n]) for n in order}
    for load in loads.values():
        load.start()
    stores = []

    def store(ref, out):
        copy = pltpu.make_async_copy(ref, outs[out], sems.at[11 + out])
        copy.start()
        stores.append(copy)

    loads[10].wait()
    vec = held[10]
    for out, row in ((3, 4), (4, 5), (5, 2), (6, 3), (11, 0), (12, 1)):
        size = outs[out].shape[0]
        picked = vec[row : row + 1, 0:size]
        for zz in range(1, p.zs):
            picked = jnp.where(z == zz, vec[row : row + 1, zz * size : (zz + 1) * size], picked)
        outs[out][...] = picked.reshape(size)
    for n, out, slot in ((2, 10, 0), (3, 13, 1), (4, 14, 2), (5, 9, 3)):
        loads[n].wait()
        wide[slot][...] = held[n][...].astype(FULL)
        store(wide[slot], out)
    for n, out in ((0, 0), (1, 1)):
        loads[n].wait()
        store(held[n], out)
    loads[7].wait()
    loads[9].wait()
    wide[5][...] = held[9][...] + held[7][...].astype(FULL)
    store(wide[5], 2)
    loads[8].wait()
    store(held[8], 7)
    loads[6].wait()
    wide[4][...] = held[6][...].astype(FULL)
    store(wide[4], 8)
    for copy in stores:
        copy.wait()


def fused(*args):
    (byte_feats, lengths, latent, *smalls, cot) = (args[0], args[1], args[2], *args[3:7], args[11], args[12], args[15])
    w_query, w_key, w_value, w_output = args[7:11]
    w_up, w_down = args[13:15]
    seqs, slots, din = byte_feats.shape
    ctx, zs = lax.axis_size("ctx"), lax.axis_size("wshard")
    feats = byte_feats.reshape(seqs * slots, din)
    cot_flat = cot.reshape(-1, cot.shape[-1])
    p = Plan(ctx, zs, feats, latent, w_query, w_key, w_value, w_output, cot_flat)
    table = scratch_table(p)
    anywhere = pl.BlockSpec(memory_space=pl.ANY)
    in_vmem = pl.BlockSpec(memory_space=pltpu.VMEM)
    struct = jax.ShapeDtypeStruct
    made = pl.pallas_call(
        functools.partial(fused_kernel, p, tuple(table)),
        out_shape=(
            struct(cot_flat.shape, LOW),
            struct(feats.shape, LOW),
            struct(w_output.shape, LOW),
            struct(w_up.shape, LOW),
            struct(w_down.shape, LOW),
            struct(w_value.shape, LOW),
            struct(w_key.shape, LOW),
            struct(latent.shape, LOW),
            struct(w_query.shape, FULL),
            struct(latent.shape, FULL),
            struct((8, p.dl), FULL),
        ),
        in_specs=[pl.BlockSpec(memory_space=pltpu.SMEM)] + [anywhere] * 8 + [in_vmem] * 6 + [anywhere],
        out_specs=(anywhere,) * 11,
        scratch_shapes=[pltpu.VMEM(shape, kind) for shape, kind in table.values()]
        + [pltpu.SemaphoreType.DMA((SEMS,))],
        compiler_params=pltpu.CompilerParams(
            collective_id=0, has_side_effects=True, vmem_limit_bytes=67043328
        ),
        name="block",
    )(lengths, feats, latent, w_query, w_key, w_value, w_output, w_up, w_down, *smalls, cot_flat)
    shapes = (
        (cot_flat.shape, LOW),
        (feats.shape, LOW),
        (latent.shape, FULL),
        *((smalls[i].shape, FULL) for i in range(4)),
        *((w.shape, FULL) for w in (w_query, w_key, w_value, w_output)),
        *((smalls[i].shape, FULL) for i in (4, 5)),
        *((w.shape, FULL) for w in (w_up, w_down)),
    )
    outs = pl.pallas_call(
        functools.partial(finish_kernel, p),
        out_shape=tuple(struct(shape, kind) for shape, kind in shapes),
        in_specs=[anywhere] * 11,
        out_specs=tuple(in_vmem if len(shape) == 1 else anywhere for shape, _ in shapes),
        scratch_shapes=[pltpu.VMEM(one.shape, one.dtype) for one in made]
        + [pltpu.VMEM(shapes[n][0], FULL) for n in (10, 13, 14, 9, 8, 2)]
        + [pltpu.SemaphoreType.DMA((26,))],
        compiler_params=pltpu.CompilerParams(vmem_limit_bytes=60 * 2**20),
        name="finish",
    )(*made)
    return (outs[0].reshape(cot.shape), outs[1].reshape(byte_feats.shape), *outs[2:])


def shards(*args):
    if lax.axis_size("ctx") == 8 and lax.axis_size("wshard") == 4 and args[0].shape[0] == 2:
        return fused(*args)
    return plain(*args)


def solution(mesh):
    sharded, plain = P("wshard", None), P("wshard")
    return jax.shard_map(
        shards,
        mesh=mesh,
        in_specs=(
            P("wshard", "ctx", None),
            plain,
            sharded,
            plain,
            plain,
            plain,
            plain,
            sharded,
            sharded,
            sharded,
            sharded,
            plain,
            plain,
            sharded,
            sharded,
            P("wshard", None, None),
        ),
        out_specs=(
            P("wshard", None, None),
            P("wshard", "ctx", None),
            sharded,
            plain,
            plain,
            plain,
            plain,
            sharded,
            sharded,
            sharded,
            sharded,
            plain,
            plain,
            sharded,
            sharded,
        ),
        check_vma=False,
    )
```
